32 devices in a mesh: dp: 16 (over z, y, core), tensor: 2 (over x).
Axes of the slice: x: 2, y: 2, z: 4, core: 2. Of those that a mesh axis runs over, the one named last changes fastest.
Arguments:
- tokens: bfloat16 [16, 1024, 768], P(None, 'dp', 'tensor'), may hold values from -6 to 6
- cotangent: bfloat16 [16, 1024, 768], P(None, 'dp', 'tensor'), may hold values from -6 to 6
- thoughts: bfloat16 [16, 6, 768], P('dp', None, 'tensor'), may hold values from -6 to 6
- latent_pos: int32 [16, 6], P('dp'), may hold values from 1 to 63, as said below
- lengths: int32 [16], replicated, may hold values from 64 to 1024, as said below
- dealing: int32 [16], replicated, may hold values from 0 to 15, each once
- qkv_weight: bfloat16 [3, 768, 768], P(None, None, 'tensor'), may hold values from -0.21875 to 0.21875
- qv_bias: float32 [2, 768], P(None, 'tensor'), may hold values from -3 to 3
- out_weight: bfloat16 [768, 768], P('tensor'), may hold values from -0.875 to 0.875
- out_bias: float32 [2, 768], replicated, may hold values from -3 to 3
- fc_weight: bfloat16 [768, 3072], P(None, 'tensor'), may hold values from -0.21875 to 0.21875
- fc_bias: float32 [3072], P('tensor'), may hold values from -3 to 3
- proj_weight: bfloat16 [3072, 768], P('tensor'), may hold values from -0.109375 to 0.109375
- norm_gain: float32 [2, 768], replicated, may hold values from 0.5 to 1.5
- norm_shift: float32 [2, 768], replicated, may hold values from -3 to 3
Outputs:
- block_out: float32 [16, 1024, 768], P(None, 'dp', 'tensor')
- input_grad: float32 [16, 1024, 768], P(None, 'dp', 'tensor')
- grad_qkv_weight: float32 [3, 768, 768], P(None, None, 'tensor')
- grad_qv_bias: float32 [2, 768], P(None, 'tensor')
- grad_out_weight: float32 [768, 768], P('tensor')
- grad_out_bias: float32 [2, 768], replicated
- grad_fc_weight: float32 [768, 3072], P(None, 'tensor')
- grad_fc_bias: float32 [3072], P('tensor')
- grad_proj_weight: float32 [3072, 768], P('tensor')
- grad_norm_gain: float32 [2, 768], replicated
- grad_norm_shift: float32 [2, 768], replicated
The draws below stay inside these ranges and needn't reach their ends.
Inputs may be any that keep to these rules, and one draw needn't show every extreme that they name: `lengths`: one sequence has exactly 1024 tokens and one exactly 64. `dealing`: dealt slot j belongs to data group j. `latent_pos`: each slot's 6 positions are consecutive and lie below every sequence's length.
All inputs are finite; a program needn't handle non-finite values.
Results may differ from the reference program's by a relative error of at most 0.012.
The reference program's roundings to bfloat16 on the way count: a program that leaves them out, or rounds other values in their place, can miss the bound.
Values may be sent and summed in bfloat16 or wider, within the bound.
No kernel may reach another device: no remote copies, remote signals or barrier semaphores. Data moves between devices by JAX's collectives and lax.ppermute only.
A program may use at most 192 MiB of HBM per device.

```python
import jax
import jax.numpy as jnp
from jax import lax

D = 768
HEADS = 12
HEAD_DIM = 64
FF = 3072
LMAX = 1024
NLAT = 6
QB = 512
NSEQ = 16


def draw_lengths(key, part):
    spread = jax.random.randint(key, (NSEQ,), LMAX // 16, LMAX + 1)
    picks = jax.random.permutation(jax.random.fold_in(key, 7), NSEQ)
    slots = jnp.arange(NSEQ, dtype=jnp.int32)
    spread = jnp.where(slots == picks[0], LMAX, spread)
    spread = jnp.where(slots == picks[1], LMAX // 16, spread)
    return spread.astype(jnp.int32)


def draw_latent_pos(key, part):
    starts = jax.random.randint(key, (NSEQ,), 1, LMAX // 16 - NLAT + 1)
    picks = jax.random.permutation(jax.random.fold_in(key, 11), NSEQ)
    slots = jnp.arange(NSEQ, dtype=jnp.int32)
    starts = jnp.where(slots == picks[0], LMAX // 16 - NLAT, starts)
    starts = jnp.where(slots == picks[1], 1, starts)
    return (starts[:, None] + jnp.arange(NLAT, dtype=jnp.int32)[None, :]).astype(jnp.int32)


def level_of(own_key, extent, shards, low, largest):
    factor_of, own = 1.0, jax.random.fold_in(own_key, 6)
    for position, blocks in shards:
        steps = jnp.exp(jax.random.uniform(jax.random.fold_in(own, position), (blocks,), jnp.float32, low / len(shards), largest / len(shards)))
        factor_of = factor_of * jnp.repeat(steps, extent[position] // blocks).reshape([-1 if axis == position else 1 for axis in range(len(extent))])
    return factor_of


def bell_draw(own_key, extent, scale, limit, split=(), kind=jnp.bfloat16):
    values = jax.random.normal(own_key, extent, jnp.float32) * scale
    if len(split) > 0:
        values = level_of(own_key, extent, split, -0.22, 0.18) * values
    return jnp.clip(values, min=-limit, max=limit).astype(kind)


def setup_inputs(seed: int = 0) -> dict:
    splits = jax.random.split(jax.random.key(seed), 16)
    tokens = bell_draw(splits[0], (NSEQ, LMAX, D), 1.0, 6.0, ((1, 16), (2, 2)))
    cotangent = bell_draw(splits[1], (NSEQ, LMAX, D), 1.0, 6.0, ((1, 16), (2, 2)))
    thoughts = bell_draw(splits[2], (NSEQ, NLAT, D), 1.0, 6.0, ((0, 16), (2, 2)))
    latent_pos = draw_latent_pos(jax.random.fold_in(splits[15], 71), 0)
    lengths = draw_lengths(jax.random.fold_in(splits[15], 71), 0)
    dealing = jax.random.permutation(splits[5], NSEQ).astype(jnp.int32)
    qkv_weight = bell_draw(splits[6], (3, D, D), D ** -0.5, 0.21875, ((2, 2),))
    qv_bias = bell_draw(splits[7], (2, D), 0.3, 3.0, ((1, 2),), jnp.float32)
    out_weight = bell_draw(splits[8], (D, D), (D // 16) ** -0.5, 0.875, ((0, 2),))
    out_bias = bell_draw(splits[9], (2, D), 0.3, 3.0, (), jnp.float32)
    fc_weight = bell_draw(splits[10], (D, FF), D ** -0.5, 0.21875, ((1, 2),))
    fc_bias = bell_draw(splits[11], (FF,), 0.5, 3.0, ((0, 2),), jnp.float32)
    proj_weight = bell_draw(splits[12], (FF, D), FF ** -0.5, 0.109375, ((0, 2),))
    norm_gain = jnp.clip(1.0 + 0.1 * jax.random.normal(splits[13], (2, D), jnp.float32), 0.5, 1.5)
    norm_shift = bell_draw(splits[14], (2, D), 0.3, 3.0, (), jnp.float32)
    return {"tokens": tokens, "cotangent": cotangent, "thoughts": thoughts, "latent_pos": latent_pos, "lengths": lengths, "dealing": dealing, "qkv_weight": qkv_weight, "qv_bias": qv_bias, "out_weight": out_weight, "out_bias": out_bias, "fc_weight": fc_weight, "fc_bias": fc_bias, "proj_weight": proj_weight, "norm_gain": norm_gain, "norm_shift": norm_shift}


highest = lax.Precision.HIGHEST
masked_score = -1e+30

@jax.custom_vjp
def low(v):
    return lax.optimization_barrier(v.astype(jnp.bfloat16)).astype(jnp.float32)

@jax.custom_vjp
def low_back(v):
    return v

def low_keep(v):
    return (low(v), None)

def low_pass(kept, grad):
    return (grad,)

def back_keep(v):
    return (v, None)

def back_low(kept, grad):
    return (low(grad),)
low.defvjp(low_keep, low_pass)
low_back.defvjp(back_keep, back_low)

def rounded(value):
    return low_back(low(value))

def layer_norm(features, scale_gain, scale_shift):
    row_mean = lax.optimization_barrier(jnp.mean(features, axis=-1, keepdims=True))
    centred = features - row_mean
    variance = lax.optimization_barrier(jnp.mean(centred * centred, axis=-1, keepdims=True))
    return centred * lax.rsqrt(variance + 1e-05) * scale_gain + scale_shift

def tanh_gelu(value):
    return jax.nn.gelu(value, approximate=True)

def attend_block(query_block, offset, key_heads, value_heads, length):
    scores = jnp.einsum('qhe,khe->hqk', query_block, key_heads, precision=highest) * HEAD_DIM ** (-0.5)
    scores = low_back(scores)
    query_pos = offset + jnp.arange(QB, dtype=jnp.int32)
    key_pos = jnp.arange(LMAX, dtype=jnp.int32)
    allowed = (key_pos[None, :] <= query_pos[:, None]) & (key_pos[None, :] < length)
    scores = jnp.where(allowed[None], scores, masked_score)
    row_top = lax.optimization_barrier(jnp.max(scores, axis=-1, keepdims=True))
    exponent = jnp.exp(scores - row_top)
    probabilities = exponent / lax.optimization_barrier(jnp.sum(exponent, axis=-1, keepdims=True))
    return jnp.einsum('hqk,khe->qhe', low(probabilities), value_heads, precision=highest)

def forward(params, input_rows, length):
    qkv_weight, qv_bias, out_weight, out_bias, fc_weight, fc_bias, proj_weight, norm_gain, norm_shift = params
    valid_rows = (jnp.arange(LMAX, dtype=jnp.int32) < length).astype(jnp.float32)[:, None]
    normed = low(layer_norm(input_rows, norm_gain[0], norm_shift[0]))
    projected = jnp.einsum('rd,cde->cre', normed, qkv_weight, precision=highest)
    queries = rounded(projected[0] + qv_bias[0]).reshape(LMAX, HEADS, HEAD_DIM)
    key_heads = rounded(projected[1]).reshape(LMAX, HEADS, HEAD_DIM)
    value_heads = rounded(projected[2] + qv_bias[1]).reshape(LMAX, HEADS, HEAD_DIM)
    query_blocks = queries.reshape(LMAX // QB, QB, HEADS, HEAD_DIM)
    offsets = jnp.arange(LMAX // QB, dtype=jnp.int32) * QB
    attend = jax.checkpoint(lambda pair_item: attend_block(pair_item[0], pair_item[1], key_heads, value_heads, length))
    attended = lax.map(attend, (query_blocks, offsets))
    heads_out = rounded(attended.reshape(LMAX, D))
    residual = input_rows + low_back(jnp.dot(heads_out, out_weight, precision=highest) + out_bias[0])
    normed_mlp = low(layer_norm(residual, norm_gain[1], norm_shift[1]))
    pre_act = low_back(jnp.dot(normed_mlp, fc_weight, precision=highest) + fc_bias)
    active = low(tanh_gelu(pre_act))
    mlp_out = low_back(jnp.dot(active, proj_weight, precision=highest) + out_bias[1])
    return valid_rows * (residual + mlp_out)

def reference(tokens, cotangent, thoughts, latent_pos, lengths, dealing, qkv_weight, qv_bias, out_weight, out_bias, fc_weight, fc_bias, proj_weight, norm_gain, norm_shift):
    params = tuple((weight_array.astype(jnp.float32) for weight_array in (qkv_weight, qv_bias, out_weight, out_bias, fc_weight, fc_bias, proj_weight, norm_gain, norm_shift)))
    dealt_rows = tokens[dealing].astype(jnp.float32)
    dealt_cot = cotangent[dealing].astype(jnp.float32)
    dealt_lengths = lengths[dealing]
    positions = jnp.arange(LMAX, dtype=jnp.int32)
    thought_rows = thoughts.astype(jnp.float32)
    input_rows = dealt_rows
    for latent in range(NLAT):
        latent_hit = positions[None, :] == latent_pos[:, latent][:, None]
        input_rows = jnp.where(latent_hit[..., None], thought_rows[:, latent][:, None, :], input_rows)

    def one_sequence(totals, sequence_item):
        rows_here, cot_here, length = sequence_item
        output, pullback = jax.vjp(lambda weights, rows_in: forward(weights, rows_in, length), params, rows_here)
        weight_grads, row_grads = pullback(cot_here)
        return (jax.tree.map(jnp.add, totals, weight_grads), (output, row_grads))
    zero_grads = jax.tree.map(jnp.zeros_like, params)
    totals, (outputs, row_grads) = lax.scan(one_sequence, zero_grads, (input_rows, dealt_cot, dealt_lengths))
    restore = jnp.zeros_like(dealing).at[dealing].set(jnp.arange(NSEQ, dtype=jnp.int32))
    return (outputs[restore], row_grads[restore], totals[0], totals[1], totals[2], totals[3], totals[4], totals[5], totals[6], totals[7], totals[8])
```

```python
import functools

import jax
import jax.numpy as jnp
from jax import lax
from jax.experimental import pallas as pl
from jax.experimental.pallas import tpu as pltpu
from jax.sharding import PartitionSpec as P

HEAD_DIM = 64
LANES = 128
AXES = ("dp", "tensor")
SCALE = HEAD_DIM ** (-0.5)
MASKED = -1e30
BF16 = jnp.bfloat16
F32 = jnp.float32


def dot_nn(left, right):
    return lax.dot_general(left, right, (((1,), (0,)), ((), ())), preferred_element_type=F32)


def dot_nt(left, right):
    return lax.dot_general(left, right, (((1,), (1,)), ((), ())), preferred_element_type=F32)


def dot_tn(left, right):
    return lax.dot_general(left, right, (((0,), (0,)), ((), ())), preferred_element_type=F32)


def own_mask(tile, start, core, length, block):
    key = lax.broadcasted_iota(jnp.int32, (tile, tile), 0)
    query = lax.broadcasted_iota(jnp.int32, (tile, tile), 1)
    key_row = start + key
    key_pos = (2 * (key_row // block) + core) * block + key_row % block
    return (key <= query) & (key_pos < length)


def other_mask(tile, start, core, length, block):
    key = lax.broadcasted_iota(jnp.int32, (tile, tile), 0)
    query = lax.broadcasted_iota(jnp.int32, (tile, tile), 1)
    key_row = start + key
    key_pos = (2 * (key_row // block) + 1 - core) * block + key_row % block
    return (key // block <= query // block - (1 - core)) & (key_pos < length)


def attend_forward_kernel(tile, block, info, q_ref, ko_ref, vo_ref, kx_ref, vx_ref, out_ref, lse_ref):
    core, length = info[0], info[1]
    rows = q_ref.shape[0]
    lane = lax.broadcasted_iota(jnp.int32, (1, LANES), 1)
    vo_t = vo_ref[...].T
    vx_t = vx_ref[...].T
    for start in range(0, rows, tile):
        stop = start + tile
        mask_own = own_mask(tile, start, core, length, block)
        mask_other = other_mask(tile, start, core, length, block)
        query = q_ref[start:stop, :] * jnp.asarray(SCALE, BF16)
        outs = []
        for half in range(2):
            picked = jnp.where(lane // HEAD_DIM == half, query, jnp.zeros_like(query))
            s_own = dot_nt(ko_ref[:stop, :], picked)
            s_other = dot_nt(kx_ref[:stop, :], picked)
            d_own = jnp.where(mask_own, s_own[start:], MASKED)
            d_other = jnp.where(mask_other, s_other[start:], MASKED)
            if start:
                s_own = jnp.concatenate([s_own[:start], d_own], axis=0)
                s_other = jnp.concatenate([s_other[:start], d_other], axis=0)
            else:
                s_own, s_other = d_own, d_other
            top = jnp.maximum(
                jnp.max(s_own, axis=0, keepdims=True), jnp.max(s_other, axis=0, keepdims=True)
            )
            e_own = jnp.exp(s_own - top)
            e_other = jnp.exp(s_other - top)
            total = jnp.sum(e_own, axis=0, keepdims=True) + jnp.sum(e_other, axis=0, keepdims=True)
            lanes = slice(half * HEAD_DIM, (half + 1) * HEAD_DIM)
            mixed = dot_nn(vo_t[lanes, :stop], e_own.astype(BF16)) + dot_nn(
                vx_t[lanes, :stop], e_other.astype(BF16)
            )
            outs.append(mixed / total)
            lse_ref[0, half : half + 1, start:stop] = top + jnp.log(total)
        out_ref[start:stop, :] = jnp.concatenate(outs, axis=0).T.astype(BF16)


def attend_backward_kernel(
    tile, block, info, q_ref, ko_ref, vo_ref, kx_ref, vx_ref, go_ref, out_ref, lse_ref,
    dq_ref, dko_ref, dvo_ref, dkx_ref, dvx_ref, ako, avo, akx, avx,
):
    core, length = info[0], info[1]
    rows = q_ref.shape[0]
    lane = lax.broadcasted_iota(jnp.int32, (1, LANES), 1)
    ko_t = ko_ref[...].T
    kx_t = kx_ref[...].T
    for acc in (ako, avo, akx, avx):
        acc[...] = jnp.zeros_like(acc)
    for start in range(0, rows, tile):
        stop = start + tile
        mask_own = own_mask(tile, start, core, length, block)
        mask_other = other_mask(tile, start, core, length, block)
        query = q_ref[start:stop, :] * jnp.asarray(SCALE, BF16)
        grad = go_ref[start:stop, :]
        product = grad.astype(F32) * out_ref[start:stop, :].astype(F32)
        parts = []
        for half in range(2):
            mine = lane // HEAD_DIM == half
            picked = jnp.where(mine, query, jnp.zeros_like(query))
            grad_half = jnp.where(mine, grad, jnp.zeros_like(grad))
            pick = jnp.broadcast_to(jnp.where(mine, 1.0, 0.0).astype(F32), (8, LANES))
            inner = lax.dot_general(
                pick, product, (((1,), (1,)), ((), ())),
                precision=lax.Precision.HIGHEST, preferred_element_type=F32,
            )[:1]
            lse = lse_ref[0, half : half + 1, start:stop]
            lanes = slice(half * HEAD_DIM, (half + 1) * HEAD_DIM)
            part = jnp.zeros((HEAD_DIM, tile), F32)
            for key_ref, value_ref, key_t, mask, acc_k, acc_v in (
                (ko_ref, vo_ref, ko_t, mask_own, ako, avo),
                (kx_ref, vx_ref, kx_t, mask_other, akx, avx),
            ):
                prob = jnp.exp(dot_nt(key_ref[:stop, :], picked) - lse)
                last = jnp.where(mask, prob[start:], 0.0)
                prob = jnp.concatenate([prob[:start], last], axis=0) if start else last
                grad_prob = dot_nt(value_ref[:stop, :], grad_half)
                grad_score = (prob * (grad_prob - inner)).astype(BF16)
                acc_v[:stop, :] += dot_nn(prob.astype(BF16), grad_half)
                acc_k[:stop, :] += dot_nn(grad_score, picked)
                part = part + dot_nn(key_t[lanes, :stop], grad_score)
            parts.append(part)
        dq_ref[start:stop, :] = (jnp.concatenate(parts, axis=0) * SCALE).T.astype(BF16)
    for acc, ref in ((ako, dko_ref), (avo, dvo_ref), (akx, dkx_ref), (avx, dvx_ref)):
        ref[...] = acc[...].astype(ref.dtype)


def attend_forward(info, block, queries, keys_own, values_own, keys_other, values_other):
    rows, width = queries.shape
    pairs = width // LANES
    tile = min(256, rows)
    column = pl.BlockSpec((rows, LANES), lambda pair, info: (0, pair))
    return pl.pallas_call(
        functools.partial(attend_forward_kernel, tile, block),
        grid_spec=pltpu.PrefetchScalarGridSpec(
            num_scalar_prefetch=1,
            grid=(pairs,),
            in_specs=[column] * 5,
            out_specs=[column, pl.BlockSpec((1, 2, rows), lambda pair, info: (pair, 0, 0))],
        ),
        out_shape=[
            jax.ShapeDtypeStruct((rows, width), BF16),
            jax.ShapeDtypeStruct((pairs, 2, rows), F32),
        ],
        name="attend_forward",
    )(info, queries, keys_own, values_own, keys_other, values_other)


def attend_backward(info, block, queries, keys_own, values_own, keys_other, values_other, grad_heads, heads_out, lse):
    rows, width = queries.shape
    pairs = width // LANES
    tile = min(256, rows)
    column = pl.BlockSpec((rows, LANES), lambda pair, info: (0, pair))
    return pl.pallas_call(
        functools.partial(attend_backward_kernel, tile, block),
        grid_spec=pltpu.PrefetchScalarGridSpec(
            num_scalar_prefetch=1,
            grid=(pairs,),
            in_specs=[column] * 7 + [pl.BlockSpec((1, 2, rows), lambda pair, info: (pair, 0, 0))],
            out_specs=[column] * 5,
            scratch_shapes=[pltpu.VMEM((rows, LANES), F32)] * 4,
        ),
        out_shape=[
            jax.ShapeDtypeStruct((rows, width), BF16),
            jax.ShapeDtypeStruct((rows, width), F32),
            jax.ShapeDtypeStruct((rows, width), F32),
            jax.ShapeDtypeStruct((rows, width), BF16),
            jax.ShapeDtypeStruct((rows, width), BF16),
        ],
        name="attend_backward",
    )(info, queries, keys_own, values_own, keys_other, values_other, grad_heads, heads_out, lse)


def normalize(features):
    mean = jnp.mean(features, axis=-1, keepdims=True)
    centred = features - mean
    variance = jnp.mean(centred * centred, axis=-1, keepdims=True)
    scale = lax.rsqrt(variance + 1e-05)
    return centred * scale, scale


def norm_back(grad, gain, xhat, scale):
    scaled = grad * gain
    row = scale * (
        scaled
        - jnp.mean(scaled, axis=-1, keepdims=True)
        - xhat * jnp.mean(scaled * xhat, axis=-1, keepdims=True)
    )
    return row, jnp.sum(grad * xhat, axis=0), jnp.sum(grad, axis=0)


ROOT = 0.7978845608028654
CUBE = 0.044715


def gelu_and_slope(value):
    square = value * value
    turn = jnp.tanh(ROOT * value * (1.0 + CUBE * square))
    slope = 0.5 * (1.0 + turn) + 0.5 * value * (1.0 - turn * turn) * ROOT * (1.0 + 3.0 * CUBE * square)
    return 0.5 * value * (1.0 + turn), slope


def solution(mesh):
    groups = mesh.shape["dp"]
    bits = groups.bit_length() - 1
    assert groups == 1 << bits and mesh.shape["tensor"] == 2

    def pairs_of(change):
        table = []
        for group in range(groups):
            for side in range(2):
                to_group, to_side = change(group, side)
                table.append((group * 2 + side, to_group * 2 + to_side))
        return table

    tensor_pairs = pairs_of(lambda group, side: (group, 1 - side))
    bit_pairs = [pairs_of(lambda group, side, k=k: (group ^ (1 << k), side)) for k in range(bits)]
    deal_groups = [
        [group * 2 + side for group in range(core, groups, 2) for side in range(2)] for core in range(2)
    ]

    def body(
        tokens, cotangent, thoughts, latent_pos, lengths, dealing, qkv_weight, qv_bias, out_weight,
        out_bias, fc_weight, fc_bias, proj_weight, norm_gain, norm_shift,
    ):
        group = lax.axis_index("dp")
        side = lax.axis_index("tensor")
        core = group % 2
        slot = group - core + side
        slots, block, half_width = tokens.shape
        width = 2 * half_width
        rows = slots * block // 2
        hidden_half = fc_weight.shape[1]

        def cross(value):
            return lax.ppermute(value, AXES, tensor_pairs)

        def flip(value, bit=0):
            return lax.ppermute(value, AXES, bit_pairs[bit])

        def part(value, index):
            size = value.shape[0] // 2
            return lax.dynamic_slice_in_dim(value, index * size, size, 0)

        def join(flag, mine, theirs, axis=0):
            return jnp.where(
                flag == 0,
                jnp.concatenate([mine, theirs], axis=axis),
                jnp.concatenate([theirs, mine], axis=axis),
            )

        def fetch(weight):
            direct = cross(part(weight, core))
            return join(core, direct, flip(direct))

        def deal(array):
            pieces = lax.all_to_all(
                array[dealing], AXES, split_axis=0, concat_axis=0, tiled=True, axis_index_groups=deal_groups
            )
            pieces = pieces.reshape(slots // 2, 2, block, half_width)
            return pieces.transpose(0, 2, 1, 3).reshape(rows, width)

        restore = jnp.zeros_like(dealing).at[dealing].set(jnp.arange(slots, dtype=jnp.int32))

        def undeal(array):
            pieces = array.astype(BF16).reshape(slots // 2, block, 2, half_width).transpose(0, 2, 1, 3)
            pieces = lax.all_to_all(
                pieces.reshape(slots, block, half_width), AXES, split_axis=0, concat_axis=0, tiled=True,
                axis_index_groups=deal_groups,
            )
            return pieces[restore].astype(F32)

        dealt = deal(tokens)
        qkv_flat = qkv_weight.reshape(3 * width, half_width)
        qkv_other = fetch(qkv_flat).reshape(3, width, half_width)
        out_other = fetch(out_weight)
        fc_other = fetch(fc_weight)
        proj_other = fetch(proj_weight)
        biases_other = cross(jnp.concatenate([qv_bias.reshape(-1), fc_bias]))
        qv_other = biases_other[:width].reshape(2, half_width)
        fc_bias_other = biases_other[width:]
        thoughts_core = flip(thoughts[0])
        near = jnp.where(core == side, thoughts[0], thoughts_core)
        far = cross(jnp.where(core == side, thoughts_core, thoughts[0]))
        thought_rows = join(side, near, far, axis=1)
        latent_core = flip(latent_pos)
        latent = jnp.where(core == side, latent_pos, latent_core)[0]
        full_cot = deal(cotangent)

        local = jnp.arange(rows, dtype=jnp.int32)
        positions = (2 * (local // block) + core) * block + local % block
        length = lengths[dealing[slot]]
        info = jnp.stack([core, length]).astype(jnp.int32)
        valid = (positions < length).astype(F32)[:, None]

        hit = positions[:, None] == latent[None, :]
        placed = jnp.dot(hit.astype(BF16), thought_rows, preferred_element_type=F32)
        inputs = jnp.where(jnp.any(hit, axis=-1, keepdims=True), placed, dealt.astype(F32))
        xhat_in, rstd_in = normalize(inputs)
        normed = (xhat_in * norm_gain[0] + norm_shift[0]).astype(BF16)

        def project(index, bias):
            own = dot_nn(normed, qkv_weight[index])
            other = dot_nn(normed, qkv_other[index])
            if bias is not None:
                own, other = own + qv_bias[bias], other + qv_other[bias]
            return jnp.concatenate([own.astype(BF16), other.astype(BF16)], axis=1)

        keys_own = project(1, None)
        keys_other = flip(keys_own)
        values_own = project(2, 1)
        values_other = flip(values_own)
        queries = project(0, 0)
        heads_out, lse = attend_forward(info, block, queries, keys_own, values_own, keys_other, values_other)
        residual = inputs + (
            dot_nn(heads_out[:, :half_width], out_weight) + dot_nn(heads_out[:, half_width:], out_other) + out_bias[0]
        )
        xhat_mid, rstd_mid = normalize(residual)
        normed_mlp = (xhat_mid * norm_gain[1] + norm_shift[1]).astype(BF16)
        grad_out = valid * full_cot.astype(F32)
        grad_mlp = grad_out.astype(BF16)

        mlp = jnp.zeros((rows, width), F32)
        grad_normed_mlp = jnp.zeros((rows, width), F32)
        grad_proj, grad_fc, grad_fc_bias = [], [], []
        for fc, bias, proj in ((fc_weight, fc_bias, proj_weight), (fc_other, fc_bias_other, proj_other)):
            active, slope = gelu_and_slope(dot_nn(normed_mlp, fc) + bias)
            active = active.astype(BF16)
            mlp = mlp + dot_nn(active, proj)
            grad_proj.append(dot_tn(active, grad_mlp))
            grad_pre = (dot_nt(grad_mlp, proj) * slope).astype(BF16)
            grad_fc.append(dot_tn(normed_mlp, grad_pre))
            grad_fc_bias.append(jnp.sum(grad_pre.astype(F32), axis=0))
            grad_normed_mlp = grad_normed_mlp + dot_nt(grad_pre, fc)
        block_out = undeal(valid * (residual + (mlp + out_bias[1])))

        def reduce_weight(own, other):
            kept_own = part(own, core) + flip(part(own, 1 - core).astype(BF16)).astype(F32)
            kept_other = part(other, core) + flip(part(other, 1 - core).astype(BF16)).astype(F32)
            total = kept_own + cross(kept_other.astype(BF16)).astype(F32)
            for bit in range(1, bits):
                flag = (group >> bit) & 1
                total = part(total, flag) + flip(part(total, 1 - flag).astype(BF16), bit).astype(F32)
            piece = total.astype(BF16)
            for bit in reversed(range(bits)):
                flag = (group >> bit) & 1
                piece = join(flag, piece, flip(piece, bit))
            return piece.astype(F32)

        def reduce_small(vectors):
            total = jnp.concatenate(vectors)
            total = total + cross(total)
            for bit in range(bits):
                total = total + flip(total, bit)
            return total

        def own_half(vector, halves):
            return lax.dynamic_slice_in_dim(vector, side * halves, halves, vector.ndim - 1)

        grad_proj_weight = reduce_weight(*grad_proj)
        grad_fc_weight = reduce_weight(*grad_fc)
        row_grad, gain_mlp, shift_mlp = norm_back(grad_normed_mlp, norm_gain[1], xhat_mid, rstd_mid)
        grad_residual = grad_out + row_grad
        small_mlp = reduce_small(
            [join(side, grad_fc_bias[0], grad_fc_bias[1]), jnp.sum(grad_mlp.astype(F32), axis=0), gain_mlp, shift_mlp]
        )

        grad_attn = grad_residual.astype(BF16)
        grad_out_weight = reduce_weight(
            dot_tn(heads_out[:, :half_width], grad_attn), dot_tn(heads_out[:, half_width:], grad_attn)
        )
        grad_heads = jnp.concatenate(
            [dot_nt(grad_attn, out_weight).astype(BF16), dot_nt(grad_attn, out_other).astype(BF16)], axis=1
        )
        grad_q, grad_ko, grad_vo, grad_kx, grad_vx = attend_backward(
            info, block, queries, keys_own, values_own, keys_other, values_other, grad_heads, heads_out, lse
        )
        grad_k = (grad_ko + flip(grad_kx).astype(F32)).astype(BF16)
        grad_v = (grad_vo + flip(grad_vx).astype(F32)).astype(BF16)
        triple = (grad_q, grad_k, grad_v)
        grad_qkv = [
            jnp.concatenate([dot_tn(normed, rows_grad[:, lanes]) for rows_grad in triple], axis=0)
            for lanes in (slice(0, half_width), slice(half_width, width))
        ]
        grad_qkv_weight = reduce_weight(*grad_qkv).reshape(3, width, half_width)
        grad_normed = jnp.zeros((rows, width), F32)
        for index, rows_grad in enumerate(triple):
            grad_normed = grad_normed + (
                dot_nt(rows_grad[:, :half_width], qkv_weight[index])
                + dot_nt(rows_grad[:, half_width:], qkv_other[index])
            )
        row_grad, gain_attn, shift_attn = norm_back(grad_normed, norm_gain[0], xhat_in, rstd_in)
        input_grad = undeal(grad_residual + row_grad)

        def ordered(vector):
            return join(side, vector[:half_width], vector[half_width:])

        small_attn = reduce_small(
            [
                ordered(jnp.sum(grad_q.astype(F32), axis=0)),
                ordered(jnp.sum(grad_v.astype(F32), axis=0)),
                jnp.sum(grad_attn.astype(F32), axis=0),
                gain_attn,
                shift_attn,
            ]
        )
        hidden = 2 * hidden_half
        grad_fc_bias = own_half(small_mlp[:hidden], hidden_half)
        bias_mlp, gain_mlp, shift_mlp = small_mlp[hidden:].reshape(3, width)
        grad_qv_bias = own_half(small_attn[: 2 * width].reshape(2, width), half_width)
        bias_attn, gain_attn, shift_attn = small_attn[2 * width :].reshape(3, width)
        return (
            block_out,
            input_grad,
            grad_qkv_weight,
            grad_qv_bias,
            grad_out_weight,
            jnp.stack([bias_attn, bias_mlp]),
            grad_fc_weight,
            grad_fc_bias,
            grad_proj_weight,
            jnp.stack([gain_attn, gain_mlp]),
            jnp.stack([shift_attn, shift_mlp]),
        )

    return jax.shard_map(
        body,
        mesh=mesh,
        in_specs=(
            P(None, "dp", "tensor"),
            P(None, "dp", "tensor"),
            P("dp", None, "tensor"),
            P("dp", None),
            P(),
            P(),
            P(None, None, "tensor"),
            P(None, "tensor"),
            P("tensor", None),
            P(),
            P(None, "tensor"),
            P("tensor"),
            P("tensor", None),
            P(),
            P(),
        ),
        out_specs=(
            P(None, "dp", "tensor"),
            P(None, "dp", "tensor"),
            P(None, None, "tensor"),
            P(None, "tensor"),
            P("tensor", None),
            P(),
            P(None, "tensor"),
            P("tensor"),
            P("tensor", None),
            P(),
            P(),
        ),
        check_vma=False,
    )
```

```python
import functools

import jax
import jax.numpy as jnp
from jax import lax
from jax.experimental import pallas as pl
from jax.experimental.pallas import tpu as pltpu
from jax.sharding import PartitionSpec as P

HEAD_DIM = 64
LANES = 128
AXES = ("dp", "tensor")
SCALE = HEAD_DIM ** (-0.5)
MASKED = -1e30
BF16 = jnp.bfloat16
F32 = jnp.float32


def dot_nn(left, right):
    return lax.dot_general(left, right, (((1,), (0,)), ((), ())), preferred_element_type=F32)


def dot_nt(left, right):
    return lax.dot_general(left, right, (((1,), (1,)), ((), ())), preferred_element_type=F32)


def dot_tn(left, right):
    return lax.dot_general(left, right, (((0,), (0,)), ((), ())), preferred_element_type=F32)


def own_mask(tile, start, core, length, block):
    key = lax.broadcasted_iota(jnp.int32, (tile, tile), 0)
    query = lax.broadcasted_iota(jnp.int32, (tile, tile), 1)
    key_row = start + key
    key_pos = (2 * (key_row // block) + core) * block + key_row % block
    return (key <= query) & (key_pos < length)


def other_mask(tile, start, core, length, block):
    key = lax.broadcasted_iota(jnp.int32, (tile, tile), 0)
    query = lax.broadcasted_iota(jnp.int32, (tile, tile), 1)
    key_row = start + key
    key_pos = (2 * (key_row // block) + 1 - core) * block + key_row % block
    return (key // block <= query // block - (1 - core)) & (key_pos < length)


def attend_forward_kernel(tile, block, info, q_ref, ko_ref, vo_ref, kx_ref, vx_ref, out_ref, lse_ref):
    core, length = info[0], info[1]
    rows = q_ref.shape[0]
    lane = lax.broadcasted_iota(jnp.int32, (1, LANES), 1)
    vo_t = vo_ref[...].T
    vx_t = vx_ref[...].T
    for start in range(0, rows, tile):
        stop = start + tile
        mask_own = own_mask(tile, start, core, length, block)
        mask_other = other_mask(tile, start, core, length, block)
        query = q_ref[start:stop, :] * jnp.asarray(SCALE, BF16)
        outs = []
        for half in range(2):
            picked = jnp.where(lane // HEAD_DIM == half, query, jnp.zeros_like(query))
            s_own = dot_nt(ko_ref[:stop, :], picked)
            s_other = dot_nt(kx_ref[:stop, :], picked)
            d_own = jnp.where(mask_own, s_own[start:], MASKED)
            d_other = jnp.where(mask_other, s_other[start:], MASKED)
            if start:
                s_own = jnp.concatenate([s_own[:start], d_own], axis=0)
                s_other = jnp.concatenate([s_other[:start], d_other], axis=0)
            else:
                s_own, s_other = d_own, d_other
            top = jnp.maximum(
                jnp.max(s_own, axis=0, keepdims=True), jnp.max(s_other, axis=0, keepdims=True)
            )
            e_own = jnp.exp(s_own - top)
            e_other = jnp.exp(s_other - top)
            total = jnp.sum(e_own, axis=0, keepdims=True) + jnp.sum(e_other, axis=0, keepdims=True)
            lanes = slice(half * HEAD_DIM, (half + 1) * HEAD_DIM)
            mixed = dot_nn(vo_t[lanes, :stop], e_own.astype(BF16)) + dot_nn(
                vx_t[lanes, :stop], e_other.astype(BF16)
            )
            outs.append(mixed / total)
            lse_ref[0, half : half + 1, start:stop] = top + jnp.log(total)
        out_ref[start:stop, :] = jnp.concatenate(outs, axis=0).T.astype(BF16)


def attend_backward_kernel(
    tile, block, info, q_ref, ko_ref, vo_ref, kx_ref, vx_ref, go_ref, out_ref, lse_ref,
    dq_ref, dko_ref, dvo_ref, dkx_ref, dvx_ref, ako, avo, akx, avx,
):
    core, length = info[0], info[1]
    rows = q_ref.shape[0]
    lane = lax.broadcasted_iota(jnp.int32, (1, LANES), 1)
    ko_t = ko_ref[...].T
    kx_t = kx_ref[...].T
    for acc in (ako, avo, akx, avx):
        acc[...] = jnp.zeros_like(acc)
    for start in range(0, rows, tile):
        stop = start + tile
        mask_own = own_mask(tile, start, core, length, block)
        mask_other = other_mask(tile, start, core, length, block)
        query = q_ref[start:stop, :] * jnp.asarray(SCALE, BF16)
        grad = go_ref[start:stop, :]
        product = grad.astype(F32) * out_ref[start:stop, :].astype(F32)
        parts = []
        for half in range(2):
            mine = lane // HEAD_DIM == half
            picked = jnp.where(mine, query, jnp.zeros_like(query))
            grad_half = jnp.where(mine, grad, jnp.zeros_like(grad))
            pick = jnp.broadcast_to(jnp.where(mine, 1.0, 0.0).astype(F32), (8, LANES))
            inner = lax.dot_general(
                pick, product, (((1,), (1,)), ((), ())),
                precision=lax.Precision.HIGHEST, preferred_element_type=F32,
            )[:1]
            lse = lse_ref[0, half : half + 1, start:stop]
            lanes = slice(half * HEAD_DIM, (half + 1) * HEAD_DIM)
            part = jnp.zeros((HEAD_DIM, tile), F32)
            for key_ref, value_ref, key_t, mask, acc_k, acc_v in (
                (ko_ref, vo_ref, ko_t, mask_own, ako, avo),
                (kx_ref, vx_ref, kx_t, mask_other, akx, avx),
            ):
                prob = jnp.exp(dot_nt(key_ref[:stop, :], picked) - lse)
                last = jnp.where(mask, prob[start:], 0.0)
                prob = jnp.concatenate([prob[:start], last], axis=0) if start else last
                grad_prob = dot_nt(value_ref[:stop, :], grad_half)
                grad_score = (prob * (grad_prob - inner)).astype(BF16)
                acc_v[:stop, :] += dot_nn(prob.astype(BF16), grad_half)
                acc_k[:stop, :] += dot_nn(grad_score, picked)
                part = part + dot_nn(key_t[lanes, :stop], grad_score)
            parts.append(part)
        dq_ref[start:stop, :] = (jnp.concatenate(parts, axis=0) * SCALE).T.astype(BF16)
    for acc, ref in ((ako, dko_ref), (avo, dvo_ref), (akx, dkx_ref), (avx, dvx_ref)):
        ref[...] = acc[...].astype(ref.dtype)


def attend_forward(info, block, queries, keys_own, values_own, keys_other, values_other):
    rows, width = queries.shape
    pairs = width // LANES
    tile = min(256, rows)
    column = pl.BlockSpec((rows, LANES), lambda pair, info: (0, pair))
    return pl.pallas_call(
        functools.partial(attend_forward_kernel, tile, block),
        grid_spec=pltpu.PrefetchScalarGridSpec(
            num_scalar_prefetch=1,
            grid=(pairs,),
            in_specs=[column] * 5,
            out_specs=[column, pl.BlockSpec((1, 2, rows), lambda pair, info: (pair, 0, 0))],
        ),
        out_shape=[
            jax.ShapeDtypeStruct((rows, width), BF16),
            jax.ShapeDtypeStruct((pairs, 2, rows), F32),
        ],
        name="attend_forward",
    )(info, queries, keys_own, values_own, keys_other, values_other)


def attend_backward(info, block, queries, keys_own, values_own, keys_other, values_other, grad_heads, heads_out, lse):
    rows, width = queries.shape
    pairs = width // LANES
    tile = min(256, rows)
    column = pl.BlockSpec((rows, LANES), lambda pair, info: (0, pair))
    return pl.pallas_call(
        functools.partial(attend_backward_kernel, tile, block),
        grid_spec=pltpu.PrefetchScalarGridSpec(
            num_scalar_prefetch=1,
            grid=(pairs,),
            in_specs=[column] * 7 + [pl.BlockSpec((1, 2, rows), lambda pair, info: (pair, 0, 0))],
            out_specs=[column] * 5,
            scratch_shapes=[pltpu.VMEM((rows, LANES), F32)] * 4,
        ),
        out_shape=[
            jax.ShapeDtypeStruct((rows, width), BF16),
            jax.ShapeDtypeStruct((rows, width), F32),
            jax.ShapeDtypeStruct((rows, width), F32),
            jax.ShapeDtypeStruct((rows, width), BF16),
            jax.ShapeDtypeStruct((rows, width), BF16),
        ],
        name="attend_backward",
    )(info, queries, keys_own, values_own, keys_other, values_other, grad_heads, heads_out, lse)


HALF = 384


def spec(shape, index):
    return pl.BlockSpec(shape, index)


def whole(shape):
    zeros = (0,) * len(shape)
    return pl.BlockSpec(shape, lambda *_: zeros)


def call(kernel, name, grid, in_specs, out_specs, out_shape, scratch=()):
    return pl.pallas_call(
        kernel,
        grid_spec=pltpu.PrefetchScalarGridSpec(
            num_scalar_prefetch=1, grid=grid, in_specs=in_specs, out_specs=out_specs, scratch_shapes=list(scratch)
        ),
        out_shape=out_shape,
        name=name,
    )


def like(shape, dtype):
    return jax.ShapeDtypeStruct(shape, dtype)


def gather_slots(index, array, dtype):
    slots, block, width = array.shape
    steps = 4
    per = slots // steps

    def kernel(index_ref, array_ref, out_ref):
        first = pl.program_id(0) * per

        def copy(i, carry):
            out_ref[i] = array_ref[index_ref[first + i]].astype(dtype)
            return carry

        lax.fori_loop(0, per, copy, 0, unroll=min(per, 4))

    return call(
        kernel, "gather_slots", (steps,), [whole(array.shape)],
        spec((per, block, width), lambda i, _: (i, 0, 0)), like(array.shape, dtype),
    )(index, array)


def statistics(features):
    mean = jnp.mean(features, axis=-1, keepdims=True)
    centred = features - mean
    variance = jnp.mean(centred * centred, axis=-1, keepdims=True)
    scale = lax.rsqrt(variance + 1e-05)
    return centred * scale, scale


def norm_rows_back(grad, gain, xhat, scale):
    scaled = grad * gain
    return scale * (
        scaled
        - jnp.mean(scaled, axis=-1, keepdims=True)
        - xhat * jnp.mean(scaled * xhat, axis=-1, keepdims=True)
    )


def sum_rows(value):
    return jnp.sum(value, axis=0, keepdims=True)


def row_positions(tile, block, core):
    row = pl.program_id(0) * tile + lax.broadcasted_iota(jnp.int32, (tile, 1), 0)
    return (2 * (row // block) + core) * block + row % block


def rows_of(pieces_ref, tile):
    halves = [pieces_ref[:, side].astype(F32).reshape(tile, HALF) for side in range(2)]
    return jnp.concatenate(halves, axis=1)


def cols(index):
    return pl.ds(pl.multiple_of(index * HALF, LANES), HALF)


def rows_at(index):
    return pl.ds(pl.multiple_of(index * HALF, LANES), HALF)


ROOT = 0.7978845608028654
CUBE = 0.044715


def gelu_and_slope(value):
    square = value * value
    turn = jnp.tanh(ROOT * value * (1.0 + CUBE * square))
    slope = 0.5 * (1.0 + turn) + 0.5 * value * (1.0 - turn * turn) * ROOT * (1.0 + 3.0 * CUBE * square)
    return 0.5 * value * (1.0 + turn), slope


def enter_kernel(tile, block, info, pieces, thoughts, norms, bias_own, bias_other, own, direct, partner,
                 inputs_ref, normed_ref, q_ref, k_ref, v_ref):
    core = info[0]
    position = row_positions(tile, block, core)
    features = rows_of(pieces, tile)
    for index in range(6):
        features = jnp.where(position == info[2 + index], thoughts[index : index + 1, :], features)
    inputs_ref[...] = features
    xhat, _ = statistics(features)
    normed = (xhat * norms[0:1, :] + norms[1:2, :]).astype(BF16)
    normed_ref[...] = normed
    near = normed_ref[:, cols(core)]
    far = normed_ref[:, cols(1 - core)]
    for index, ref, bias in ((1, k_ref, None), (2, v_ref, 1), (0, q_ref, 0)):
        mine = dot_nn(normed, own[index])
        theirs = dot_nn(near, direct[index]) + dot_nn(far, partner[index])
        if bias is not None:
            mine = mine + bias_own[bias : bias + 1, :]
            theirs = theirs + bias_other[bias : bias + 1, :]
        ref[:, :HALF] = mine.astype(BF16)
        ref[:, HALF:] = theirs.astype(BF16)


def middle_kernel(tile, block, info, heads, inputs, pieces, norms, own, direct, partner,
                  residual_ref, normed_ref, grad_ref, mixed):
    core, length = info[0], info[1]
    position = row_positions(tile, block, core)
    grad = rows_of(pieces, tile)
    grad_ref[...] = jnp.where(position < length, grad, 0.0).astype(BF16)
    mixed[...] = dot_nn(heads[:, :HALF], own[...]) + norms[2:3, :]
    mixed[:, cols(core)] += dot_nn(heads[:, HALF:], direct[...])
    mixed[:, cols(1 - core)] += dot_nn(heads[:, HALF:], partner[...])
    residual = inputs[...] + mixed[...]
    residual_ref[...] = residual
    xhat, _ = statistics(residual)
    normed_ref[...] = (xhat * norms[0:1, :] + norms[1:2, :]).astype(BF16)


def mlp_kernel(first, info, normed, grad, *refs):
    core = info[0]
    step = pl.program_id(0)
    if first:
        fc_ref, bias, proj_ref, mlp_ref, back_ref, keep0, keep1, send0, send1, fcb_ref, normed_t, active_t = refs
        fc, proj = fc_ref[...], proj_ref[...]
    else:
        (fc_direct, fc_partner, bias, proj_direct, proj_partner, mlp_in, back_in,
         mlp_ref, back_ref, keep0, keep1, send0, send1, fcb_ref, normed_t, active_t) = refs
        near = core == step
        fc = jnp.where(near, fc_direct[...], fc_partner[...])
        proj = jnp.where(near, proj_direct[...], proj_partner[...])

    @pl.when(step == 0)
    def _():
        normed_t[...] = normed[...].T

    active, slope = gelu_and_slope(dot_nn(normed[...], fc) + bias[...])
    active = active.astype(BF16)
    active_t[...] = active.T
    grad_pre = (dot_nt(grad[...], proj) * slope).astype(BF16)
    mlp = dot_nn(active, proj)
    back = dot_nt(grad_pre, fc)
    fcb_ref[...] = sum_rows(grad_pre.astype(F32))

    @pl.when(step == 0)
    def _():
        mlp_ref[...] = mlp if first else mlp_in[...] + mlp
        back_ref[...] = back if first else back_in[...] + back

    @pl.when(step == 1)
    def _():
        mlp_ref[...] += mlp
        back_ref[...] += back

    for at, keep, send in ((0, keep0, send0), (1, keep1, send1)):
        @pl.when(step == at)
        def _(keep=keep, send=send):
            for index, ref in ((core, keep), (1 - core, send)):
                ref[:, : 2 * HALF] = dot_nn(normed_t[rows_at(index), :], grad_pre).astype(BF16)
                ref[:, 2 * HALF :] = dot_nn(active_t[rows_at(index), :], grad[...]).astype(BF16)


def back_kernel(tile, block, info, back, mlp, residual, grad, norms, own, direct, partner,
                grad_residual_ref, grad_attn_ref, grad_heads_ref, block_ref, small_ref):
    core, length = info[0], info[1]
    position = row_positions(tile, block, core)
    after = residual[...]
    block_out = jnp.where(position < length, after + (mlp[...] + norms[1:2, :]), 0.0)
    blocks = tile // block
    for side in range(2):
        block_ref[:, side] = block_out[:, side * HALF : (side + 1) * HALF].reshape(blocks, block, HALF).astype(BF16)
    xhat, scale = statistics(after)
    incoming = back[...]
    grad_out = grad[...].astype(F32)
    grad_residual = grad_out + norm_rows_back(incoming, norms[0:1, :], xhat, scale)
    grad_residual_ref[...] = grad_residual
    grad_attn = grad_residual.astype(BF16)
    grad_attn_ref[...] = grad_attn
    grad_heads_ref[:, :HALF] = dot_nt(grad_attn, own[...]).astype(BF16)
    theirs = dot_nt(grad_attn_ref[:, cols(core)], direct[...])
    theirs = theirs + dot_nt(grad_attn_ref[:, cols(1 - core)], partner[...])
    grad_heads_ref[:, HALF:] = theirs.astype(BF16)
    sums = jnp.concatenate(
        [sum_rows(incoming * xhat), sum_rows(incoming), sum_rows(grad_out), sum_rows(grad_attn.astype(F32))], axis=0
    )

    @pl.when(pl.program_id(0) == 0)
    def _():
        small_ref[...] = sums

    @pl.when(pl.program_id(0) > 0)
    def _():
        small_ref[...] += sums


def attention_grads_kernel(info, normed, heads, grad_attn, dq, dk, dk_far, dv, dv_far, keep, send, normed_t):
    core = info[0]

    @pl.when(pl.program_id(0) == 0)
    def _():
        normed_t[...] = normed[...].T

    grads = [
        dq[...],
        (dk[...] + dk_far[...].astype(F32)).astype(BF16),
        (dv[...] + dv_far[...].astype(F32)).astype(BF16),
    ]
    heads_t = heads[...].T
    for index, ref in ((core, keep), (1 - core, send)):
        left = normed_t[rows_at(index), :]
        for place, grad in enumerate(grads):
            ref[0, :, place * HALF : (place + 1) * HALF] = dot_nn(left, grad).astype(BF16)
        ref[0, :, 3 * HALF :] = dot_nn(heads_t, grad_attn[:, cols(index)]).astype(BF16)


def leave_kernel(tile, block, info, inputs, grad_residual, norms, dq, dk, dk_far, dv, dv_far, own, direct, partner,
                 pieces_ref, small_ref, back):
    core = info[0]
    grads = [
        dq[...],
        (dk[...] + dk_far[...].astype(F32)).astype(BF16),
        (dv[...] + dv_far[...].astype(F32)).astype(BF16),
    ]
    back[...] = sum(dot_nt(grad[:, :HALF], own[index]) for index, grad in enumerate(grads))
    back[:, cols(core)] += sum(dot_nt(grad[:, HALF:], direct[index]) for index, grad in enumerate(grads))
    back[:, cols(1 - core)] += sum(dot_nt(grad[:, HALF:], partner[index]) for index, grad in enumerate(grads))
    incoming = back[...]
    xhat, scale = statistics(inputs[...])
    result = grad_residual[...] + norm_rows_back(incoming, norms[0:1, :], xhat, scale)
    blocks = tile // block
    for side in range(2):
        pieces_ref[:, side] = result[:, side * HALF : (side + 1) * HALF].reshape(blocks, block, HALF).astype(BF16)
    sums = jnp.concatenate(
        [sum_rows(incoming * xhat), sum_rows(incoming), sum_rows(grads[0].astype(F32)), sum_rows(grads[2].astype(F32))],
        axis=0,
    )

    @pl.when(pl.program_id(0) == 0)
    def _():
        small_ref[...] = sums

    @pl.when(pl.program_id(0) > 0)
    def _():
        small_ref[...] += sums


def finish_mlp_kernel(info, mine0, theirs0, mine1, theirs1, fc_ref, proj_ref):
    core = info[0]
    for at, mine, theirs in ((0, mine0, theirs0), (1, mine1, theirs1)):
        @pl.when(pl.program_id(0) == at)
        def _(mine=mine, theirs=theirs):
            for index, ref in ((core, mine), (1 - core, theirs)):
                fc_ref[rows_at(index), :] = ref[:, : 2 * HALF].astype(F32)
                proj_ref[rows_at(index), :] = ref[:, 2 * HALF :].astype(F32)


def finish_attention_kernel(info, mine, theirs, qkv_ref, out_ref):
    core = info[0]
    for index, ref in ((core, mine), (1 - core, theirs)):
        for place in range(3):
            qkv_ref[place, rows_at(index), :] = ref[:, place * HALF : (place + 1) * HALF].astype(F32)
        out_ref[:, cols(index)] = ref[:, 3 * HALF :].astype(F32)


def solution(mesh):
    groups = mesh.shape["dp"]
    bits = groups.bit_length() - 1
    assert groups == 1 << bits and mesh.shape["tensor"] == 2

    def pairs_of(change):
        table = []
        for group in range(groups):
            for side in range(2):
                to_group, to_side = change(group, side)
                table.append((group * 2 + side, to_group * 2 + to_side))
        return table

    tensor_pairs = pairs_of(lambda group, side: (group, 1 - side))
    bit_pairs = [pairs_of(lambda group, side, k=k: (group ^ (1 << k), side)) for k in range(bits)]
    deal_groups = [
        [group * 2 + side for group in range(core, groups, 2) for side in range(2)] for core in range(2)
    ]

    def body(
        tokens, cotangent, thoughts, latent_pos, lengths, dealing, qkv_weight, qv_bias, out_weight,
        out_bias, fc_weight, fc_bias, proj_weight, norm_gain, norm_shift,
    ):
        group = lax.axis_index("dp")
        side = lax.axis_index("tensor")
        core = group % 2
        slot = group - core + side
        slots, block, half_width = tokens.shape
        width = 2 * half_width
        rows = slots * block // 2
        hidden_half = fc_weight.shape[1]
        assert half_width == HALF and hidden_half == 4 * HALF
        tile = 256
        blocks = tile // block

        def cross(value):
            return lax.ppermute(value, AXES, tensor_pairs)

        def flip(value, bit=0):
            return lax.ppermute(value, AXES, bit_pairs[bit])

        def part(value, index, axis=0):
            size = value.shape[axis] // 2
            return lax.dynamic_slice_in_dim(value, index * size, size, axis)

        def join(flag, mine, theirs, axis=0):
            return jnp.where(
                flag == 0,
                jnp.concatenate([mine, theirs], axis=axis),
                jnp.concatenate([theirs, mine], axis=axis),
            )

        def exchange(array):
            return lax.all_to_all(
                array, AXES, split_axis=0, concat_axis=0, tiled=True, axis_index_groups=deal_groups
            )

        def deal(array):
            return exchange(gather_slots(dealing, array, BF16)).reshape(slots // 2, 2, block, half_width)

        order = jnp.arange(slots, dtype=jnp.int32)
        restore = jnp.sum(jnp.where(dealing[None, :] == order[:, None], order[None, :], 0), axis=1)

        def undeal(pieces):
            return gather_slots(restore, exchange(pieces.reshape(slots, block, half_width)), F32)

        dealt = deal(tokens)
        qkv_direct = cross(part(qkv_weight, core, 1))
        qkv_partner = flip(qkv_direct)
        biases_other = cross(jnp.concatenate([qv_bias.reshape(-1), fc_bias]))
        qv_other = biases_other[:width].reshape(2, half_width)
        fc_bias_other = biases_other[width:].reshape(1, hidden_half)
        thoughts_core = flip(thoughts[0])
        near = jnp.where(core == side, thoughts[0], thoughts_core)
        far = cross(jnp.where(core == side, thoughts_core, thoughts[0]))
        thought_rows = join(side, near, far, axis=1).astype(F32)
        latent_core = flip(latent_pos)
        latent = jnp.where(core == side, latent_pos, latent_core)[0]
        length = lengths[dealing[slot]]
        info = jnp.concatenate([jnp.stack([core, length]).astype(jnp.int32), latent])

        later = (out_weight, fc_weight, proj_weight)
        out_weight_l, fc_weight_l, proj_weight_l, qkv_direct = lax.optimization_barrier((*later, qkv_direct))
        out_direct = cross(part(out_weight_l, core, 1))
        fc_direct = cross(part(fc_weight_l, core, 1))
        proj_direct = cross(part(proj_weight_l, core))
        out_partner = flip(out_direct)
        fc_partner = flip(fc_direct)
        proj_partner = flip(proj_direct)
        cot_pieces = deal(cotangent)

        steps = rows // tile
        rowwise = spec((tile, width), lambda i, _: (i, 0))
        pieces_spec = spec((blocks, 2, block, half_width), lambda i, _: (i, 0, 0, 0))
        qkv_specs = [whole(qkv_weight.shape), whole(qkv_direct.shape), whole(qkv_direct.shape)]
        out_specs = [whole(out_weight.shape), whole(out_direct.shape), whole(out_direct.shape)]
        rows_bf, rows_f = like((rows, width), BF16), like((rows, width), F32)

        inputs, normed, queries, keys_own, values_own = call(
            functools.partial(enter_kernel, tile, block), "enter", (steps,),
            [pieces_spec, whole((6, width)), whole((2, width)), whole((2, half_width)), whole((2, half_width)), *qkv_specs],
            [rowwise] * 5, [rows_f, rows_bf, rows_bf, rows_bf, rows_bf],
        )(info, dealt, thought_rows, jnp.stack([norm_gain[0], norm_shift[0]]), qv_bias, qv_other,
          qkv_weight, qkv_direct, qkv_partner)
        keys_other, values_other = flip(keys_own), flip(values_own)
        heads_out, lse = attend_forward(info, block, queries, keys_own, values_own, keys_other, values_other)

        residual, normed_mlp, grad_mlp = call(
            functools.partial(middle_kernel, tile, block), "middle", (steps,),
            [rowwise, rowwise, pieces_spec, whole((3, width)), *out_specs],
            [rowwise] * 3, [rows_f, rows_bf, rows_bf], [pltpu.VMEM((tile, width), F32)],
        )(info, heads_out, inputs, cot_pieces, jnp.stack([norm_gain[1], norm_shift[1], out_bias[0]]),
          out_weight, out_direct, out_partner)

        full = whole((rows, width))
        chunk = 2 * half_width
        quarter = like((half_width, 2 * chunk), BF16)
        mlp_outs = [full, full, *[whole(quarter.shape)] * 4, spec((1, chunk), lambda i, _: (0, i))]
        mlp_shapes = [rows_f, rows_f, quarter, quarter, quarter, quarter, like((1, hidden_half), F32)]
        mlp_scratch = [pltpu.VMEM((width, rows), BF16), pltpu.VMEM((chunk, rows), BF16)]
        bias_spec = spec((1, chunk), lambda i, _: (0, i))
        mlp, back, *grads_own, fcb_own = call(
            functools.partial(mlp_kernel, True), "mlp_own", (2,),
            [full, full, spec((width, chunk), lambda i, _: (0, i)), bias_spec, spec((chunk, width), lambda i, _: (i, 0))],
            mlp_outs, mlp_shapes, mlp_scratch,
        )(info, normed_mlp, grad_mlp, fc_weight, fc_bias.reshape(1, hidden_half), proj_weight)
        mlp, back, *grads_other, fcb_other = call(
            functools.partial(mlp_kernel, False), "mlp_other", (2,),
            [full, full, whole((width, chunk)), whole((width, chunk)), bias_spec, whole((chunk, width)),
             whole((chunk, width)), full, full],
            mlp_outs, mlp_shapes, mlp_scratch,
        )(info, normed_mlp, grad_mlp, fc_direct, fc_partner, fc_bias_other, proj_direct, proj_partner, mlp, back)

        def add(terms, index, size):
            total = 0.0
            for array, offset in terms:
                total = total + lax.dynamic_slice_in_dim(array, offset + index * size, size, 0).astype(F32)
            return total.astype(BF16)

        def reduce_quarter(own_terms, other_terms):
            size = own_terms[0].shape[0]
            sent = add([(term, 0) for term in other_terms], 0, size)
            terms = [(term, 0) for term in own_terms] + [(cross(sent), 0)]
            for bit in range(1, bits):
                flag = (group >> bit) & 1
                size //= 2
                received = flip(add(terms, 1 - flag, size), bit)
                terms = [(array, offset + flag * size) for array, offset in terms] + [(received, 0)]
            piece = add(terms, 0, size)
            for bit in reversed(range(1, bits)):
                piece = join((group >> bit) & 1, piece, flip(piece, bit))
            return piece

        quarters = []
        for at in range(2):
            keep_own, send_own = grads_own[at], grads_own[2 + at]
            keep_other, send_other = grads_other[at], grads_other[2 + at]
            mine = reduce_quarter([keep_own, flip(send_own)], [keep_other, flip(send_other)])
            quarters += [mine, flip(mine)]

        grad_residual, grad_attn, grad_heads, block_pieces, small_mlp = call(
            functools.partial(back_kernel, tile, block), "back", (steps,),
            [rowwise, rowwise, rowwise, rowwise, whole((2, width)), *out_specs],
            [rowwise, rowwise, rowwise, pieces_spec, whole((4, width))],
            [rows_f, rows_bf, rows_bf, like((slots // 2, 2, block, half_width), BF16), like((4, width), F32)],
        )(info, back, mlp, residual, grad_mlp, jnp.stack([norm_gain[1], out_bias[1]]), out_weight, out_direct, out_partner)
        block_out = undeal(block_pieces)

        grad_q, grad_ko, grad_vo, grad_kx, grad_vx = attend_backward(
            info, block, queries, keys_own, values_own, keys_other, values_other, grad_heads, heads_out, lse
        )
        far_k, far_v = flip(grad_kx), flip(grad_vx)
        by_half = spec((rows, half_width), lambda i, _: (0, i))
        stacked = spec((1, half_width, 2 * chunk), lambda i, _: (i, 0, 0))
        keep, send = call(
            attention_grads_kernel, "attention_grads", (2,),
            [full, by_half, full, *[by_half] * 5], [stacked] * 2,
            [like((2, half_width, 2 * chunk), BF16)] * 2, [pltpu.VMEM((width, rows), BF16)],
        )(info, normed, heads_out, grad_attn, grad_q, grad_ko, far_k, grad_vo, far_v)
        got = flip(send)
        mine = reduce_quarter([keep[0], got[0]], [keep[1], got[1]])
        qkv_grad, out_grad = call(
            finish_attention_kernel, "finish_attention", (1,), [whole(mine.shape)] * 2,
            [whole(qkv_weight.shape), whole(out_weight.shape)],
            [like(qkv_weight.shape, F32), like(out_weight.shape, F32)],
        )(info, mine, flip(mine))

        input_pieces, small_attn = call(
            functools.partial(leave_kernel, tile, block), "leave", (steps,),
            [rowwise, rowwise, whole((1, width)), *[rowwise] * 5, *qkv_specs],
            [pieces_spec, whole((4, width))],
            [like((slots // 2, 2, block, half_width), BF16), like((4, width), F32)],
            [pltpu.VMEM((tile, width), F32)],
        )(info, inputs, grad_residual, norm_gain[:1], grad_q, grad_ko, far_k, grad_vo, far_v,
          qkv_weight, qkv_direct, qkv_partner)
        input_grad = undeal(input_pieces)
        half_spec = spec((half_width, 2 * chunk), lambda i, _: (0, 0))
        fc_grad, proj_grad = call(
            finish_mlp_kernel, "finish_mlp", (2,), [half_spec] * 4,
            [spec((width, chunk), lambda i, _: (0, i)), spec((chunk, width), lambda i, _: (i, 0))],
            [like(fc_weight.shape, F32), like(proj_weight.shape, F32)],
        )(info, *quarters)

        def ordered(vectors):
            return join(side, vectors[:, : vectors.shape[1] // 2], vectors[:, vectors.shape[1] // 2 :], axis=1)

        hidden = 2 * hidden_half
        fcb = join(side, fcb_own, fcb_other, axis=1).reshape(hidden // width, width)
        small = jnp.concatenate([small_mlp, small_attn[:2], ordered(small_attn[2:]), fcb], axis=0)
        small = small + flip(small)
        small = small + cross(small)
        for bit in range(1, bits):
            small = small + flip(small, bit)
        gain_mlp, shift_mlp, bias_mlp, bias_attn, gain_attn, shift_attn = (small[i] for i in range(6))
        return (
            block_out,
            input_grad,
            qkv_grad,
            part(small[6:8], side, 1),
            out_grad,
            jnp.stack([bias_attn, bias_mlp]),
            fc_grad,
            part(small[8:].reshape(hidden), side),
            proj_grad,
            jnp.stack([gain_attn, gain_mlp]),
            jnp.stack([shift_attn, shift_mlp]),
        )

    return jax.shard_map(
        body,
        mesh=mesh,
        in_specs=(
            P(None, "dp", "tensor"),
            P(None, "dp", "tensor"),
            P("dp", None, "tensor"),
            P("dp", None),
            P(),
            P(),
            P(None, None, "tensor"),
            P(None, "tensor"),
            P("tensor", None),
            P(),
            P(None, "tensor"),
            P("tensor"),
            P("tensor", None),
            P(),
            P(),
        ),
        out_specs=(
            P(None, "dp", "tensor"),
            P(None, "dp", "tensor"),
            P(None, None, "tensor"),
            P(None, "tensor"),
            P("tensor", None),
            P(),
            P(None, "tensor"),
            P("tensor"),
            P("tensor", None),
            P(),
            P(),
        ),
        check_vma=False,
    )
```

```python
import functools

import jax
import jax.numpy as jnp
from jax import lax
from jax.experimental import pallas as pl
from jax.experimental.pallas import tpu as pltpu
from jax.sharding import PartitionSpec as P

HEAD_DIM = 64
LANES = 128
AXES = ("dp", "tensor")
SCALE = HEAD_DIM ** (-0.5)
MASKED = -1e30
BF16 = jnp.bfloat16
F32 = jnp.float32


def dot_nn(left, right):
    return lax.dot_general(left, right, (((1,), (0,)), ((), ())), preferred_element_type=F32)


def dot_nt(left, right):
    return lax.dot_general(left, right, (((1,), (1,)), ((), ())), preferred_element_type=F32)


def dot_tn(left, right):
    return lax.dot_general(left, right, (((0,), (0,)), ((), ())), preferred_element_type=F32)


def own_mask(tile, start, core, length, block):
    key = lax.broadcasted_iota(jnp.int32, (tile, tile), 0)
    query = lax.broadcasted_iota(jnp.int32, (tile, tile), 1)
    key_row = start + key
    key_pos = (2 * (key_row // block) + core) * block + key_row % block
    return (key <= query) & (key_pos < length)


def other_mask(tile, start, core, length, block):
    key = lax.broadcasted_iota(jnp.int32, (tile, tile), 0)
    query = lax.broadcasted_iota(jnp.int32, (tile, tile), 1)
    key_row = start + key
    key_pos = (2 * (key_row // block) + 1 - core) * block + key_row % block
    return (key // block <= query // block - (1 - core)) & (key_pos < length)


def attend_forward_kernel(tile, block, info, q_ref, ko_ref, vo_ref, kx_ref, vx_ref, out_ref, lse_ref):
    core, length = info[0], info[1]
    rows = q_ref.shape[0]
    lane = lax.broadcasted_iota(jnp.int32, (1, LANES), 1)
    vo_t = vo_ref[...].T
    vx_t = vx_ref[...].T
    for start in range(0, rows, tile):
        stop = start + tile
        mask_own = own_mask(tile, start, core, length, block)
        mask_other = other_mask(tile, start, core, length, block)
        query = q_ref[start:stop, :] * jnp.asarray(SCALE, BF16)
        outs = []
        for half in range(2):
            picked = jnp.where(lane // HEAD_DIM == half, query, jnp.zeros_like(query))
            s_own = dot_nt(ko_ref[:stop, :], picked)
            s_other = dot_nt(kx_ref[:stop, :], picked)
            d_own = jnp.where(mask_own, s_own[start:], MASKED)
            d_other = jnp.where(mask_other, s_other[start:], MASKED)
            if start:
                s_own = jnp.concatenate([s_own[:start], d_own], axis=0)
                s_other = jnp.concatenate([s_other[:start], d_other], axis=0)
            else:
                s_own, s_other = d_own, d_other
            top = jnp.maximum(
                jnp.max(s_own, axis=0, keepdims=True), jnp.max(s_other, axis=0, keepdims=True)
            )
            e_own = jnp.exp(s_own - top)
            e_other = jnp.exp(s_other - top)
            total = jnp.sum(e_own, axis=0, keepdims=True) + jnp.sum(e_other, axis=0, keepdims=True)
            lanes = slice(half * HEAD_DIM, (half + 1) * HEAD_DIM)
            mixed = dot_nn(vo_t[lanes, :stop], e_own.astype(BF16)) + dot_nn(
                vx_t[lanes, :stop], e_other.astype(BF16)
            )
            outs.append(mixed / total)
            lse_ref[0, half : half + 1, start:stop] = top + jnp.log(total)
        out_ref[start:stop, :] = jnp.concatenate(outs, axis=0).T.astype(BF16)


def attend_backward_kernel(
    tile, block, info, q_ref, ko_ref, vo_ref, kx_ref, vx_ref, go_ref, out_ref, lse_ref,
    dq_ref, dko_ref, dvo_ref, dkx_ref, dvx_ref, ako, avo, akx, avx,
):
    core, length = info[0], info[1]
    rows = q_ref.shape[0]
    lane = lax.broadcasted_iota(jnp.int32, (1, LANES), 1)
    ko_t = ko_ref[...].T
    kx_t = kx_ref[...].T
    for acc in (ako, avo, akx, avx):
        acc[...] = jnp.zeros_like(acc)
    for start in range(0, rows, tile):
        stop = start + tile
        mask_own = own_mask(tile, start, core, length, block)
        mask_other = other_mask(tile, start, core, length, block)
        query = q_ref[start:stop, :] * jnp.asarray(SCALE, BF16)
        grad = go_ref[start:stop, :]
        product = grad.astype(F32) * out_ref[start:stop, :].astype(F32)
        parts = []
        for half in range(2):
            mine = lane // HEAD_DIM == half
            picked = jnp.where(mine, query, jnp.zeros_like(query))
            grad_half = jnp.where(mine, grad, jnp.zeros_like(grad))
            pick = jnp.broadcast_to(jnp.where(mine, 1.0, 0.0).astype(F32), (8, LANES))
            inner = lax.dot_general(
                pick, product, (((1,), (1,)), ((), ())),
                precision=lax.Precision.HIGHEST, preferred_element_type=F32,
            )[:1]
            lse = lse_ref[0, half : half + 1, start:stop]
            lanes = slice(half * HEAD_DIM, (half + 1) * HEAD_DIM)
            part = jnp.zeros((HEAD_DIM, tile), F32)
            for key_ref, value_ref, key_t, mask, acc_k, acc_v in (
                (ko_ref, vo_ref, ko_t, mask_own, ako, avo),
                (kx_ref, vx_ref, kx_t, mask_other, akx, avx),
            ):
                prob = jnp.exp(dot_nt(key_ref[:stop, :], picked) - lse)
                last = jnp.where(mask, prob[start:], 0.0)
                prob = jnp.concatenate([prob[:start], last], axis=0) if start else last
                grad_prob = dot_nt(value_ref[:stop, :], grad_half)
                grad_score = (prob * (grad_prob - inner)).astype(BF16)
                acc_v[:stop, :] += dot_nn(prob.astype(BF16), grad_half)
                acc_k[:stop, :] += dot_nn(grad_score, picked)
                part = part + dot_nn(key_t[lanes, :stop], grad_score)
            parts.append(part)
        dq_ref[start:stop, :] = (jnp.concatenate(parts, axis=0) * SCALE).T.astype(BF16)
    for acc, ref in ((ako, dko_ref), (avo, dvo_ref), (akx, dkx_ref), (avx, dvx_ref)):
        ref[...] = acc[...].astype(ref.dtype)


def attend_forward(info, block, queries, keys_own, values_own, keys_other, values_other):
    rows, width = queries.shape
    pairs = width // LANES
    tile = min(256, rows)
    column = pl.BlockSpec((rows, LANES), lambda pair, info: (0, pair))
    return pl.pallas_call(
        functools.partial(attend_forward_kernel, tile, block),
        grid_spec=pltpu.PrefetchScalarGridSpec(
            num_scalar_prefetch=1,
            grid=(pairs,),
            in_specs=[column] * 5,
            out_specs=[column, pl.BlockSpec((1, 2, rows), lambda pair, info: (pair, 0, 0))],
        ),
        out_shape=[
            jax.ShapeDtypeStruct((rows, width), BF16),
            jax.ShapeDtypeStruct((pairs, 2, rows), F32),
        ],
        name="attend_forward",
    )(info, queries, keys_own, values_own, keys_other, values_other)


def attend_backward(info, block, first, pairs, queries, keys_own, values_own, keys_other, values_other, grad_heads,
                    heads_out, lse):
    rows = queries.shape[0]
    tile = min(256, rows)
    column = pl.BlockSpec((rows, LANES), lambda pair, info: (0, first + pair))
    result = pl.BlockSpec((rows, LANES), lambda pair, info: (0, pair))
    dtypes = (BF16, F32, F32, BF16, BF16)
    return pl.pallas_call(
        functools.partial(attend_backward_kernel, tile, block),
        grid_spec=pltpu.PrefetchScalarGridSpec(
            num_scalar_prefetch=1,
            grid=(pairs,),
            in_specs=[column] * 7 + [pl.BlockSpec((1, 2, rows), lambda pair, info: (first + pair, 0, 0))],
            out_specs=[result] * 5,
            scratch_shapes=[pltpu.VMEM((rows, LANES), F32)] * 4,
        ),
        out_shape=[jax.ShapeDtypeStruct((rows, pairs * LANES), dtype) for dtype in dtypes],
        name="attend_backward",
    )(info, queries, keys_own, values_own, keys_other, values_other, grad_heads, heads_out, lse)


HALF = 384


def spec(shape, index):
    return pl.BlockSpec(shape, index)


def whole(shape):
    zeros = (0,) * len(shape)
    return pl.BlockSpec(shape, lambda *_: zeros)


def call(kernel, name, grid, in_specs, out_specs, out_shape, scratch=()):
    return pl.pallas_call(
        kernel,
        grid_spec=pltpu.PrefetchScalarGridSpec(
            num_scalar_prefetch=1, grid=grid, in_specs=in_specs, out_specs=out_specs, scratch_shapes=list(scratch)
        ),
        out_shape=out_shape,
        name=name,
    )


def like(shape, dtype):
    return jax.ShapeDtypeStruct(shape, dtype)


def gather_slots(index, array, dtype):
    slots, block, width = array.shape
    steps = 4
    per = slots // steps

    def kernel(index_ref, array_ref, out_ref):
        first = pl.program_id(0) * per

        def copy(i, carry):
            out_ref[i] = array_ref[index_ref[first + i]].astype(dtype)
            return carry

        lax.fori_loop(0, per, copy, 0, unroll=min(per, 4))

    return call(
        kernel, "gather_slots", (steps,), [whole(array.shape)],
        spec((per, block, width), lambda i, _: (i, 0, 0)), like(array.shape, dtype),
    )(index, array)


def statistics(features):
    mean = jnp.mean(features, axis=-1, keepdims=True)
    centred = features - mean
    variance = jnp.mean(centred * centred, axis=-1, keepdims=True)
    scale = lax.rsqrt(variance + 1e-05)
    return centred * scale, scale


def norm_rows_back(grad, gain, xhat, scale):
    scaled = grad * gain
    return scale * (
        scaled
        - jnp.mean(scaled, axis=-1, keepdims=True)
        - xhat * jnp.mean(scaled * xhat, axis=-1, keepdims=True)
    )


def sum_rows(value):
    return jnp.sum(value, axis=0, keepdims=True)


def row_positions(tile, block, core):
    row = pl.program_id(0) * tile + lax.broadcasted_iota(jnp.int32, (tile, 1), 0)
    return (2 * (row // block) + core) * block + row % block


def rows_of(pieces_ref, tile):
    halves = [pieces_ref[:, side].astype(F32).reshape(tile, HALF) for side in range(2)]
    return jnp.concatenate(halves, axis=1)


def cols(index):
    return pl.ds(pl.multiple_of(index * HALF, LANES), HALF)


def rows_at(index):
    return pl.ds(pl.multiple_of(index * HALF, LANES), HALF)


ROOT = 0.7978845608028654
CUBE = 0.044715


def gelu_and_slope(value):
    square = value * value
    turn = jnp.tanh(ROOT * value * (1.0 + CUBE * square))
    slope = 0.5 * (1.0 + turn) + 0.5 * value * (1.0 - turn * turn) * ROOT * (1.0 + 3.0 * CUBE * square)
    return 0.5 * value * (1.0 + turn), slope


def enter_kernel(tile, block, info, pieces, thoughts, norms, bias_own, bias_other, own, direct, partner,
                 inputs_ref, normed_ref, k_ref, v_ref):
    core = info[0]
    position = row_positions(tile, block, core)
    features = rows_of(pieces, tile)
    for index in range(6):
        features = jnp.where(position == info[2 + index], thoughts[index : index + 1, :], features)
    inputs_ref[...] = features
    xhat, _ = statistics(features)
    normed = (xhat * norms[0:1, :] + norms[1:2, :]).astype(BF16)
    normed_ref[...] = normed
    project(core, normed_ref, own[1], direct[0], partner[0], None, None, k_ref)
    project(core, normed_ref, own[2], direct[1], partner[1], bias_own[1:2, :], bias_other[1:2, :], v_ref)


def project(core, normed, own, direct, partner, bias_own, bias_other, ref):
    mine = dot_nn(normed[...], own)
    theirs = dot_nn(normed[:, cols(core)], direct) + dot_nn(normed[:, cols(1 - core)], partner)
    if bias_own is not None:
        mine = mine + bias_own
        theirs = theirs + bias_other
    ref[:, :HALF] = mine.astype(BF16)
    ref[:, HALF:] = theirs.astype(BF16)


def queries_kernel(info, normed, bias_own, bias_other, own, direct, partner, q_ref):
    project(info[0], normed, own[0], direct[0], partner[0], bias_own[0:1, :], bias_other[0:1, :], q_ref)


def cotangent_kernel(tile, block, info, pieces, grad_ref):
    position = row_positions(tile, block, info[0])
    grad_ref[...] = jnp.where(position < info[1], rows_of(pieces, tile), 0.0).astype(BF16)


def middle_kernel(info, heads, inputs, norms, own, direct, partner, residual_ref, normed_ref, mixed):
    core = info[0]
    mixed[...] = dot_nn(heads[:, :HALF], own[...]) + norms[2:3, :]
    mixed[:, cols(core)] += dot_nn(heads[:, HALF:], direct[...])
    mixed[:, cols(1 - core)] += dot_nn(heads[:, HALF:], partner[...])
    residual = inputs[...] + mixed[...]
    residual_ref[...] = residual
    xhat, _ = statistics(residual)
    normed_ref[...] = (xhat * norms[0:1, :] + norms[1:2, :]).astype(BF16)


def mlp_rows_kernel(info, normed, grad, fc, bias, proj, mlp_ref, back_ref, active_t_ref, pre_ref, fcb_ref, mlp_sum, back_sum):
    step = pl.program_id(0)
    active, slope = gelu_and_slope(dot_nn(normed[...], fc[...]) + bias[...])
    active = active.astype(BF16)
    active_t_ref[...] = active.T
    grad_pre = (dot_nt(grad[...], proj[...]) * slope).astype(BF16)
    pre_ref[...] = grad_pre
    fcb_ref[...] = sum_rows(grad_pre.astype(F32))
    mlp = dot_nn(active, proj[...])
    back = dot_nt(grad_pre, fc[...])

    @pl.when(step == 0)
    def _():
        mlp_sum[...] = mlp
        back_sum[...] = back

    @pl.when(step > 0)
    def _():
        mlp_ref[...] = (mlp_sum[...] + mlp).astype(mlp_ref.dtype)
        back_ref[...] = (back_sum[...] + back).astype(back_ref.dtype)


def mlp_grads_kernel(info, normed0, normed1, grad0, grad1, active0, active1, pre0, pre1, keep, send, normed_t):
    core = info[0]

    @pl.when(pl.program_id(0) == 0)
    def _():
        normed_t[0] = normed0[...].T
        normed_t[1] = normed1[...].T

    for index, ref in ((core, keep), (1 - core, send)):
        fc = dot_nn(normed_t[0, rows_at(index), :], pre0[...]) + dot_nn(normed_t[1, rows_at(index), :], pre1[...])
        proj = dot_nn(active0[rows_at(index), :], grad0[...]) + dot_nn(active1[rows_at(index), :], grad1[...])
        ref[:, : 2 * HALF] = fc.astype(BF16)
        ref[:, 2 * HALF :] = proj.astype(BF16)


def back_kernel(info, back, back_far, residual, grad, norms, own, direct, partner,
                grad_residual_ref, grad_attn_ref, grad_heads_ref, small_ref):
    core = info[0]
    xhat, scale = statistics(residual[...])
    incoming = back[...] + back_far[...].astype(F32)
    grad_out = grad[...].astype(F32)
    grad_residual = grad_out + norm_rows_back(incoming, norms[0:1, :], xhat, scale)
    grad_residual_ref[...] = grad_residual
    grad_attn = grad_residual.astype(BF16)
    grad_attn_ref[...] = grad_attn
    grad_heads_ref[:, :HALF] = dot_nt(grad_attn, own[...]).astype(BF16)
    theirs = dot_nt(grad_attn_ref[:, cols(core)], direct[...])
    theirs = theirs + dot_nt(grad_attn_ref[:, cols(1 - core)], partner[...])
    grad_heads_ref[:, HALF:] = theirs.astype(BF16)
    sums = jnp.concatenate(
        [sum_rows(incoming * xhat), sum_rows(incoming), sum_rows(grad_out), sum_rows(grad_attn.astype(F32))], axis=0
    )

    @pl.when(pl.program_id(0) == 0)
    def _():
        small_ref[...] = sums

    @pl.when(pl.program_id(0) > 0)
    def _():
        small_ref[...] += sums


def block_kernel(tile, block, info, residual, mlp, mlp_far, bias, block_ref):
    position = row_positions(tile, block, info[0])
    result = residual[...] + (mlp[...] + mlp_far[...].astype(F32) + bias[...])
    result = jnp.where(position < info[1], result, 0.0)
    for side in range(2):
        half = result[:, side * HALF : (side + 1) * HALF].reshape(tile // block, block, HALF)
        block_ref[:, side] = half.astype(BF16)


def key_value_grads(dk, dk_far, dv, dv_far):
    return (
        (dk[...] + dk_far[...].astype(F32)).astype(BF16),
        (dv[...] + dv_far[...].astype(F32)).astype(BF16),
    )


def attention_grads_kernel(info, normed, heads, grad_attn, dq, dk, dk_far, dv, dv_far, keep, send, normed_t):
    core = info[0]
    normed_t[...] = normed[...].T
    grads = (dq[...], *key_value_grads(dk, dk_far, dv, dv_far))
    heads_t = heads[...].T
    for index, ref in ((1 - core, send), (core, keep)):
        left = normed_t[rows_at(index), :]
        for place, grad in enumerate(grads):
            ref[:, place * HALF : (place + 1) * HALF] = dot_nn(left, grad).astype(BF16)
        ref[:, 3 * HALF :] = dot_nn(heads_t, grad_attn[:, cols(index)]).astype(BF16)


def leave_kernel(tile, block, info, inputs, grad_residual, norms, dq0, dk0, dk_far0, dv0, dv_far0,
                 dq1, dk1, dk_far1, dv1, dv_far1, own, direct, partner, direct_q, partner_q, pieces_ref, small_ref, back):
    core = info[0]
    mine = (dq0[...], *key_value_grads(dk0, dk_far0, dv0, dv_far0))
    theirs = (dq1[...], *key_value_grads(dk1, dk_far1, dv1, dv_far1))
    back[...] = sum(dot_nt(grad, own[index]) for index, grad in enumerate(mine))
    far_q, far_k, far_v = theirs
    back[:, cols(core)] += dot_nt(far_q, direct_q[0]) + dot_nt(far_k, direct[0]) + dot_nt(far_v, direct[1])
    back[:, cols(1 - core)] += dot_nt(far_q, partner_q[0]) + dot_nt(far_k, partner[0]) + dot_nt(far_v, partner[1])
    incoming = back[...]
    xhat, scale = statistics(inputs[...])
    result = grad_residual[...] + norm_rows_back(incoming, norms[0:1, :], xhat, scale)
    blocks = tile // block
    for side in range(2):
        pieces_ref[:, side] = result[:, side * HALF : (side + 1) * HALF].reshape(blocks, block, HALF).astype(BF16)
    biases = [
        jnp.concatenate([sum_rows(mine[place].astype(F32)), sum_rows(theirs[place].astype(F32))], axis=1)
        for place in (0, 2)
    ]
    sums = jnp.concatenate([sum_rows(incoming * xhat), sum_rows(incoming), *biases], axis=0)

    @pl.when(pl.program_id(0) == 0)
    def _():
        small_ref[...] = sums

    @pl.when(pl.program_id(0) > 0)
    def _():
        small_ref[...] += sums


def split_kernel(size, bases, info, *refs):
    terms, outs = refs[: len(bases)], refs[len(bases) :]
    place, near = info[9], info[8]
    for k, out in enumerate(outs):
        offset = jnp.bitwise_xor(place, k) * size
        total, received = 0.0, []
        for term, based in zip(terms, bases):
            start = offset + near * (4 * size) if based else offset
            value = term[pl.ds(pl.multiple_of(start, 16), size), :].astype(F32)
            if term.shape[1] == out.shape[1]:
                total = total + value
            else:
                received.append(value)
        if received:
            total = total + jnp.concatenate(received, axis=1)
        out[...] = total.astype(out.dtype)


def finish_rows(info, refs):
    core = info[0]
    pieces, size = refs[0].shape[0], refs[0].shape[1]
    for index, ref in enumerate(refs):
        base = (core if index < len(refs) // 2 else 1 - core) * HALF
        if pieces > 1:
            base = base + (info[8] if index % 2 == 0 else 1 - info[8]) * (HALF // 2)
        for k in range(pieces):
            start = base + jnp.bitwise_xor(info[9], k) * size if pieces > 1 else base
            yield pl.ds(pl.multiple_of(start, 8), size), ref, k


def finish_mlp_kernel(count, info, *refs):
    fc_ref, proj_ref = refs[count:]
    for rows, ref, k in finish_rows(info, refs[:count]):
        fc_ref[rows, :] = ref[k, :, : 2 * HALF].astype(F32)
        proj_ref[rows, :] = ref[k, :, 2 * HALF :].astype(F32)


def finish_attention_kernel(count, info, *refs):
    qkv_ref, turned_ref = refs[count:]
    for rows, ref, k in finish_rows(info, refs[:count]):
        for place in range(3):
            qkv_ref[place, rows, :] = ref[k, :, place * HALF : (place + 1) * HALF].astype(F32)
        turned_ref[rows, :] = ref[k, :, 3 * HALF :].astype(F32)


def solution(mesh):
    groups = mesh.shape["dp"]
    bits = groups.bit_length() - 1
    assert groups == 1 << bits and mesh.shape["tensor"] == 2

    def pairs_of(change):
        table = []
        for group in range(groups):
            for side in range(2):
                to_group, to_side = change(group, side)
                table.append((group * 2 + side, to_group * 2 + to_side))
        return table

    tensor_pairs = pairs_of(lambda group, side: (group, 1 - side))
    upper_pairs = [pairs_of(lambda group, side, k=k: (group ^ (k << 2), side)) for k in range(4)] if bits == 4 else []
    bit_pairs = [pairs_of(lambda group, side, k=k: (group ^ (1 << k), side)) for k in range(bits)]
    deal_groups = [
        [group * 2 + side for group in range(core, groups, 2) for side in range(2)] for core in range(2)
    ]

    def body(
        tokens, cotangent, thoughts, latent_pos, lengths, dealing, qkv_weight, qv_bias, out_weight,
        out_bias, fc_weight, fc_bias, proj_weight, norm_gain, norm_shift,
    ):
        group = lax.axis_index("dp")
        side = lax.axis_index("tensor")
        core = group % 2
        slot = group - core + side
        slots, block, half_width = tokens.shape
        width = 2 * half_width
        rows = slots * block // 2
        hidden_half = fc_weight.shape[1]
        assert half_width == HALF and hidden_half == 4 * HALF
        tile = 256
        blocks = tile // block

        def cross(value):
            return lax.ppermute(value, AXES, tensor_pairs)

        def flip(value, bit=0):
            return lax.ppermute(value, AXES, bit_pairs[bit])

        def part(value, index, axis=0):
            size = value.shape[axis] // 2
            return lax.dynamic_slice_in_dim(value, index * size, size, axis)

        def join(flag, mine, theirs, axis=0):
            return jnp.where(
                flag == 0,
                jnp.concatenate([mine, theirs], axis=axis),
                jnp.concatenate([theirs, mine], axis=axis),
            )

        def exchange(array):
            return lax.all_to_all(
                array, AXES, split_axis=0, concat_axis=0, tiled=True, axis_index_groups=deal_groups
            )

        def deal(array):
            return exchange(gather_slots(dealing, array, BF16)).reshape(slots // 2, 2, block, half_width)

        order = jnp.arange(slots, dtype=jnp.int32)
        restore = jnp.sum(jnp.where(dealing[None, :] == order[:, None], order[None, :], 0), axis=1)

        qkv_sent = part(qkv_weight, core, 1)
        dealt = deal(tokens)
        kv_direct = cross(qkv_sent[1:])
        kv_partner = flip(kv_direct)
        biases_other = cross(qv_bias)
        thoughts_core = flip(thoughts[0])
        near = jnp.where(core == side, thoughts[0], thoughts_core)
        far = cross(jnp.where(core == side, thoughts_core, thoughts[0]))
        latent_core = flip(latent_pos)
        latent = jnp.where(core == side, latent_pos, latent_core)[0]
        length = lengths[dealing[slot]]
        info = jnp.concatenate(
            [jnp.stack([core, length]).astype(jnp.int32), latent, jnp.stack([(group >> 1) & 1, group >> 2]).astype(jnp.int32)]
        )

        cot_dealt = gather_slots(dealing, cotangent, BF16)
        out_sent = part(out_weight, core, 1)
        q_sent, out_sent, kv_direct, cot_dealt, far, biases_other = lax.optimization_barrier(
            (qkv_sent[:1], out_sent, kv_direct, cot_dealt, far, biases_other)
        )
        q_direct = cross(q_sent)
        thought_rows = join(side, near, far, axis=1).astype(F32)
        qv_other = biases_other
        out_direct = cross(out_sent)
        cot_pieces = exchange(cot_dealt).reshape(slots // 2, 2, block, half_width)

        steps = rows // tile
        rowwise = spec((tile, width), lambda i, _: (i, 0))
        pieces_spec = spec((blocks, 2, block, half_width), lambda i, _: (i, 0, 0, 0))
        kv_specs = [whole(qkv_weight.shape), whole(kv_direct.shape), whole(kv_direct.shape)]
        q_specs = [whole(q_direct.shape)] * 2
        out_specs = [whole(out_weight.shape), whole(out_sent.shape), whole(out_sent.shape)]
        rows_bf, rows_f = like((rows, width), BF16), like((rows, width), F32)

        inputs, normed, keys_own, values_own = call(
            functools.partial(enter_kernel, tile, block), "enter", (steps,),
            [pieces_spec, whole((6, width)), whole((2, width)), whole((2, half_width)), whole((2, half_width)), *kv_specs],
            [rowwise] * 4, [rows_f, rows_bf, rows_bf, rows_bf],
        )(info, dealt, thought_rows, jnp.stack([norm_gain[0], norm_shift[0]]), qv_bias, qv_other,
          qkv_weight, kv_direct, kv_partner)
        q_direct, keys_own, values_own, normed = lax.optimization_barrier((q_direct, keys_own, values_own, normed))
        q_partner = flip(q_direct)
        keys_other, values_other = flip(keys_own), flip(values_own)
        grad_mlp = call(
            functools.partial(cotangent_kernel, tile, block), "cotangent", (steps,), [pieces_spec], rowwise, rows_bf
        )(info, cot_pieces)
        queries = call(
            queries_kernel, "queries", (steps,),
            [rowwise, whole((2, half_width)), whole((2, half_width)), whole(qkv_weight.shape), *q_specs], rowwise, rows_bf,
        )(info, normed, qv_bias, qv_other, qkv_weight, q_direct, q_partner)
        queries, grad_mlp, keys_other, values_other, out_direct = lax.optimization_barrier(
            (queries, grad_mlp, keys_other, values_other, out_direct)
        )
        grad_far = cross(grad_mlp)
        out_partner = flip(out_direct)
        heads_out, lse = attend_forward(info, block, queries, keys_own, values_own, keys_other, values_other)
        heads_out, grad_far = lax.optimization_barrier((heads_out, grad_far))
        residual, normed_mlp = call(
            middle_kernel, "middle", (steps,),
            [rowwise, rowwise, whole((3, width)), *out_specs],
            [rowwise] * 2, [rows_f, rows_bf], [pltpu.VMEM((tile, width), F32)],
        )(info, heads_out, inputs, jnp.stack([norm_gain[1], norm_shift[1], out_bias[0]]),
          out_weight, out_direct, out_partner)
        normed_far = cross(normed_mlp)

        full = whole((rows, width))
        chunk = 2 * half_width

        def mlp_rows(normed_rows, grad_rows, dtype):
            by_unit = spec((rows, chunk), lambda i, _: (0, i))
            result = like((rows, width), dtype)
            return call(
                mlp_rows_kernel, "mlp_rows", (2,),
                [full, full, spec((width, chunk), lambda i, _: (0, i)), spec((1, chunk), lambda i, _: (0, i)),
                 spec((chunk, width), lambda i, _: (i, 0))],
                [full, full, spec((chunk, rows), lambda i, _: (i, 0)), by_unit, spec((1, chunk), lambda i, _: (0, i))],
                [result, result, like((hidden_half, rows), BF16), like((rows, hidden_half), BF16),
                 like((1, hidden_half), F32)],
                [pltpu.VMEM((rows, width), F32)] * 2,
            )(info, normed_rows, grad_rows, fc_weight, fc_bias.reshape(1, hidden_half), proj_weight)

        mlp, back, active0, pre0, fcb0 = mlp_rows(normed_mlp, grad_mlp, F32)
        normed_far, mlp = lax.optimization_barrier((normed_far, mlp))
        mlp_sent, back_sent, active1, pre1, fcb1 = mlp_rows(normed_far, grad_far, BF16)
        back_far = cross(back_sent)
        quarter_spec = spec((half_width, 2 * chunk), lambda i, _: (0, i))
        by_unit = spec((rows, chunk), lambda i, _: (0, i))
        unit_rows = spec((chunk, rows), lambda i, _: (i, 0))
        mlp_keep, mlp_send = call(
            mlp_grads_kernel, "mlp_grads", (2,),
            [full] * 4 + [unit_rows] * 2 + [by_unit] * 2, [quarter_spec] * 2,
            [like((half_width, 4 * chunk), BF16)] * 2, [pltpu.VMEM((2, width, rows), BF16)],
        )(info, normed_mlp, normed_far, grad_mlp, grad_far, active0, active1, pre0, pre1)

        back_far, mlp_keep, mlp_send, mlp_sent = lax.optimization_barrier((back_far, mlp_keep, mlp_send, mlp_sent))
        mlp_far = cross(mlp_sent)
        near = (group >> 1) & 1

        def add(terms, index, size):
            total = 0.0
            for array, offset in terms:
                total = total + lax.dynamic_slice_in_dim(array, offset + index * size, size, 0).astype(F32)
            return total.astype(BF16)

        half = half_width // 2
        piece = half // 4
        upper = list(range(2, bits))

        def upper_sends(terms, got):
            shape = (piece, terms[0].shape[1])
            terms = [*terms, *got]
            bases = tuple(term.shape[0] == half_width for term in terms)
            return call(
                functools.partial(split_kernel, piece, bases), "split", (1,),
                [whole(term.shape) for term in terms], [whole(shape)] * 4,
                [like(shape, F32)] + [like(shape, BF16)] * 3,
            )(info, *terms)

        def upper_flip(values):
            return [lax.ppermute(value, AXES, upper_pairs[k + 1]) for k, value in enumerate(values)]

        def upper_reduce_by_bits(terms, got):
            terms = [(term, near * half if term.shape[0] > half else 0) for term in terms]
            terms.append((jnp.concatenate(got, axis=1), 0))
            size = half
            for link in upper:
                size //= 2
                flag = (group >> link) & 1
                new = flip(add(terms, 1 - flag, size), link)
                terms = [(term, offset + flag * size) for term, offset in terms] + [(new, 0)]
            result = add(terms, 0, size)
            for link in reversed(upper):
                result = join((group >> link) & 1, result, flip(result, link))
            return result

        mlp_got = flip(mlp_send)
        grad_residual, grad_attn, grad_heads, small_mlp = call(
            back_kernel, "back", (steps,),
            [rowwise, rowwise, rowwise, rowwise, whole((1, width)), *out_specs],
            [rowwise, rowwise, rowwise, whole((4, width))],
            [rows_f, rows_bf, rows_bf, like((4, width), F32)],
        )(info, back, back_far, residual, grad_mlp, norm_gain[1:], out_weight, out_direct, out_partner)
        pairs = half_width // LANES
        grad_heads, mlp_got = lax.optimization_barrier((grad_heads, mlp_got))
        mlp_sent = [
            add([(term[:, at : at + 2 * chunk], 0) for term in (mlp_keep, mlp_got)], 1 - near, half)
            for at in (0, 2 * chunk)
        ]
        grad_heads, *mlp_sent = lax.optimization_barrier((grad_heads, *mlp_sent))
        mlp_bit = [flip(mlp_sent[0], 1)]

        def backward(first, grad):
            grad_q, grad_ko, grad_vo, grad_kx, grad_vx = attend_backward(
                info, block, first, pairs, queries, keys_own, values_own, keys_other, values_other, grad, heads_out, lse
            )
            return grad_q, grad_ko, grad_vo, grad_kx, grad_vx

        def with_far(grads, *ties):
            grad_q, grad_ko, grad_vo, grad_kx, grad_vx = grads
            far_k, far_v, *ties = lax.optimization_barrier((flip(grad_kx), flip(grad_vx), *ties))
            return (grad_q, grad_ko, far_k, grad_vo, far_v), ties

        other = backward(pairs, grad_heads)
        mlp_far, mlp_bit[0], mlp_sent[1], *other = lax.optimization_barrier((mlp_far, mlp_bit[0], mlp_sent[1], *other))
        mlp_bit.append(flip(mlp_sent[1], 1))
        block_pieces = call(
            functools.partial(block_kernel, tile, block), "block", (steps,),
            [rowwise, rowwise, rowwise, whole((1, width))], pieces_spec,
            like((slots // 2, 2, block, half_width), BF16),
        )(info, residual, mlp, mlp_far, out_bias[1:])
        other, (block_pieces,) = with_far(other, block_pieces)
        block_back = exchange(block_pieces.reshape(slots, block, half_width))

        def attention_grads(column, grads):
            shape = (half_width, 4 * half_width)
            return call(
                attention_grads_kernel, "attention_grads", (1,),
                [full, spec((rows, half_width), lambda i, _: (0, column)), full, *[whole((rows, half_width))] * 5],
                [whole(shape)] * 2, [like(shape, BF16)] * 2, [pltpu.VMEM((width, rows), BF16)],
            )(info, normed, heads_out, grad_attn, *grads)

        keep_other, send_other = attention_grads(1, other)
        got_other = flip(send_other)
        x_first, x_last = (add([(keep_other, 0), (got_other, 0)], place, half) for place in (1 - near, near))
        x_first, x_last, grad_heads = lax.optimization_barrier((x_first, x_last, grad_heads))
        x_first = cross(x_first)
        own = backward(0, grad_heads)
        x_first, x_last, *own = lax.optimization_barrier((x_first, x_last, *own))
        x_last = cross(x_last)
        mlp_terms = [mlp_keep, mlp_got]
        if upper_pairs:
            mlp_bit[0], mlp_bit[1], block_back, *own = lax.optimization_barrier((*mlp_bit, block_back, *own))
            mlp_mine, *mlp_sends = upper_sends(mlp_terms, mlp_bit)
            own, mlp_sends = with_far(own, *mlp_sends)
            mlp_sends = upper_flip(mlp_sends)
        else:
            own, _ = with_far(own)
        keep_own, send_own = attention_grads(0, own)
        got_own = flip(send_own)
        half_rows = spec((tile, half_width), lambda i, _: (i, 0))
        input_pieces, small_attn = call(
            functools.partial(leave_kernel, tile, block), "leave", (steps,),
            [rowwise, rowwise, whole((1, width)), *[half_rows] * 10, *kv_specs, *q_specs],
            [pieces_spec, whole((4, width))],
            [like((slots // 2, 2, block, half_width), BF16), like((4, width), F32)],
            [pltpu.VMEM((tile, width), F32)],
        )(info, inputs, grad_residual, norm_gain[:1], *own, *other, qkv_weight, kv_direct, kv_partner, q_direct, q_partner)
        if upper_pairs:
            input_pieces, small_attn, got_own, x_last, *mlp_sends = lax.optimization_barrier(
                (input_pieces, small_attn, got_own, x_last, *mlp_sends)
            )
        first = [lax.dynamic_slice_in_dim(term, (1 - near) * half, half, 0) for term in (keep_own, got_own)]
        attention_bit = flip(sum(term.astype(F32) for term in (*first, x_first)).astype(BF16), 1)
        input_back = exchange(input_pieces.reshape(slots, block, half_width))

        def ordered(vectors):
            return join(side, vectors[:, :half_width], vectors[:, half_width:], axis=1)

        hidden = 2 * hidden_half
        fcb = join(side, fcb0 + fcb1, jnp.zeros_like(fcb0), axis=1).reshape(hidden // width, width)
        small = jnp.concatenate([small_mlp, small_attn[:2], ordered(small_attn[2:]), fcb], axis=0)
        attention_terms = [keep_own, got_own, x_last]
        if upper_pairs:
            def total_of(mine, received):
                for value in received:
                    mine = mine + value.astype(F32)
                return mine.astype(BF16)

            def stage(value, change):
                return value + change(value)

            mlp_result = total_of(mlp_mine, mlp_sends)
            mlp_stack = upper_flip([mlp_result] * 3)
            small = stage(small, flip)
            attention_bit, *mlp_stack, small = lax.optimization_barrier((attention_bit, *mlp_stack, small))
            mlp_stack = jnp.stack([mlp_result, *mlp_stack])
            mlp_over = flip(mlp_stack, 1)
            mine, *sends = upper_sends(attention_terms, [attention_bit])
            sends = upper_flip(sends)
            small = stage(small, cross)
            *sends, small = lax.optimization_barrier((*sends, small))
            result = total_of(mine, sends)
            stack = upper_flip([result] * 3)
            small = stage(small, functools.partial(flip, bit=1))
            *stack, small = lax.optimization_barrier((*stack, small))
            stack = jnp.stack([result, *stack])
            over = flip(stack, 1)
            near_core = flip(stack)
            mlp_core = flip(mlp_stack)
            for bit in range(2, bits):
                small = stage(small, functools.partial(flip, bit=bit))
            mlp_over, small, near_core, mlp_core = lax.optimization_barrier((mlp_over, small, near_core, mlp_core))
            mlp_all = [mlp_stack, mlp_over, mlp_core, flip(mlp_over)]
            attention_all = [stack, over, near_core, flip(over)]
        else:
            def gather_all(result):
                result = join(near, result, flip(result, 1))[None]
                return [result, flip(result)]

            small = small + flip(small)
            small = small + cross(small)
            for bit in range(1, bits):
                small = small + flip(small, bit)
            mlp_all = gather_all(upper_reduce_by_bits(mlp_terms, mlp_bit))
            attention_all = gather_all(upper_reduce_by_bits(attention_terms, [attention_bit]))
        block_out = gather_slots(restore, block_back, F32)
        input_grad = gather_slots(restore, input_back, F32)
        count = len(mlp_all)
        size = mlp_all[0].shape[:2]
        fc_grad, proj_grad = call(
            functools.partial(finish_mlp_kernel, count), "finish_mlp", (2,),
            [spec((*size, 2 * chunk), lambda i, _: (0, 0, i))] * count,
            [spec((width, chunk), lambda i, _: (0, i)), spec((chunk, width), lambda i, _: (i, 0))],
            [like(fc_weight.shape, F32), like(proj_weight.shape, F32)],
        )(info, *mlp_all)
        qkv_grad, turned = call(
            functools.partial(finish_attention_kernel, count), "finish_attention", (1,),
            [whole((*size, 2 * chunk))] * count, [whole(qkv_weight.shape), whole((width, half_width))],
            [like(qkv_weight.shape, F32), like((width, half_width), F32)],
        )(info, *attention_all)
        out_grad = jnp.concatenate([turned[:half_width], turned[half_width:]], axis=1)

        gain_mlp, shift_mlp, bias_mlp, bias_attn, gain_attn, shift_attn = (small[i] for i in range(6))
        return (
            block_out,
            input_grad,
            qkv_grad,
            part(small[6:8], side, 1),
            out_grad,
            jnp.stack([bias_attn, bias_mlp]),
            fc_grad,
            part(small[8:].reshape(hidden), side),
            proj_grad,
            jnp.stack([gain_attn, gain_mlp]),
            jnp.stack([shift_attn, shift_mlp]),
        )

    return jax.shard_map(
        body,
        mesh=mesh,
        in_specs=(
            P(None, "dp", "tensor"),
            P(None, "dp", "tensor"),
            P("dp", None, "tensor"),
            P("dp", None),
            P(),
            P(),
            P(None, None, "tensor"),
            P(None, "tensor"),
            P("tensor", None),
            P(),
            P(None, "tensor"),
            P("tensor"),
            P("tensor", None),
            P(),
            P(),
        ),
        out_specs=(
            P(None, "dp", "tensor"),
            P(None, "dp", "tensor"),
            P(None, None, "tensor"),
            P(None, "tensor"),
            P("tensor", None),
            P(),
            P(None, "tensor"),
            P("tensor"),
            P("tensor", None),
            P(),
            P(),
        ),
        check_vma=False,
    )
```

```python
import functools

import jax
import jax.numpy as jnp
from jax import lax
from jax.experimental import pallas as pl
from jax.experimental.pallas import tpu as pltpu
from jax.sharding import PartitionSpec as P

HEAD_DIM = 64
LANES = 128
AXES = ("dp", "tensor")
SCALE = HEAD_DIM ** (-0.5)
MASKED = -1e30
BF16 = jnp.bfloat16
F32 = jnp.float32


def dot_nn(left, right):
    return lax.dot_general(left, right, (((1,), (0,)), ((), ())), preferred_element_type=F32)


def dot_nt(left, right):
    return lax.dot_general(left, right, (((1,), (1,)), ((), ())), preferred_element_type=F32)


def dot_tn(left, right):
    return lax.dot_general(left, right, (((0,), (0,)), ((), ())), preferred_element_type=F32)


def own_mask(tile, start, core, length, block):
    key = lax.broadcasted_iota(jnp.int32, (tile, tile), 0)
    query = lax.broadcasted_iota(jnp.int32, (tile, tile), 1)
    key_row = start + key
    key_pos = (2 * (key_row // block) + core) * block + key_row % block
    return (key <= query) & (key_pos < length)


def other_mask(tile, start, core, length, block):
    key = lax.broadcasted_iota(jnp.int32, (tile, tile), 0)
    query = lax.broadcasted_iota(jnp.int32, (tile, tile), 1)
    key_row = start + key
    key_pos = (2 * (key_row // block) + 1 - core) * block + key_row % block
    return (key // block <= query // block - (1 - core)) & (key_pos < length)


def attend_forward_kernel(tile, block, info, q_ref, ko_ref, vo_ref, kx_ref, vx_ref, out_ref, lse_ref):
    core, length = info[0], info[1]
    rows = q_ref.shape[0]
    lane = lax.broadcasted_iota(jnp.int32, (1, LANES), 1)
    vo_t = vo_ref[...].T
    vx_t = vx_ref[...].T
    for start in range(0, rows, tile):
        stop = start + tile
        mask_own = own_mask(tile, start, core, length, block)
        mask_other = other_mask(tile, start, core, length, block)
        query = q_ref[start:stop, :] * jnp.asarray(SCALE, BF16)
        outs = []
        for half in range(2):
            picked = jnp.where(lane // HEAD_DIM == half, query, jnp.zeros_like(query))
            s_own = dot_nt(ko_ref[:stop, :], picked)
            s_other = dot_nt(kx_ref[:stop, :], picked)
            d_own = jnp.where(mask_own, s_own[start:], MASKED)
            d_other = jnp.where(mask_other, s_other[start:], MASKED)
            if start:
                s_own = jnp.concatenate([s_own[:start], d_own], axis=0)
                s_other = jnp.concatenate([s_other[:start], d_other], axis=0)
            else:
                s_own, s_other = d_own, d_other
            top = jnp.maximum(
                jnp.max(s_own, axis=0, keepdims=True), jnp.max(s_other, axis=0, keepdims=True)
            )
            e_own = jnp.exp(s_own - top)
            e_other = jnp.exp(s_other - top)
            total = jnp.sum(e_own, axis=0, keepdims=True) + jnp.sum(e_other, axis=0, keepdims=True)
            lanes = slice(half * HEAD_DIM, (half + 1) * HEAD_DIM)
            mixed = dot_nn(vo_t[lanes, :stop], e_own.astype(BF16)) + dot_nn(
                vx_t[lanes, :stop], e_other.astype(BF16)
            )
            outs.append(mixed / total)
            lse_ref[0, half : half + 1, start:stop] = top + jnp.log(total)
        out_ref[start:stop, :] = jnp.concatenate(outs, axis=0).T.astype(BF16)


def attend_backward_kernel(
    tile, block, info, q_ref, ko_ref, vo_ref, kx_ref, vx_ref, go_ref, out_ref, lse_ref,
    dq_ref, dko_ref, dvo_ref, dkx_ref, dvx_ref, ako, avo, akx, avx,
):
    core, length = info[0], info[1]
    rows = q_ref.shape[0]
    lane = lax.broadcasted_iota(jnp.int32, (1, LANES), 1)
    ko_t = ko_ref[...].T
    kx_t = kx_ref[...].T
    for acc in (ako, avo, akx, avx):
        acc[...] = jnp.zeros_like(acc)
    for start in range(0, rows, tile):
        stop = start + tile
        mask_own = own_mask(tile, start, core, length, block)
        mask_other = other_mask(tile, start, core, length, block)
        query = q_ref[start:stop, :] * jnp.asarray(SCALE, BF16)
        grad = go_ref[start:stop, :]
        product = grad.astype(F32) * out_ref[start:stop, :].astype(F32)
        parts = []
        for half in range(2):
            mine = lane // HEAD_DIM == half
            picked = jnp.where(mine, query, jnp.zeros_like(query))
            grad_half = jnp.where(mine, grad, jnp.zeros_like(grad))
            pick = jnp.broadcast_to(jnp.where(mine, 1.0, 0.0).astype(F32), (8, LANES))
            inner = lax.dot_general(
                pick, product, (((1,), (1,)), ((), ())),
                precision=lax.Precision.HIGHEST, preferred_element_type=F32,
            )[:1]
            lse = lse_ref[0, half : half + 1, start:stop]
            lanes = slice(half * HEAD_DIM, (half + 1) * HEAD_DIM)
            part = jnp.zeros((HEAD_DIM, tile), F32)
            for key_ref, value_ref, key_t, mask, acc_k, acc_v in (
                (ko_ref, vo_ref, ko_t, mask_own, ako, avo),
                (kx_ref, vx_ref, kx_t, mask_other, akx, avx),
            ):
                prob = jnp.exp(dot_nt(key_ref[:stop, :], picked) - lse)
                last = jnp.where(mask, prob[start:], 0.0)
                prob = jnp.concatenate([prob[:start], last], axis=0) if start else last
                grad_prob = dot_nt(value_ref[:stop, :], grad_half)
                grad_score = (prob * (grad_prob - inner)).astype(BF16)
                acc_v[:stop, :] += dot_nn(prob.astype(BF16), grad_half)
                acc_k[:stop, :] += dot_nn(grad_score, picked)
                part = part + dot_nn(key_t[lanes, :stop], grad_score)
            parts.append(part)
        dq_ref[start:stop, :] = (jnp.concatenate(parts, axis=0) * SCALE).T.astype(BF16)
    for acc, ref in ((ako, dko_ref), (avo, dvo_ref), (akx, dkx_ref), (avx, dvx_ref)):
        ref[...] = acc[...].astype(ref.dtype)


def attend_forward(info, block, queries, keys_own, values_own, keys_other, values_other):
    rows, width = queries.shape
    pairs = width // LANES
    tile = min(256, rows)
    column = pl.BlockSpec((rows, LANES), lambda pair, info: (0, pair))
    return pl.pallas_call(
        functools.partial(attend_forward_kernel, tile, block),
        grid_spec=pltpu.PrefetchScalarGridSpec(
            num_scalar_prefetch=1,
            grid=(pairs,),
            in_specs=[column] * 5,
            out_specs=[column, pl.BlockSpec((1, 2, rows), lambda pair, info: (pair, 0, 0))],
        ),
        out_shape=[
            jax.ShapeDtypeStruct((rows, width), BF16),
            jax.ShapeDtypeStruct((pairs, 2, rows), F32),
        ],
        name="attend_forward",
    )(info, queries, keys_own, values_own, keys_other, values_other)


def attend_backward(info, block, first, pairs, queries, keys_own, values_own, keys_other, values_other, grad_heads,
                    heads_out, lse):
    rows = queries.shape[0]
    tile = min(256, rows)
    column = pl.BlockSpec((rows, LANES), lambda pair, info: (0, first + pair))
    result = pl.BlockSpec((rows, LANES), lambda pair, info: (0, pair))
    dtypes = (BF16, F32, F32, BF16, BF16)
    return pl.pallas_call(
        functools.partial(attend_backward_kernel, tile, block),
        grid_spec=pltpu.PrefetchScalarGridSpec(
            num_scalar_prefetch=1,
            grid=(pairs,),
            in_specs=[column] * 7 + [pl.BlockSpec((1, 2, rows), lambda pair, info: (first + pair, 0, 0))],
            out_specs=[result] * 5,
            scratch_shapes=[pltpu.VMEM((rows, LANES), F32)] * 4,
        ),
        out_shape=[jax.ShapeDtypeStruct((rows, pairs * LANES), dtype) for dtype in dtypes],
        name="attend_backward",
    )(info, queries, keys_own, values_own, keys_other, values_other, grad_heads, heads_out, lse)


HALF = 384


def spec(shape, index):
    return pl.BlockSpec(shape, index)


def whole(shape):
    zeros = (0,) * len(shape)
    return pl.BlockSpec(shape, lambda *_: zeros)


def call(kernel, name, grid, in_specs, out_specs, out_shape, scratch=()):
    return pl.pallas_call(
        kernel,
        grid_spec=pltpu.PrefetchScalarGridSpec(
            num_scalar_prefetch=1, grid=grid, in_specs=in_specs, out_specs=out_specs, scratch_shapes=list(scratch)
        ),
        out_shape=out_shape,
        name=name,
    )


def like(shape, dtype):
    return jax.ShapeDtypeStruct(shape, dtype)


def gather_slots(index, array, dtype):
    slots, block, width = array.shape
    steps = 4
    per = slots // steps

    def kernel(index_ref, array_ref, out_ref):
        first = pl.program_id(0) * per

        def copy(i, carry):
            out_ref[i] = array_ref[index_ref[first + i]].astype(dtype)
            return carry

        lax.fori_loop(0, per, copy, 0, unroll=min(per, 4))

    return call(
        kernel, "gather_slots", (steps,), [whole(array.shape)],
        spec((per, block, width), lambda i, _: (i, 0, 0)), like(array.shape, dtype),
    )(index, array)


def statistics(features):
    mean = jnp.mean(features, axis=-1, keepdims=True)
    centred = features - mean
    variance = jnp.mean(centred * centred, axis=-1, keepdims=True)
    scale = lax.rsqrt(variance + 1e-05)
    return centred * scale, scale


def norm_rows_back(grad, gain, xhat, scale):
    scaled = grad * gain
    return scale * (
        scaled
        - jnp.mean(scaled, axis=-1, keepdims=True)
        - xhat * jnp.mean(scaled * xhat, axis=-1, keepdims=True)
    )


def sum_rows(value):
    return jnp.sum(value, axis=0, keepdims=True)


def row_positions(tile, block, core):
    row = pl.program_id(0) * tile + lax.broadcasted_iota(jnp.int32, (tile, 1), 0)
    return (2 * (row // block) + core) * block + row % block


def rows_of(pieces_ref, tile):
    halves = [pieces_ref[:, side].astype(F32).reshape(tile, HALF) for side in range(2)]
    return jnp.concatenate(halves, axis=1)


def cols(index):
    return pl.ds(pl.multiple_of(index * HALF, LANES), HALF)


def rows_at(index):
    return pl.ds(pl.multiple_of(index * HALF, LANES), HALF)


ROOT = 0.7978845608028654
CUBE = 0.044715


def gelu_and_slope(value):
    square = value * value
    turn = jnp.tanh(ROOT * value * (1.0 + CUBE * square))
    slope = 0.5 * (1.0 + turn) + 0.5 * value * (1.0 - turn * turn) * ROOT * (1.0 + 3.0 * CUBE * square)
    return 0.5 * value * (1.0 + turn), slope


def enter_kernel(tile, block, info, pieces, thoughts, norms, bias_own, bias_other, own_k, own_v, direct, partner,
                 inputs_ref, normed_ref, k_ref, v_ref):
    core = info[0]
    position = row_positions(tile, block, core)
    features = rows_of(pieces, tile)
    for index in range(6):
        features = jnp.where(position == info[2 + index], thoughts[index : index + 1, :], features)
    inputs_ref[...] = features
    xhat, _ = statistics(features)
    normed = (xhat * norms[0:1, :] + norms[1:2, :]).astype(BF16)
    normed_ref[...] = normed
    project(core, normed_ref, own_k[0], direct[0], partner[0], None, None, k_ref)
    project(core, normed_ref, own_v[0], direct[1], partner[1], bias_own[1:2, :], bias_other[1:2, :], v_ref)


def project(core, normed, own, direct, partner, bias_own, bias_other, ref):
    mine = dot_nn(normed[...], own)
    theirs = dot_nn(normed[:, cols(core)], direct) + dot_nn(normed[:, cols(1 - core)], partner)
    if bias_own is not None:
        mine = mine + bias_own
        theirs = theirs + bias_other
    ref[:, :HALF] = mine.astype(BF16)
    ref[:, HALF:] = theirs.astype(BF16)


def queries_kernel(info, normed, bias_own, bias_other, own, direct, partner, q_ref):
    project(info[0], normed, own[0], direct[0], partner[0], bias_own[0:1, :], bias_other[0:1, :], q_ref)


def cotangent_kernel(tile, block, info, pieces, grad_ref):
    position = row_positions(tile, block, info[0])
    grad_ref[...] = jnp.where(position < info[1], rows_of(pieces, tile), 0.0).astype(BF16)


def middle_kernel(info, heads, inputs, norms, own, direct, partner, residual_ref, normed_ref, mixed):
    core = info[0]
    mixed[...] = dot_nn(heads[:, :HALF], own[...]) + norms[2:3, :]
    mixed[:, cols(core)] += dot_nn(heads[:, HALF:], direct[...])
    mixed[:, cols(1 - core)] += dot_nn(heads[:, HALF:], partner[...])
    residual = inputs[...] + mixed[...]
    residual_ref[...] = residual
    xhat, _ = statistics(residual)
    normed_ref[...] = (xhat * norms[0:1, :] + norms[1:2, :]).astype(BF16)


def mlp_rows_kernel(info, normed, grad, fc, bias, proj, mlp_ref, back_ref, active_t_ref, pre_ref, fcb_ref, mlp_sum, back_sum):
    step = pl.program_id(1)
    active, slope = gelu_and_slope(dot_nn(normed[...], fc[...]) + bias[...])
    active = active.astype(BF16)
    active_t_ref[...] = active.T
    grad_pre = (dot_nt(grad[...], proj[...]) * slope).astype(BF16)
    pre_ref[...] = grad_pre
    fcb_ref[0] = sum_rows(grad_pre.astype(F32))
    mlp = dot_nn(active, proj[...])
    back = dot_nt(grad_pre, fc[...])

    @pl.when(step == 0)
    def _():
        mlp_sum[...] = mlp
        back_sum[...] = back

    @pl.when((step > 0) & (step < pl.num_programs(1) - 1))
    def _():
        mlp_sum[...] += mlp
        back_sum[...] += back

    @pl.when(step == pl.num_programs(1) - 1)
    def _():
        mlp_ref[...] = (mlp_sum[...] + mlp).astype(mlp_ref.dtype)
        back_ref[...] = (back_sum[...] + back).astype(back_ref.dtype)


def mlp_grads_kernel(info, normed0, normed1, grad0, grad1, active0, active1, pre0, pre1, keep, send, normed_t):
    core = info[0]

    @pl.when(pl.program_id(0) == 0)
    def _():
        normed_t[0] = normed0[...].T
        normed_t[1] = normed1[...].T

    for index, ref in ((core, keep), (1 - core, send)):
        fc = dot_nn(normed_t[0, rows_at(index), :], pre0[...]) + dot_nn(normed_t[1, rows_at(index), :], pre1[...])
        proj = dot_nn(active0[rows_at(index), :], grad0[...]) + dot_nn(active1[rows_at(index), :], grad1[...])
        ref[:, : 2 * HALF] = fc.astype(BF16)
        ref[:, 2 * HALF :] = proj.astype(BF16)


def back_kernel(info, back, back_far, residual, grad, norms, own, direct, partner,
                grad_residual_ref, grad_attn_ref, grad_heads_ref, small_ref):
    core = info[0]
    xhat, scale = statistics(residual[...])
    incoming = back[...] + back_far[...].astype(F32)
    grad_out = grad[...].astype(F32)
    grad_residual = grad_out + norm_rows_back(incoming, norms[0:1, :], xhat, scale)
    grad_residual_ref[...] = grad_residual
    grad_attn = grad_residual.astype(BF16)
    grad_attn_ref[...] = grad_attn
    grad_heads_ref[:, :HALF] = dot_nt(grad_attn, own[...]).astype(BF16)
    theirs = dot_nt(grad_attn_ref[:, cols(core)], direct[...])
    theirs = theirs + dot_nt(grad_attn_ref[:, cols(1 - core)], partner[...])
    grad_heads_ref[:, HALF:] = theirs.astype(BF16)
    sums = jnp.concatenate(
        [sum_rows(incoming * xhat), sum_rows(incoming), sum_rows(grad_out), sum_rows(grad_attn.astype(F32))], axis=0
    )

    @pl.when(pl.program_id(0) == 0)
    def _():
        small_ref[...] = sums

    @pl.when(pl.program_id(0) > 0)
    def _():
        small_ref[...] += sums


def block_kernel(tile, block, info, residual, mlp, mlp_far, bias, block_ref):
    position = row_positions(tile, block, info[0])
    result = residual[...] + (mlp[...] + mlp_far[...].astype(F32) + bias[...])
    result = jnp.where(position < info[1], result, 0.0)
    for side in range(2):
        half = result[:, side * HALF : (side + 1) * HALF].reshape(tile // block, block, HALF)
        block_ref[:, side] = half.astype(BF16)


def key_value_grads(dk, dk_far, dv, dv_far):
    return (
        (dk[...] + dk_far[...].astype(F32)).astype(BF16),
        (dv[...] + dv_far[...].astype(F32)).astype(BF16),
    )


def attention_grads_kernel(info, normed, heads, grad_attn, dq, dk, dk_far, dv, dv_far, keep, send, normed_t):
    core = info[0]
    normed_t[...] = normed[...].T
    grads = (dq[...], *key_value_grads(dk, dk_far, dv, dv_far))
    heads_t = heads[...].T
    for index, ref in ((1 - core, send), (core, keep)):
        left = normed_t[rows_at(index), :]
        for place, grad in enumerate(grads):
            ref[:, place * HALF : (place + 1) * HALF] = dot_nn(left, grad).astype(BF16)
        ref[:, 3 * HALF :] = dot_nn(heads_t, grad_attn[:, cols(index)]).astype(BF16)


def leave_kernel(tile, block, info, inputs, grad_residual, norms, dq0, dk0, dk_far0, dv0, dv_far0,
                 dq1, dk1, dk_far1, dv1, dv_far1, own, direct, partner, direct_q, partner_q, pieces_ref, small_ref, back):
    core = info[0]
    mine = (dq0[...], *key_value_grads(dk0, dk_far0, dv0, dv_far0))
    theirs = (dq1[...], *key_value_grads(dk1, dk_far1, dv1, dv_far1))
    back[...] = sum(dot_nt(grad, own[index]) for index, grad in enumerate(mine))
    far_q, far_k, far_v = theirs
    back[:, cols(core)] += dot_nt(far_q, direct_q[0]) + dot_nt(far_k, direct[0]) + dot_nt(far_v, direct[1])
    back[:, cols(1 - core)] += dot_nt(far_q, partner_q[0]) + dot_nt(far_k, partner[0]) + dot_nt(far_v, partner[1])
    incoming = back[...]
    xhat, scale = statistics(inputs[...])
    result = grad_residual[...] + norm_rows_back(incoming, norms[0:1, :], xhat, scale)
    blocks = tile // block
    for side in range(2):
        pieces_ref[:, side] = result[:, side * HALF : (side + 1) * HALF].reshape(blocks, block, HALF).astype(BF16)
    biases = [
        jnp.concatenate([sum_rows(mine[place].astype(F32)), sum_rows(theirs[place].astype(F32))], axis=1)
        for place in (0, 2)
    ]
    sums = jnp.concatenate([sum_rows(incoming * xhat), sum_rows(incoming), *biases], axis=0)

    @pl.when(pl.program_id(0) == 0)
    def _():
        small_ref[...] = sums

    @pl.when(pl.program_id(0) > 0)
    def _():
        small_ref[...] += sums


def finish_rows(info, refs):
    core, near = info[0], info[8]
    size = refs[0].shape[0]
    for index, ref in enumerate(refs):
        base = (core if index < 2 else 1 - core) * HALF
        yield base, (near if index % 2 == 0 else 1 - near) * size, ref


def finish_mlp_kernel(info, *refs):
    fc_ref, proj_ref = refs[4:]
    for base, offset, ref in finish_rows(info, refs[:4]):
        rows = pl.ds(pl.multiple_of(base + offset, 64), ref.shape[0])
        fc_ref[rows, :] = ref[:, : 2 * HALF].astype(F32)
        proj_ref[rows, :] = ref[:, 2 * HALF :].astype(F32)


def finish_attention_kernel(info, *refs):
    qkv_ref, out_ref = refs[4:]
    for base, offset, ref in finish_rows(info, refs[:4]):
        rows = pl.ds(pl.multiple_of(base + offset, 64), ref.shape[0])
        for place in range(3):
            qkv_ref[place, rows, :] = ref[:, place * HALF : (place + 1) * HALF].astype(F32)
        heads = pl.ds(pl.multiple_of(offset, 64), ref.shape[0])
        out_ref[heads, pl.ds(pl.multiple_of(base, LANES), HALF)] = ref[:, 3 * HALF :].astype(F32)


def solution(mesh):
    groups = mesh.shape["dp"]
    bits = groups.bit_length() - 1
    assert groups == 1 << bits and mesh.shape["tensor"] == 2

    def pairs_of(change):
        table = []
        for group in range(groups):
            for side in range(2):
                to_group, to_side = change(group, side)
                table.append((group * 2 + side, to_group * 2 + to_side))
        return table

    tensor_pairs = pairs_of(lambda group, side: (group, 1 - side))
    bit_pairs = [pairs_of(lambda group, side, k=k: (group ^ (1 << k), side)) for k in range(bits)]
    deal_groups = [
        [group * 2 + side for group in range(core, groups, 2) for side in range(2)] for core in range(2)
    ]

    def body(
        tokens, cotangent, thoughts, latent_pos, lengths, dealing, qkv_weight, qv_bias, out_weight,
        out_bias, fc_weight, fc_bias, proj_weight, norm_gain, norm_shift,
    ):
        group = lax.axis_index("dp")
        side = lax.axis_index("tensor")
        core = group % 2
        slot = group - core + side
        slots, block, half_width = tokens.shape
        width = 2 * half_width
        rows = slots * block // 2
        hidden_half = fc_weight.shape[1]
        assert half_width == HALF and hidden_half == 4 * HALF
        tile = 256
        blocks = tile // block

        def cross(value):
            return lax.ppermute(value, AXES, tensor_pairs)

        def flip(value, bit=0):
            return lax.ppermute(value, AXES, bit_pairs[bit])

        def part(value, index, axis=0):
            size = value.shape[axis] // 2
            return lax.dynamic_slice_in_dim(value, index * size, size, axis)

        def join(flag, mine, theirs, axis=0):
            return jnp.where(
                flag == 0,
                jnp.concatenate([mine, theirs], axis=axis),
                jnp.concatenate([theirs, mine], axis=axis),
            )

        def exchange(array):
            return lax.all_to_all(
                array, AXES, split_axis=0, concat_axis=0, tiled=True, axis_index_groups=deal_groups
            )

        def deal(array):
            return exchange(gather_slots(dealing, array, BF16)).reshape(slots // 2, 2, block, half_width)

        order = jnp.arange(slots, dtype=jnp.int32)
        restore = jnp.sum(jnp.where(dealing[None, :] == order[:, None], order[None, :], 0), axis=1)

        qkv_sent = part(qkv_weight, core, 1)
        thoughts_core = flip(thoughts[0])
        tokens, thoughts_core = lax.optimization_barrier((tokens, thoughts_core))
        dealt = deal(tokens)
        kv_direct = cross(qkv_sent[1:])
        kv_partner = flip(kv_direct)
        biases_other = cross(qv_bias)
        near = jnp.where(core == side, thoughts[0], thoughts_core)
        far = cross(jnp.where(core == side, thoughts_core, thoughts[0]))
        latent_core = flip(latent_pos)
        latent = jnp.where(core == side, latent_pos, latent_core)[0]
        length = lengths[dealing[slot]]
        info = jnp.concatenate(
            [jnp.stack([core, length]).astype(jnp.int32), latent, jnp.stack([(group >> 1) & 1, group >> 2]).astype(jnp.int32)]
        )

        cot_dealt = gather_slots(dealing, cotangent, BF16)
        out_sent = part(out_weight, core, 1)
        thought_rows = join(side, near, far, axis=1).astype(F32)
        norms_in = jnp.stack([norm_gain[0], norm_shift[0]])
        norms_mid = jnp.stack([norm_gain[1], norm_shift[1], out_bias[0]])
        q_sent, out_sent, kv_direct, cot_dealt, thought_rows, biases_other, info, norms_in, norms_mid = (
            lax.optimization_barrier(
                (qkv_sent[:1], out_sent, kv_direct, cot_dealt, thought_rows, biases_other, info, norms_in, norms_mid)
            )
        )
        q_direct = cross(q_sent)
        qv_other = biases_other
        out_direct = cross(out_sent)
        cot_pieces = exchange(cot_dealt).reshape(slots // 2, 2, block, half_width)

        steps = rows // tile
        rowwise = spec((tile, width), lambda i, _: (i, 0))
        pieces_spec = spec((blocks, 2, block, half_width), lambda i, _: (i, 0, 0, 0))
        one, two, three = (spec((1, width, half_width), lambda i, _, place=place: (place, 0, 0)) for place in range(3))
        kv_specs = [whole(kv_direct.shape)] * 2
        q_specs = [whole(q_direct.shape)] * 2
        out_specs = [whole(out_weight.shape), whole(out_sent.shape), whole(out_sent.shape)]
        rows_bf, rows_f = like((rows, width), BF16), like((rows, width), F32)

        inputs, normed, keys_own, values_own = call(
            functools.partial(enter_kernel, tile, block), "enter", (steps,),
            [pieces_spec, whole((6, width)), whole((2, width)), whole((2, half_width)), whole((2, half_width)), two, three, *kv_specs],
            [rowwise] * 4, [rows_f, rows_bf, rows_bf, rows_bf],
        )(info, dealt, thought_rows, norms_in, qv_bias, qv_other,
          qkv_weight, qkv_weight, kv_direct, kv_partner)
        keys_other, values_other = flip(keys_own), flip(values_own)
        grad_mlp = call(
            functools.partial(cotangent_kernel, tile, block), "cotangent", (steps,), [pieces_spec], rowwise, rows_bf
        )(info, cot_pieces)
        q_direct, grad_mlp = lax.optimization_barrier((q_direct, grad_mlp))
        q_partner = flip(q_direct)
        queries = call(
            queries_kernel, "queries", (steps,),
            [rowwise, whole((2, half_width)), whole((2, half_width)), one, *q_specs], rowwise, rows_bf,
        )(info, normed, qv_bias, qv_other, qkv_weight, q_direct, q_partner)
        queries, grad_mlp, keys_other, values_other, out_direct = lax.optimization_barrier(
            (queries, grad_mlp, keys_other, values_other, out_direct)
        )
        grad_far = cross(grad_mlp)
        out_partner = flip(out_direct)
        heads_out, lse = attend_forward(info, block, queries, keys_own, values_own, keys_other, values_other)
        heads_out, grad_far = lax.optimization_barrier((heads_out, grad_far))
        residual, normed_mlp = call(
            middle_kernel, "middle", (steps,),
            [rowwise, rowwise, whole((3, width)), *out_specs],
            [rowwise] * 2, [rows_f, rows_bf], [pltpu.VMEM((tile, width), F32)],
        )(info, heads_out, inputs, norms_mid,
          out_weight, out_direct, out_partner)
        normed_far = cross(normed_mlp)

        full = whole((rows, width))
        chunk = 2 * half_width

        def mlp_rows(normed_rows, grad_rows, dtype):
            units = hidden_half // 3
            by_row = spec((tile, width), lambda r, i, _: (r, 0))
            result = like((rows, width), dtype)
            return call(
                mlp_rows_kernel, "mlp_rows", (steps, 3),
                [by_row, by_row, spec((width, units), lambda r, i, _: (0, i)), spec((1, units), lambda r, i, _: (0, i)),
                 spec((units, width), lambda r, i, _: (i, 0))],
                [by_row, by_row, spec((units, tile), lambda r, i, _: (i, r)), spec((tile, units), lambda r, i, _: (r, i)),
                 spec((1, 1, units), lambda r, i, _: (r, 0, i))],
                [result, result, like((hidden_half, rows), BF16), like((rows, hidden_half), BF16),
                 like((steps, 1, hidden_half), F32)],
                [pltpu.VMEM((tile, width), F32)] * 2,
            )(info, normed_rows, grad_rows, fc_weight, fc_bias.reshape(1, hidden_half), proj_weight)

        mlp, back, active0, pre0, fcb0 = mlp_rows(normed_mlp, grad_mlp, F32)
        normed_far, mlp = lax.optimization_barrier((normed_far, mlp))
        mlp_sent, back_sent, active1, pre1, fcb1 = mlp_rows(normed_far, grad_far, BF16)
        back_far = cross(back_sent)
        quarter_spec = spec((half_width, 2 * chunk), lambda i, _: (0, i))
        by_unit = spec((rows, chunk), lambda i, _: (0, i))
        unit_rows = spec((chunk, rows), lambda i, _: (i, 0))
        mlp_keep, mlp_send = call(
            mlp_grads_kernel, "mlp_grads", (2,),
            [full] * 4 + [unit_rows] * 2 + [by_unit] * 2, [quarter_spec] * 2,
            [like((half_width, 4 * chunk), BF16)] * 2, [pltpu.VMEM((2, width, rows), BF16)],
        )(info, normed_mlp, normed_far, grad_mlp, grad_far, active0, active1, pre0, pre1)

        back_far, mlp_keep, mlp_send, mlp_sent = lax.optimization_barrier((back_far, mlp_keep, mlp_send, mlp_sent))
        mlp_far = cross(mlp_sent)
        near = (group >> 1) & 1
        half = half_width // 2
        upper = list(range(2, bits))
        levels = len(upper)
        flags = [(group >> link) & 1 for link in upper]
        sizes = [half >> (level + 1) for level in range(levels)]
        starts = [sum(flag * size for flag, size in zip(flags[:level], sizes)) for level in range(levels + 1)]

        def rows_sum(terms, start, size):
            total = 0.0
            for array, base in terms:
                total = total + lax.dynamic_slice_in_dim(array, base + start, size, 0).astype(F32)
            return total.astype(BF16)

        def section(level):
            if level == levels:
                return starts[level], sizes[-1]
            return starts[level] + (1 - flags[level]) * sizes[level], sizes[level]

        def widen(level, mine, theirs):
            return join(flags[level], mine, theirs)

        mlp_got = flip(mlp_send)
        grad_residual, grad_attn, grad_heads, small_mlp = call(
            back_kernel, "back", (steps,),
            [rowwise, rowwise, rowwise, rowwise, whole((1, width)), *out_specs],
            [rowwise, rowwise, rowwise, whole((4, width))],
            [rows_f, rows_bf, rows_bf, like((4, width), F32)],
        )(info, back, back_far, residual, grad_mlp, norm_gain[1:], out_weight, out_direct, out_partner)
        pairs = half_width // LANES
        grad_heads, mlp_got = lax.optimization_barrier((grad_heads, mlp_got))
        mlp_rows_kept = [(mlp_keep, near * half), (mlp_got, near * half)]
        mlp_rows_sent = [(mlp_keep, (1 - near) * half), (mlp_got, (1 - near) * half)]
        over_y = [rows_sum(mlp_rows_sent, *section(level)) for level in range(levels + 1)]
        grad_heads, *over_y = lax.optimization_barrier((grad_heads, *over_y))
        over_y[0] = flip(over_y[0], 1)

        def mlp_section(level):
            start, size = section(level)
            return rows_sum([*mlp_rows_kept, (over_y[level], -start)], start, size)

        def backward(first, grad):
            grad_q, grad_ko, grad_vo, grad_kx, grad_vx = attend_backward(
                info, block, first, pairs, queries, keys_own, values_own, keys_other, values_other, grad, heads_out, lse
            )
            return grad_q, grad_ko, grad_vo, grad_kx, grad_vx

        def with_far(grads, *ties):
            grad_q, grad_ko, grad_vo, grad_kx, grad_vx = grads
            far_k, far_v, *ties = lax.optimization_barrier((flip(grad_kx), flip(grad_vx), *ties))
            return (grad_q, grad_ko, far_k, grad_vo, far_v), ties

        other = backward(pairs, grad_heads)
        mlp_far, *tied = lax.optimization_barrier((mlp_far, *over_y, *other))
        over_y, other = tied[: levels + 1], tied[levels + 1 :]
        over_y[1] = flip(over_y[1], 1)
        block_pieces = call(
            functools.partial(block_kernel, tile, block), "block", (steps,),
            [rowwise, rowwise, rowwise, whole((1, width))], pieces_spec,
            like((slots // 2, 2, block, half_width), BF16),
        )(info, residual, mlp, mlp_far, out_bias[1:])
        other, (block_pieces,) = with_far(other, block_pieces)
        block_back = exchange(block_pieces.reshape(slots, block, half_width))

        def attention_grads(column, grads):
            shape = (half_width, 4 * half_width)
            return call(
                attention_grads_kernel, "attention_grads", (1,),
                [full, spec((rows, half_width), lambda i, _: (0, column)), full, *[whole((rows, half_width))] * 5],
                [whole(shape)] * 2, [like(shape, BF16)] * 2, [pltpu.VMEM((width, rows), BF16)],
            )(info, normed, heads_out, grad_attn, *grads)

        keep_other, send_other = attention_grads(1, other)
        keep_other, send_other, *over_y = lax.optimization_barrier((keep_other, send_other, *over_y))
        over_y[2:] = [flip(value, 1) for value in over_y[2:]]
        got_other = flip(send_other)
        mlp_stage = mlp_section(0)
        x_first, x_last = (
            rows_sum([(keep_other, place * half), (got_other, place * half)], 0, half) for place in (1 - near, near)
        )
        x_first, x_last, mlp_stage, grad_heads = lax.optimization_barrier((x_first, x_last, mlp_stage, grad_heads))
        x_first = cross(x_first)
        mlp_stage = flip(mlp_stage, upper[0])
        own = backward(0, grad_heads)
        x_first, x_last, mlp_stage, *tied = lax.optimization_barrier((x_first, x_last, mlp_stage, *over_y[2:], *own))
        over_y[2:], own = tied[: levels - 1], tied[levels - 1 :]
        x_last = cross(x_last)
        mlp_rows_kept.append((mlp_stage, -starts[1]))
        own, (mlp_stage,) = with_far(own, mlp_section(1))
        mlp_stage = flip(mlp_stage, upper[1])
        keep_own, send_own = attention_grads(0, own)
        keep_own, send_own, mlp_stage = lax.optimization_barrier((keep_own, send_own, mlp_stage))
        mlp_rows_kept.append((mlp_stage, -starts[2]))
        for level in range(2, levels):
            mlp_rows_kept.append((flip(mlp_section(level), upper[level]), -starts[level + 1]))
        mlp_piece = mlp_section(levels)
        for level in reversed(range(2, levels)):
            mlp_piece = widen(level, mlp_piece, flip(mlp_piece, upper[level]))
        block_out = gather_slots(restore, block_back, F32)
        mlp_piece, block_out, *own = lax.optimization_barrier((mlp_piece, block_out, *own))
        mlp_stage = flip(mlp_piece, upper[1])
        got_own = flip(send_own)
        half_rows = spec((tile, half_width), lambda i, _: (i, 0))
        input_pieces, small_attn = call(
            functools.partial(leave_kernel, tile, block), "leave", (steps,),
            [rowwise, rowwise, whole((1, width)), *[half_rows] * 10, whole(qkv_weight.shape), *kv_specs, *q_specs],
            [pieces_spec, whole((4, width))],
            [like((slots // 2, 2, block, half_width), BF16), like((4, width), F32)],
            [pltpu.VMEM((tile, width), F32)],
        )(info, inputs, grad_residual, norm_gain[:1], *own, *other, qkv_weight, kv_direct, kv_partner, q_direct, q_partner)
        input_pieces, small_attn, got_own, x_last, mlp_stage = lax.optimization_barrier(
            (input_pieces, small_attn, got_own, x_last, mlp_stage)
        )
        sent = rows_sum([(keep_own, (1 - near) * half), (got_own, (1 - near) * half), (x_first, 0)], 0, half)
        over_bit = flip(sent, 1)
        mlp_piece = widen(1, mlp_piece, mlp_stage)
        mlp_stage = flip(mlp_piece, upper[0])
        input_back = exchange(input_pieces.reshape(slots, block, half_width))

        def ordered(vectors):
            return join(side, vectors[:, :half_width], vectors[:, half_width:], axis=1)

        hidden = 2 * hidden_half
        fcb0 = jnp.sum(fcb0 + fcb1, axis=0)
        fcb = join(side, fcb0, jnp.zeros_like(fcb0), axis=1).reshape(hidden // width, width)
        small = jnp.concatenate([small_mlp, small_attn[:2], ordered(small_attn[2:]), fcb], axis=0)
        links = [flip, cross, *[functools.partial(flip, bit=bit) for bit in range(1, bits)]]

        def add_over(value):
            return value + links.pop(0)(value) if links else value

        small = add_over(small)
        over_bit, mlp_stage, small = lax.optimization_barrier((over_bit, mlp_stage, small))
        mlp_piece = widen(0, mlp_piece, mlp_stage)
        kept = [(keep_own, near * half), (got_own, near * half), (x_last, 0), (over_bit, 0)]
        for level in range(levels):
            stage = flip(rows_sum(kept, *section(level)), upper[level])
            if level == 0:
                mlp_over, mlp_core = flip(mlp_piece, 1), flip(mlp_piece)
            small = add_over(small)
            stage, small, input_back = lax.optimization_barrier((stage, small, input_back))
            kept.append((stage, -starts[level + 1]))
        piece = rows_sum(kept, *section(levels))
        for level in reversed(range(levels)):
            stage = flip(piece, upper[level])
            small = add_over(small)
            stage, small = lax.optimization_barrier((stage, small))
            piece = widen(level, piece, stage)
        while links:
            small = add_over(small)
        over, near_core = flip(piece, 1), flip(piece)
        mlp_over, mlp_core, piece = lax.optimization_barrier((mlp_over, mlp_core, piece))
        mlp_all = [mlp_piece, mlp_over, mlp_core, flip(mlp_over)]
        input_grad = gather_slots(restore, input_back, F32)
        fc_grad, proj_grad = call(
            finish_mlp_kernel, "finish_mlp", (2,), [spec((half, 2 * chunk), lambda i, _: (0, i))] * 4,
            [spec((width, chunk), lambda i, _: (0, i)), spec((chunk, width), lambda i, _: (i, 0))],
            [like(fc_weight.shape, F32), like(proj_weight.shape, F32)],
        )(info, *mlp_all)
        over, fc_grad, proj_grad, input_grad, small = lax.optimization_barrier((over, fc_grad, proj_grad, input_grad, small))
        qkv_grad, out_grad = call(
            finish_attention_kernel, "finish_attention", (1,), [whole((half, 2 * chunk))] * 4,
            [whole(qkv_weight.shape), whole(out_weight.shape)],
            [like(qkv_weight.shape, F32), like(out_weight.shape, F32)],
        )(info, piece, over, near_core, flip(over))

        gain_mlp, shift_mlp, bias_mlp, bias_attn, gain_attn, shift_attn = (small[i] for i in range(6))
        return (
            block_out,
            input_grad,
            qkv_grad,
            part(small[6:8], side, 1),
            out_grad,
            jnp.stack([bias_attn, bias_mlp]),
            fc_grad,
            part(small[8:].reshape(hidden), side),
            proj_grad,
            jnp.stack([gain_attn, gain_mlp]),
            jnp.stack([shift_attn, shift_mlp]),
        )

    return jax.shard_map(
        body,
        mesh=mesh,
        in_specs=(
            P(None, "dp", "tensor"),
            P(None, "dp", "tensor"),
            P("dp", None, "tensor"),
            P("dp", None),
            P(),
            P(),
            P(None, None, "tensor"),
            P(None, "tensor"),
            P("tensor", None),
            P(),
            P(None, "tensor"),
            P("tensor"),
            P("tensor", None),
            P(),
            P(),
        ),
        out_specs=(
            P(None, "dp", "tensor"),
            P(None, "dp", "tensor"),
            P(None, None, "tensor"),
            P(None, "tensor"),
            P("tensor", None),
            P(),
            P(None, "tensor"),
            P("tensor"),
            P("tensor", None),
            P(),
            P(),
        ),
        check_vma=False,
    )
```

```python
import functools

import jax
import jax.numpy as jnp
from jax import lax
from jax.experimental import pallas as pl
from jax.experimental.pallas import tpu as pltpu
from jax.sharding import PartitionSpec as P

HEAD_DIM = 64
LANES = 128
AXES = ("dp", "tensor")
SCALE = HEAD_DIM ** (-0.5)
MASKED = -1e30
BF16 = jnp.bfloat16
F32 = jnp.float32


def dot_nn(left, right):
    return lax.dot_general(left, right, (((1,), (0,)), ((), ())), preferred_element_type=F32)


def dot_nt(left, right):
    return lax.dot_general(left, right, (((1,), (1,)), ((), ())), preferred_element_type=F32)


def dot_tn(left, right):
    return lax.dot_general(left, right, (((0,), (0,)), ((), ())), preferred_element_type=F32)


def own_mask(tile, start, core, length, block):
    key = lax.broadcasted_iota(jnp.int32, (tile, tile), 0)
    query = lax.broadcasted_iota(jnp.int32, (tile, tile), 1)
    key_row = start + key
    key_pos = (2 * (key_row // block) + core) * block + key_row % block
    return (key <= query) & (key_pos < length)


def other_mask(tile, start, core, length, block):
    key = lax.broadcasted_iota(jnp.int32, (tile, tile), 0)
    query = lax.broadcasted_iota(jnp.int32, (tile, tile), 1)
    key_row = start + key
    key_pos = (2 * (key_row // block) + 1 - core) * block + key_row % block
    return (key // block <= query // block - (1 - core)) & (key_pos < length)


def attend_forward_kernel(tile, block, info, q_ref, ko_ref, vo_ref, kx_ref, vx_ref, out_ref, lse_ref):
    core, length = info[0], info[1]
    rows = q_ref.shape[0]
    lane = lax.broadcasted_iota(jnp.int32, (1, LANES), 1)
    vo_t = vo_ref[...].T
    vx_t = vx_ref[...].T
    for start in range(0, rows, tile):
        stop = start + tile
        mask_own = own_mask(tile, start, core, length, block)
        mask_other = other_mask(tile, start, core, length, block)
        query = q_ref[start:stop, :] * jnp.asarray(SCALE, BF16)
        outs = []
        for half in range(2):
            picked = jnp.where(lane // HEAD_DIM == half, query, jnp.zeros_like(query))
            s_own = dot_nt(ko_ref[:stop, :], picked)
            s_other = dot_nt(kx_ref[:stop, :], picked)
            d_own = jnp.where(mask_own, s_own[start:], MASKED)
            d_other = jnp.where(mask_other, s_other[start:], MASKED)
            if start:
                s_own = jnp.concatenate([s_own[:start], d_own], axis=0)
                s_other = jnp.concatenate([s_other[:start], d_other], axis=0)
            else:
                s_own, s_other = d_own, d_other
            top = jnp.maximum(
                jnp.max(s_own, axis=0, keepdims=True), jnp.max(s_other, axis=0, keepdims=True)
            )
            e_own = jnp.exp(s_own - top)
            e_other = jnp.exp(s_other - top)
            total = jnp.sum(e_own, axis=0, keepdims=True) + jnp.sum(e_other, axis=0, keepdims=True)
            lanes = slice(half * HEAD_DIM, (half + 1) * HEAD_DIM)
            mixed = dot_nn(vo_t[lanes, :stop], e_own.astype(BF16)) + dot_nn(
                vx_t[lanes, :stop], e_other.astype(BF16)
            )
            outs.append(mixed / total)
            lse_ref[0, half : half + 1, start:stop] = top + jnp.log(total)
        out_ref[start:stop, :] = jnp.concatenate(outs, axis=0).T.astype(BF16)


def attend_backward_kernel(
    tile, block, info, q_ref, ko_ref, vo_ref, kx_ref, vx_ref, go_ref, out_ref, lse_ref,
    dq_ref, dko_ref, dvo_ref, dkx_ref, dvx_ref, ako, avo, akx, avx,
):
    core, length = info[0], info[1]
    rows = q_ref.shape[0]
    lane = lax.broadcasted_iota(jnp.int32, (1, LANES), 1)
    ko_t = ko_ref[...].T
    kx_t = kx_ref[...].T
    for acc in (ako, avo, akx, avx):
        acc[...] = jnp.zeros_like(acc)
    for start in range(0, rows, tile):
        stop = start + tile
        mask_own = own_mask(tile, start, core, length, block)
        mask_other = other_mask(tile, start, core, length, block)
        query = q_ref[start:stop, :] * jnp.asarray(SCALE, BF16)
        grad = go_ref[start:stop, :]
        product = grad.astype(F32) * out_ref[start:stop, :].astype(F32)
        parts = []
        for half in range(2):
            mine = lane // HEAD_DIM == half
            picked = jnp.where(mine, query, jnp.zeros_like(query))
            grad_half = jnp.where(mine, grad, jnp.zeros_like(grad))
            pick = jnp.broadcast_to(jnp.where(mine, 1.0, 0.0).astype(F32), (8, LANES))
            inner = lax.dot_general(
                pick, product, (((1,), (1,)), ((), ())),
                precision=lax.Precision.HIGHEST, preferred_element_type=F32,
            )[:1]
            lse = lse_ref[0, half : half + 1, start:stop]
            lanes = slice(half * HEAD_DIM, (half + 1) * HEAD_DIM)
            part = jnp.zeros((HEAD_DIM, tile), F32)
            for key_ref, value_ref, key_t, mask, acc_k, acc_v in (
                (ko_ref, vo_ref, ko_t, mask_own, ako, avo),
                (kx_ref, vx_ref, kx_t, mask_other, akx, avx),
            ):
                prob = jnp.exp(dot_nt(key_ref[:stop, :], picked) - lse)
                last = jnp.where(mask, prob[start:], 0.0)
                prob = jnp.concatenate([prob[:start], last], axis=0) if start else last
                grad_prob = dot_nt(value_ref[:stop, :], grad_half)
                grad_score = (prob * (grad_prob - inner)).astype(BF16)
                acc_v[:stop, :] += dot_nn(prob.astype(BF16), grad_half)
                acc_k[:stop, :] += dot_nn(grad_score, picked)
                part = part + dot_nn(key_t[lanes, :stop], grad_score)
            parts.append(part)
        dq_ref[start:stop, :] = (jnp.concatenate(parts, axis=0) * SCALE).T.astype(BF16)
    for acc, ref in ((ako, dko_ref), (avo, dvo_ref), (akx, dkx_ref), (avx, dvx_ref)):
        ref[...] = acc[...].astype(ref.dtype)


def attend_forward(info, block, queries, keys_own, values_own, keys_other, values_other):
    rows, width = queries.shape
    pairs = width // LANES
    tile = min(256, rows)
    column = pl.BlockSpec((rows, LANES), lambda pair, info: (0, pair))
    return pl.pallas_call(
        functools.partial(attend_forward_kernel, tile, block),
        grid_spec=pltpu.PrefetchScalarGridSpec(
            num_scalar_prefetch=1,
            grid=(pairs,),
            in_specs=[column] * 5,
            out_specs=[column, pl.BlockSpec((1, 2, rows), lambda pair, info: (pair, 0, 0))],
        ),
        out_shape=[
            jax.ShapeDtypeStruct((rows, width), BF16),
            jax.ShapeDtypeStruct((pairs, 2, rows), F32),
        ],
        name="attend_forward",
    )(info, queries, keys_own, values_own, keys_other, values_other)


def attend_backward(info, block, first, pairs, queries, keys_own, values_own, keys_other, values_other, grad_heads,
                    heads_out, lse):
    rows = queries.shape[0]
    tile = min(256, rows)
    column = pl.BlockSpec((rows, LANES), lambda pair, info: (0, first + pair))
    result = pl.BlockSpec((rows, LANES), lambda pair, info: (0, pair))
    dtypes = (BF16, F32, F32, BF16, BF16)
    return pl.pallas_call(
        functools.partial(attend_backward_kernel, tile, block),
        grid_spec=pltpu.PrefetchScalarGridSpec(
            num_scalar_prefetch=1,
            grid=(pairs,),
            in_specs=[column] * 7 + [pl.BlockSpec((1, 2, rows), lambda pair, info: (first + pair, 0, 0))],
            out_specs=[result] * 5,
            scratch_shapes=[pltpu.VMEM((rows, LANES), F32)] * 4,
        ),
        out_shape=[jax.ShapeDtypeStruct((rows, pairs * LANES), dtype) for dtype in dtypes],
        name="attend_backward",
    )(info, queries, keys_own, values_own, keys_other, values_other, grad_heads, heads_out, lse)


HALF = 384


def spec(shape, index):
    return pl.BlockSpec(shape, index)


def whole(shape):
    zeros = (0,) * len(shape)
    return pl.BlockSpec(shape, lambda *_: zeros)


def call(kernel, name, grid, in_specs, out_specs, out_shape, scratch=()):
    return pl.pallas_call(
        kernel,
        grid_spec=pltpu.PrefetchScalarGridSpec(
            num_scalar_prefetch=1, grid=grid, in_specs=in_specs, out_specs=out_specs, scratch_shapes=list(scratch)
        ),
        out_shape=out_shape,
        name=name,
    )


def like(shape, dtype):
    return jax.ShapeDtypeStruct(shape, dtype)


def gather_slots(index, array, dtype):
    slots, block, width = array.shape
    steps = 4
    per = slots // steps

    def kernel(index_ref, array_ref, out_ref):
        first = pl.program_id(0) * per

        def copy(i, carry):
            out_ref[i] = array_ref[index_ref[first + i]].astype(dtype)
            return carry

        lax.fori_loop(0, per, copy, 0, unroll=min(per, 4))

    return call(
        kernel, "gather_slots", (steps,), [whole(array.shape)],
        spec((per, block, width), lambda i, _: (i, 0, 0)), like(array.shape, dtype),
    )(index, array)


def statistics(features):
    mean = jnp.mean(features, axis=-1, keepdims=True)
    centred = features - mean
    variance = jnp.mean(centred * centred, axis=-1, keepdims=True)
    scale = lax.rsqrt(variance + 1e-05)
    return centred * scale, scale


def norm_rows_back(grad, gain, xhat, scale):
    scaled = grad * gain
    return scale * (
        scaled
        - jnp.mean(scaled, axis=-1, keepdims=True)
        - xhat * jnp.mean(scaled * xhat, axis=-1, keepdims=True)
    )


def sum_rows(value):
    return jnp.sum(value, axis=0, keepdims=True)


def row_positions(tile, block, core):
    row = pl.program_id(0) * tile + lax.broadcasted_iota(jnp.int32, (tile, 1), 0)
    return (2 * (row // block) + core) * block + row % block


def rows_of(pieces_ref, tile):
    halves = [pieces_ref[:, side].astype(F32).reshape(tile, HALF) for side in range(2)]
    return jnp.concatenate(halves, axis=1)


def cols(index):
    return pl.ds(pl.multiple_of(index * HALF, LANES), HALF)


def rows_at(index):
    return pl.ds(pl.multiple_of(index * HALF, LANES), HALF)


ROOT = 0.7978845608028654
CUBE = 0.044715


def gelu_and_slope(value):
    square = value * value
    turn = jnp.tanh(ROOT * value * (1.0 + CUBE * square))
    slope = 0.5 * (1.0 + turn) + 0.5 * value * (1.0 - turn * turn) * ROOT * (1.0 + 3.0 * CUBE * square)
    return 0.5 * value * (1.0 + turn), slope


def enter_kernel(tile, block, info, pieces, thoughts, norms, bias_own, bias_other, own_k, own_v, direct, partner,
                 inputs_ref, normed_ref, k_ref, v_ref):
    core = info[0]
    position = row_positions(tile, block, core)
    features = rows_of(pieces, tile)
    for index in range(6):
        features = jnp.where(position == info[2 + index], thoughts[index : index + 1, :], features)
    inputs_ref[...] = features
    xhat, _ = statistics(features)
    normed = (xhat * norms[0:1, :] + norms[1:2, :]).astype(BF16)
    normed_ref[...] = normed
    project(core, normed_ref, own_k[0], direct[0], partner[0], None, None, k_ref)
    project(core, normed_ref, own_v[0], direct[1], partner[1], bias_own[1:2, :], bias_other[1:2, :], v_ref)


def project(core, normed, own, direct, partner, bias_own, bias_other, ref):
    mine = dot_nn(normed[...], own)
    theirs = dot_nn(normed[:, cols(core)], direct) + dot_nn(normed[:, cols(1 - core)], partner)
    if bias_own is not None:
        mine = mine + bias_own
        theirs = theirs + bias_other
    ref[:, :HALF] = mine.astype(BF16)
    ref[:, HALF:] = theirs.astype(BF16)


def queries_kernel(info, normed, bias_own, bias_other, own, direct, partner, q_ref):
    project(info[0], normed, own[0], direct[0], partner[0], bias_own[0:1, :], bias_other[0:1, :], q_ref)


def cotangent_kernel(tile, block, info, pieces, grad_ref):
    position = row_positions(tile, block, info[0])
    grad_ref[...] = jnp.where(position < info[1], rows_of(pieces, tile), 0.0).astype(BF16)


def middle_kernel(info, heads, inputs, norms, own, direct, partner, residual_ref, normed_ref, mixed):
    core = info[0]
    mixed[...] = dot_nn(heads[:, :HALF], own[...]) + norms[2:3, :]
    mixed[:, cols(core)] += dot_nn(heads[:, HALF:], direct[...])
    mixed[:, cols(1 - core)] += dot_nn(heads[:, HALF:], partner[...])
    residual = inputs[...] + mixed[...]
    residual_ref[...] = residual
    xhat, _ = statistics(residual)
    normed_ref[...] = (xhat * norms[0:1, :] + norms[1:2, :]).astype(BF16)


def mlp_rows_kernel(info, normed, grad, fc, bias, proj, mlp_ref, back_ref, active_t_ref, pre_ref, fcb_ref, mlp_sum, back_sum):
    step = pl.program_id(1)
    active, slope = gelu_and_slope(dot_nn(normed[...], fc[...]) + bias[...])
    active = active.astype(BF16)
    active_t_ref[...] = active.T
    grad_pre = (dot_nt(grad[...], proj[...]) * slope).astype(BF16)
    pre_ref[...] = grad_pre
    fcb_ref[0] = sum_rows(grad_pre.astype(F32))
    mlp = dot_nn(active, proj[...])
    back = dot_nt(grad_pre, fc[...])

    @pl.when(step == 0)
    def _():
        mlp_sum[...] = mlp
        back_sum[...] = back

    @pl.when((step > 0) & (step < pl.num_programs(1) - 1))
    def _():
        mlp_sum[...] += mlp
        back_sum[...] += back

    @pl.when(step == pl.num_programs(1) - 1)
    def _():
        mlp_ref[...] = (mlp_sum[...] + mlp).astype(mlp_ref.dtype)
        back_ref[...] = (back_sum[...] + back).astype(back_ref.dtype)


def mlp_grads_kernel(info, normed0, normed1, grad0, grad1, active0, active1, pre0, pre1, keep, send, normed_t):
    core = info[0]

    @pl.when(pl.program_id(0) == 0)
    def _():
        normed_t[0] = normed0[...].T
        normed_t[1] = normed1[...].T

    for index, ref in ((core, keep), (1 - core, send)):
        fc = dot_nn(normed_t[0, rows_at(index), :], pre0[...]) + dot_nn(normed_t[1, rows_at(index), :], pre1[...])
        proj = dot_nn(active0[rows_at(index), :], grad0[...]) + dot_nn(active1[rows_at(index), :], grad1[...])
        ref[:, : 2 * HALF] = fc.astype(BF16)
        ref[:, 2 * HALF :] = proj.astype(BF16)


def back_kernel(info, back, back_far, residual, grad, norms, own, direct, partner,
                grad_residual_ref, grad_attn_ref, grad_heads_ref, small_ref):
    core = info[0]
    xhat, scale = statistics(residual[...])
    incoming = back[...] + back_far[...].astype(F32)
    grad_out = grad[...].astype(F32)
    grad_residual = grad_out + norm_rows_back(incoming, norms[0:1, :], xhat, scale)
    grad_residual_ref[...] = grad_residual
    grad_attn = grad_residual.astype(BF16)
    grad_attn_ref[...] = grad_attn
    grad_heads_ref[:, :HALF] = dot_nt(grad_attn, own[...]).astype(BF16)
    theirs = dot_nt(grad_attn_ref[:, cols(core)], direct[...])
    theirs = theirs + dot_nt(grad_attn_ref[:, cols(1 - core)], partner[...])
    grad_heads_ref[:, HALF:] = theirs.astype(BF16)
    sums = jnp.concatenate(
        [sum_rows(incoming * xhat), sum_rows(incoming), sum_rows(grad_out), sum_rows(grad_attn.astype(F32))], axis=0
    )

    @pl.when(pl.program_id(0) == 0)
    def _():
        small_ref[...] = sums

    @pl.when(pl.program_id(0) > 0)
    def _():
        small_ref[...] += sums


def block_kernel(tile, block, info, residual, mlp, mlp_far, bias, block_ref):
    position = row_positions(tile, block, info[0])
    result = residual[...] + (mlp[...] + mlp_far[...].astype(F32) + bias[...])
    result = jnp.where(position < info[1], result, 0.0)
    for side in range(2):
        half = result[:, side * HALF : (side + 1) * HALF].reshape(tile // block, block, HALF)
        block_ref[:, side] = half.astype(BF16)


def key_value_grads(dk, dk_far, dv, dv_far):
    return (
        (dk[...] + dk_far[...].astype(F32)).astype(BF16),
        (dv[...] + dv_far[...].astype(F32)).astype(BF16),
    )


def attention_grads_kernel(info, normed, heads, grad_attn, dq, dk, dk_far, dv, dv_far, keep, send, normed_t):
    core = info[0]
    normed_t[...] = normed[...].T
    grads = (dq[...], *key_value_grads(dk, dk_far, dv, dv_far))
    heads_t = heads[...].T
    for index, ref in ((1 - core, send), (core, keep)):
        left = normed_t[rows_at(index), :]
        for place, grad in enumerate(grads):
            ref[:, place * HALF : (place + 1) * HALF] = dot_nn(left, grad).astype(BF16)
        ref[:, 3 * HALF :] = dot_nn(heads_t, grad_attn[:, cols(index)]).astype(BF16)


def leave_kernel(tile, block, info, inputs, grad_residual, norms, dq0, dk0, dk_far0, dv0, dv_far0,
                 dq1, dk1, dk_far1, dv1, dv_far1, own, direct, partner, direct_q, partner_q, pieces_ref, small_ref, back):
    core = info[0]
    mine = (dq0[...], *key_value_grads(dk0, dk_far0, dv0, dv_far0))
    theirs = (dq1[...], *key_value_grads(dk1, dk_far1, dv1, dv_far1))
    back[...] = sum(dot_nt(grad, own[index]) for index, grad in enumerate(mine))
    far_q, far_k, far_v = theirs
    back[:, cols(core)] += dot_nt(far_q, direct_q[0]) + dot_nt(far_k, direct[0]) + dot_nt(far_v, direct[1])
    back[:, cols(1 - core)] += dot_nt(far_q, partner_q[0]) + dot_nt(far_k, partner[0]) + dot_nt(far_v, partner[1])
    incoming = back[...]
    xhat, scale = statistics(inputs[...])
    result = grad_residual[...] + norm_rows_back(incoming, norms[0:1, :], xhat, scale)
    blocks = tile // block
    for side in range(2):
        pieces_ref[:, side] = result[:, side * HALF : (side + 1) * HALF].reshape(blocks, block, HALF).astype(BF16)
    biases = [
        jnp.concatenate([sum_rows(mine[place].astype(F32)), sum_rows(theirs[place].astype(F32))], axis=1)
        for place in (0, 2)
    ]
    sums = jnp.concatenate([sum_rows(incoming * xhat), sum_rows(incoming), *biases], axis=0)

    @pl.when(pl.program_id(0) == 0)
    def _():
        small_ref[...] = sums

    @pl.when(pl.program_id(0) > 0)
    def _():
        small_ref[...] += sums


def finish_rows(info, refs):
    core, near = info[0], info[8]
    size = refs[0].shape[0]
    for index, ref in enumerate(refs):
        base = (core if index < 2 else 1 - core) * HALF
        yield base, (near if index % 2 == 0 else 1 - near) * size, ref


def finish_mlp_kernel(info, *refs):
    fc_ref, proj_ref = refs[4:]
    for base, offset, ref in finish_rows(info, refs[:4]):
        rows = pl.ds(pl.multiple_of(base + offset, 64), ref.shape[0])
        fc_ref[rows, :] = ref[:, : 2 * HALF].astype(F32)
        proj_ref[rows, :] = ref[:, 2 * HALF :].astype(F32)


def finish_attention_kernel(info, *refs):
    qkv_ref, out_ref = refs[4:]
    for base, offset, ref in finish_rows(info, refs[:4]):
        rows = pl.ds(pl.multiple_of(base + offset, 64), ref.shape[0])
        for place in range(3):
            qkv_ref[place, rows, :] = ref[:, place * HALF : (place + 1) * HALF].astype(F32)
        heads = pl.ds(pl.multiple_of(offset, 64), ref.shape[0])
        out_ref[heads, pl.ds(pl.multiple_of(base, LANES), HALF)] = ref[:, 3 * HALF :].astype(F32)


def solution(mesh):
    groups = mesh.shape["dp"]
    bits = groups.bit_length() - 1
    assert groups == 1 << bits and mesh.shape["tensor"] == 2

    def pairs_of(change):
        table = []
        for group in range(groups):
            for side in range(2):
                to_group, to_side = change(group, side)
                table.append((group * 2 + side, to_group * 2 + to_side))
        return table

    tensor_pairs = pairs_of(lambda group, side: (group, 1 - side))
    bit_pairs = [pairs_of(lambda group, side, k=k: (group ^ (1 << k), side)) for k in range(bits)]
    deal_groups = [
        [group * 2 + side for group in range(core, groups, 2) for side in range(2)] for core in range(2)
    ]

    def body(
        tokens, cotangent, thoughts, latent_pos, lengths, dealing, qkv_weight, qv_bias, out_weight,
        out_bias, fc_weight, fc_bias, proj_weight, norm_gain, norm_shift,
    ):
        group = lax.axis_index("dp")
        side = lax.axis_index("tensor")
        core = group % 2
        slot = group - core + side
        slots, block, half_width = tokens.shape
        width = 2 * half_width
        rows = slots * block // 2
        hidden_half = fc_weight.shape[1]
        assert half_width == HALF and hidden_half == 4 * HALF
        tile = 256
        blocks = tile // block

        def cross(value):
            return lax.ppermute(value, AXES, tensor_pairs)

        def flip(value, bit=0):
            return lax.ppermute(value, AXES, bit_pairs[bit])

        def part(value, index, axis=0):
            size = value.shape[axis] // 2
            return lax.dynamic_slice_in_dim(value, index * size, size, axis)

        def join(flag, mine, theirs, axis=0):
            return jnp.where(
                flag == 0,
                jnp.concatenate([mine, theirs], axis=axis),
                jnp.concatenate([theirs, mine], axis=axis),
            )

        def exchange(array):
            return lax.all_to_all(
                array, AXES, split_axis=0, concat_axis=0, tiled=True, axis_index_groups=deal_groups
            )

        def deal(array):
            return exchange(gather_slots(dealing, array, BF16)).reshape(slots // 2, 2, block, half_width)

        order = jnp.arange(slots, dtype=jnp.int32)
        restore = jnp.sum(jnp.where(dealing[None, :] == order[:, None], order[None, :], 0), axis=1)

        qkv_sent = part(qkv_weight, core, 1)
        thoughts_core = flip(thoughts[0])
        tokens, thoughts_core = lax.optimization_barrier((tokens, thoughts_core))
        dealt = deal(tokens)
        kv_direct = cross(qkv_sent[1:])
        kv_partner = flip(kv_direct)
        biases_other = cross(qv_bias)
        near = jnp.where(core == side, thoughts[0], thoughts_core)
        far = cross(jnp.where(core == side, thoughts_core, thoughts[0]))
        latent_core = flip(latent_pos)
        latent = jnp.where(core == side, latent_pos, latent_core)[0]
        length = lengths[dealing[slot]]
        info = jnp.concatenate(
            [jnp.stack([core, length]).astype(jnp.int32), latent, jnp.stack([(group >> 1) & 1, group >> 2]).astype(jnp.int32)]
        )

        cot_dealt = gather_slots(dealing, cotangent, BF16)
        out_sent = part(out_weight, core, 1)
        thought_rows = join(side, near, far, axis=1).astype(F32)
        norms_in = jnp.stack([norm_gain[0], norm_shift[0]])
        norms_mid = jnp.stack([norm_gain[1], norm_shift[1], out_bias[0]])
        q_sent, out_sent, kv_direct, cot_dealt, thought_rows, biases_other, info, norms_in, norms_mid = (
            lax.optimization_barrier(
                (qkv_sent[:1], out_sent, kv_direct, cot_dealt, thought_rows, biases_other, info, norms_in, norms_mid)
            )
        )
        q_direct = cross(q_sent)
        qv_other = biases_other
        out_direct = cross(out_sent)
        cot_pieces = exchange(cot_dealt).reshape(slots // 2, 2, block, half_width)

        steps = rows // tile
        rowwise = spec((tile, width), lambda i, _: (i, 0))
        pieces_spec = spec((blocks, 2, block, half_width), lambda i, _: (i, 0, 0, 0))
        one, two, three = (spec((1, width, half_width), lambda i, _, place=place: (place, 0, 0)) for place in range(3))
        kv_specs = [whole(kv_direct.shape)] * 2
        q_specs = [whole(q_direct.shape)] * 2
        out_specs = [whole(out_weight.shape), whole(out_sent.shape), whole(out_sent.shape)]
        rows_bf, rows_f = like((rows, width), BF16), like((rows, width), F32)

        inputs, normed, keys_own, values_own = call(
            functools.partial(enter_kernel, tile, block), "enter", (steps,),
            [pieces_spec, whole((6, width)), whole((2, width)), whole((2, half_width)), whole((2, half_width)), two, three, *kv_specs],
            [rowwise] * 4, [rows_f, rows_bf, rows_bf, rows_bf],
        )(info, dealt, thought_rows, norms_in, qv_bias, qv_other,
          qkv_weight, qkv_weight, kv_direct, kv_partner)
        q_direct, keys_own, values_own, normed = lax.optimization_barrier((q_direct, keys_own, values_own, normed))
        q_partner = flip(q_direct)
        keys_other, values_other = flip(keys_own), flip(values_own)
        queries = call(
            queries_kernel, "queries", (steps,),
            [rowwise, whole((2, half_width)), whole((2, half_width)), one, *q_specs], rowwise, rows_bf,
        )(info, normed, qv_bias, qv_other, qkv_weight, q_direct, q_partner)
        queries, out_direct, cot_pieces = lax.optimization_barrier((queries, out_direct, cot_pieces))
        grad_mlp = call(
            functools.partial(cotangent_kernel, tile, block), "cotangent", (steps,), [pieces_spec], rowwise, rows_bf
        )(info, cot_pieces)
        queries, grad_mlp, keys_other, values_other = lax.optimization_barrier(
            (queries, grad_mlp, keys_other, values_other)
        )
        grad_far = cross(grad_mlp)
        out_partner = flip(out_direct)
        heads_out, lse = attend_forward(info, block, queries, keys_own, values_own, keys_other, values_other)
        heads_out, grad_far = lax.optimization_barrier((heads_out, grad_far))
        residual, normed_mlp = call(
            middle_kernel, "middle", (steps,),
            [rowwise, rowwise, whole((3, width)), *out_specs],
            [rowwise] * 2, [rows_f, rows_bf], [pltpu.VMEM((tile, width), F32)],
        )(info, heads_out, inputs, norms_mid,
          out_weight, out_direct, out_partner)
        normed_far = cross(normed_mlp)

        full = whole((rows, width))
        chunk = 2 * half_width

        def mlp_rows(normed_rows, grad_rows, dtype):
            units = hidden_half // 3
            by_row = spec((tile, width), lambda r, i, _: (r, 0))
            result = like((rows, width), dtype)
            return call(
                mlp_rows_kernel, "mlp_rows", (steps, 3),
                [by_row, by_row, spec((width, units), lambda r, i, _: (0, i)), spec((1, units), lambda r, i, _: (0, i)),
                 spec((units, width), lambda r, i, _: (i, 0))],
                [by_row, by_row, spec((units, tile), lambda r, i, _: (i, r)), spec((tile, units), lambda r, i, _: (r, i)),
                 spec((1, 1, units), lambda r, i, _: (r, 0, i))],
                [result, result, like((hidden_half, rows), BF16), like((rows, hidden_half), BF16),
                 like((steps, 1, hidden_half), F32)],
                [pltpu.VMEM((tile, width), F32)] * 2,
            )(info, normed_rows, grad_rows, fc_weight, fc_bias.reshape(1, hidden_half), proj_weight)

        mlp, back, active0, pre0, fcb0 = mlp_rows(normed_mlp, grad_mlp, F32)
        normed_far, mlp = lax.optimization_barrier((normed_far, mlp))
        mlp_sent, back_sent, active1, pre1, fcb1 = mlp_rows(normed_far, grad_far, BF16)
        back_far = cross(back_sent)
        quarter_spec = spec((half_width, 2 * chunk), lambda i, _: (0, i))
        by_unit = spec((rows, chunk), lambda i, _: (0, i))
        unit_rows = spec((chunk, rows), lambda i, _: (i, 0))
        mlp_keep, mlp_send = call(
            mlp_grads_kernel, "mlp_grads", (2,),
            [full] * 4 + [unit_rows] * 2 + [by_unit] * 2, [quarter_spec] * 2,
            [like((half_width, 4 * chunk), BF16)] * 2, [pltpu.VMEM((2, width, rows), BF16)],
        )(info, normed_mlp, normed_far, grad_mlp, grad_far, active0, active1, pre0, pre1)

        back_far, mlp_keep, mlp_send, mlp_sent = lax.optimization_barrier((back_far, mlp_keep, mlp_send, mlp_sent))
        mlp_far = cross(mlp_sent)
        near = (group >> 1) & 1
        half = half_width // 2
        upper = list(range(2, bits))
        levels = len(upper)
        flags = [(group >> link) & 1 for link in upper]
        sizes = [half >> (level + 1) for level in range(levels)]
        starts = [sum(flag * size for flag, size in zip(flags[:level], sizes)) for level in range(levels + 1)]

        def rows_sum(terms, start, size):
            total = 0.0
            for array, base in terms:
                total = total + lax.dynamic_slice_in_dim(array, base + start, size, 0).astype(F32)
            return total.astype(BF16)

        def section(level):
            if level == levels:
                return starts[level], sizes[-1]
            return starts[level] + (1 - flags[level]) * sizes[level], sizes[level]

        def widen(level, mine, theirs):
            return join(flags[level], mine, theirs)

        mlp_got = flip(mlp_send)
        grad_residual, grad_attn, grad_heads, small_mlp = call(
            back_kernel, "back", (steps,),
            [rowwise, rowwise, rowwise, rowwise, whole((1, width)), *out_specs],
            [rowwise, rowwise, rowwise, whole((4, width))],
            [rows_f, rows_bf, rows_bf, like((4, width), F32)],
        )(info, back, back_far, residual, grad_mlp, norm_gain[1:], out_weight, out_direct, out_partner)
        pairs = half_width // LANES
        grad_heads, mlp_got = lax.optimization_barrier((grad_heads, mlp_got))
        mlp_rows_kept = [(mlp_keep, near * half), (mlp_got, near * half)]
        mlp_rows_sent = [(mlp_keep, (1 - near) * half), (mlp_got, (1 - near) * half)]
        over_y = [rows_sum(mlp_rows_sent, *section(level)) for level in range(levels + 1)]
        grad_heads, *over_y = lax.optimization_barrier((grad_heads, *over_y))
        over_y[0] = flip(over_y[0], 1)

        def mlp_section(level):
            start, size = section(level)
            return rows_sum([*mlp_rows_kept, (over_y[level], -start)], start, size)

        def backward(first, grad):
            grad_q, grad_ko, grad_vo, grad_kx, grad_vx = attend_backward(
                info, block, first, pairs, queries, keys_own, values_own, keys_other, values_other, grad, heads_out, lse
            )
            return grad_q, grad_ko, grad_vo, grad_kx, grad_vx

        def with_far(grads, *ties):
            grad_q, grad_ko, grad_vo, grad_kx, grad_vx = grads
            far_k, far_v, *ties = lax.optimization_barrier((flip(grad_kx), flip(grad_vx), *ties))
            return (grad_q, grad_ko, far_k, grad_vo, far_v), ties

        other = backward(pairs, grad_heads)
        mlp_far, *tied = lax.optimization_barrier((mlp_far, *over_y, *other))
        over_y, other = tied[: levels + 1], tied[levels + 1 :]
        over_y[1] = flip(over_y[1], 1)
        block_pieces = call(
            functools.partial(block_kernel, tile, block), "block", (steps,),
            [rowwise, rowwise, rowwise, whole((1, width))], pieces_spec,
            like((slots // 2, 2, block, half_width), BF16),
        )(info, residual, mlp, mlp_far, out_bias[1:])
        other, (block_pieces,) = with_far(other, block_pieces)
        block_back = exchange(block_pieces.reshape(slots, block, half_width))

        def attention_grads(column, grads):
            shape = (half_width, 4 * half_width)
            return call(
                attention_grads_kernel, "attention_grads", (1,),
                [full, spec((rows, half_width), lambda i, _: (0, column)), full, *[whole((rows, half_width))] * 5],
                [whole(shape)] * 2, [like(shape, BF16)] * 2, [pltpu.VMEM((width, rows), BF16)],
            )(info, normed, heads_out, grad_attn, *grads)

        keep_other, send_other = attention_grads(1, other)
        keep_other, send_other, *over_y = lax.optimization_barrier((keep_other, send_other, *over_y))
        over_y[2:] = [flip(value, 1) for value in over_y[2:]]
        got_other = flip(send_other)
        mlp_stage = mlp_section(0)
        x_first, x_last = (
            rows_sum([(keep_other, place * half), (got_other, place * half)], 0, half) for place in (1 - near, near)
        )
        x_first, x_last, mlp_stage, grad_heads = lax.optimization_barrier((x_first, x_last, mlp_stage, grad_heads))
        x_first = cross(x_first)
        mlp_stage = flip(mlp_stage, upper[0])
        own = backward(0, grad_heads)
        x_first, x_last, mlp_stage, block_back, *tied = lax.optimization_barrier(
            (x_first, x_last, mlp_stage, block_back, *over_y[2:], *own)
        )
        over_y[2:], own = tied[: levels - 1], tied[levels - 1 :]
        x_last = cross(x_last)
        mlp_rows_kept.append((mlp_stage, -starts[1]))
        own, (mlp_stage,) = with_far(own, mlp_section(1))
        mlp_stage = flip(mlp_stage, upper[1])
        keep_own, send_own = attention_grads(0, own)
        block_out = gather_slots(restore, block_back, F32)
        got_own, mlp_stage, block_out = lax.optimization_barrier((flip(send_own), mlp_stage, block_out))
        mlp_rows_kept.append((mlp_stage, -starts[2]))
        for level in range(2, levels):
            mlp_rows_kept.append((flip(mlp_section(level), upper[level]), -starts[level + 1]))
        mlp_piece = mlp_section(levels)
        for level in reversed(range(2, levels)):
            mlp_piece = widen(level, mlp_piece, flip(mlp_piece, upper[level]))
        sent = rows_sum([(keep_own, (1 - near) * half), (got_own, (1 - near) * half), (x_first, 0)], 0, half)
        sent, mlp_piece, *own = lax.optimization_barrier((sent, mlp_piece, *own))
        over_bit = flip(sent, 1)
        mlp_stage = flip(mlp_piece, upper[1])
        half_rows = spec((tile, half_width), lambda i, _: (i, 0))
        input_pieces, small_attn = call(
            functools.partial(leave_kernel, tile, block), "leave", (steps,),
            [rowwise, rowwise, whole((1, width)), *[half_rows] * 10, whole(qkv_weight.shape), *kv_specs, *q_specs],
            [pieces_spec, whole((4, width))],
            [like((slots // 2, 2, block, half_width), BF16), like((4, width), F32)],
            [pltpu.VMEM((tile, width), F32)],
        )(info, inputs, grad_residual, norm_gain[:1], *own, *other, qkv_weight, kv_direct, kv_partner, q_direct, q_partner)
        input_pieces, small_attn, over_bit, mlp_stage, x_last = lax.optimization_barrier(
            (input_pieces, small_attn, over_bit, mlp_stage, x_last)
        )

        def ordered(vectors):
            return join(side, vectors[:, :half_width], vectors[:, half_width:], axis=1)

        hidden = 2 * hidden_half
        fcb0 = jnp.sum(fcb0 + fcb1, axis=0)
        fcb = join(side, fcb0, jnp.zeros_like(fcb0), axis=1).reshape(hidden // width, width)
        small = jnp.concatenate([small_mlp, small_attn[:2], ordered(small_attn[2:]), fcb], axis=0)
        links = [functools.partial(flip, bit=1), flip, cross, *[functools.partial(flip, bit=bit) for bit in upper]]

        def add_over(value):
            return value + links.pop(0)(value) if links else value

        kept = [(keep_own, near * half), (got_own, near * half), (x_last, 0), (over_bit, 0)]
        for level in range(levels):
            stage = flip(rows_sum(kept, *section(level)), upper[level])
            if level == 0:
                mlp_piece = widen(1, mlp_piece, mlp_stage)
                mlp_stage = flip(mlp_piece, upper[0])
            small = add_over(small)
            stage, small = lax.optimization_barrier((stage, small))
            if level == 1:
                stage, mlp_stage, input_pieces = lax.optimization_barrier((stage, mlp_stage, input_pieces))
                mlp_piece = widen(0, mlp_piece, mlp_stage)
                mlp_over, mlp_core = flip(mlp_piece, 1), flip(mlp_piece)
                input_back = exchange(input_pieces.reshape(slots, block, half_width))
            kept.append((stage, -starts[level + 1]))
        piece = rows_sum(kept, *section(levels))
        for level in reversed(range(levels)):
            stage = flip(piece, upper[level])
            small = add_over(small)
            stage, small = lax.optimization_barrier((stage, small))
            if level == levels - 1:
                stage, mlp_core = lax.optimization_barrier((stage, mlp_core))
            if level == 0:
                stage, mlp_over, input_back = lax.optimization_barrier((stage, mlp_over, input_back))
            piece = widen(level, piece, stage)
        while links:
            small = add_over(small)
        over, near_core = flip(piece, 1), flip(piece)
        mlp_over, mlp_core, piece = lax.optimization_barrier((mlp_over, mlp_core, piece))
        mlp_all = [mlp_piece, mlp_over, mlp_core, flip(mlp_over)]
        input_grad = gather_slots(restore, input_back, F32)
        fc_grad, proj_grad = call(
            finish_mlp_kernel, "finish_mlp", (2,), [spec((half, 2 * chunk), lambda i, _: (0, i))] * 4,
            [spec((width, chunk), lambda i, _: (0, i)), spec((chunk, width), lambda i, _: (i, 0))],
            [like(fc_weight.shape, F32), like(proj_weight.shape, F32)],
        )(info, *mlp_all)
        over, fc_grad, proj_grad, input_grad, small = lax.optimization_barrier((over, fc_grad, proj_grad, input_grad, small))
        qkv_grad, out_grad = call(
            finish_attention_kernel, "finish_attention", (1,), [whole((half, 2 * chunk))] * 4,
            [whole(qkv_weight.shape), whole(out_weight.shape)],
            [like(qkv_weight.shape, F32), like(out_weight.shape, F32)],
        )(info, piece, over, near_core, flip(over))

        gain_mlp, shift_mlp, bias_mlp, bias_attn, gain_attn, shift_attn = (small[i] for i in range(6))
        return (
            block_out,
            input_grad,
            qkv_grad,
            part(small[6:8], side, 1),
            out_grad,
            jnp.stack([bias_attn, bias_mlp]),
            fc_grad,
            part(small[8:].reshape(hidden), side),
            proj_grad,
            jnp.stack([gain_attn, gain_mlp]),
            jnp.stack([shift_attn, shift_mlp]),
        )

    return jax.shard_map(
        body,
        mesh=mesh,
        in_specs=(
            P(None, "dp", "tensor"),
            P(None, "dp", "tensor"),
            P("dp", None, "tensor"),
            P("dp", None),
            P(),
            P(),
            P(None, None, "tensor"),
            P(None, "tensor"),
            P("tensor", None),
            P(),
            P(None, "tensor"),
            P("tensor"),
            P("tensor", None),
            P(),
            P(),
        ),
        out_specs=(
            P(None, "dp", "tensor"),
            P(None, "dp", "tensor"),
            P(None, None, "tensor"),
            P(None, "tensor"),
            P("tensor", None),
            P(),
            P(None, "tensor"),
            P("tensor"),
            P("tensor", None),
            P(),
            P(),
        ),
        check_vma=False,
    )
```

```python
import functools

import jax
import jax.numpy as jnp
from jax import lax
from jax.experimental import pallas as pl
from jax.experimental.pallas import tpu as pltpu
from jax.sharding import PartitionSpec as P

HEAD_DIM = 64
LANES = 128
AXES = ("dp", "tensor")
SCALE = HEAD_DIM ** (-0.5)
MASKED = -1e30
BF16 = jnp.bfloat16
F32 = jnp.float32


def dot_nn(left, right):
    return lax.dot_general(left, right, (((1,), (0,)), ((), ())), preferred_element_type=F32)


def dot_nt(left, right):
    return lax.dot_general(left, right, (((1,), (1,)), ((), ())), preferred_element_type=F32)


def dot_tn(left, right):
    return lax.dot_general(left, right, (((0,), (0,)), ((), ())), preferred_element_type=F32)


def own_mask(tile, start, core, length, block):
    key = lax.broadcasted_iota(jnp.int32, (tile, tile), 0)
    query = lax.broadcasted_iota(jnp.int32, (tile, tile), 1)
    key_row = start + key
    key_pos = (2 * (key_row // block) + core) * block + key_row % block
    return (key <= query) & (key_pos < length)


def other_mask(tile, start, core, length, block):
    key = lax.broadcasted_iota(jnp.int32, (tile, tile), 0)
    query = lax.broadcasted_iota(jnp.int32, (tile, tile), 1)
    key_row = start + key
    key_pos = (2 * (key_row // block) + 1 - core) * block + key_row % block
    return (key // block <= query // block - (1 - core)) & (key_pos < length)


def attend_forward_kernel(tile, block, info, q_ref, ko_ref, vo_ref, kx_ref, vx_ref, out_ref, lse_ref):
    core, length = info[0], info[1]
    rows = q_ref.shape[0]
    lane = lax.broadcasted_iota(jnp.int32, (1, LANES), 1)
    vo_t = vo_ref[...].T
    vx_t = vx_ref[...].T
    for start in range(0, rows, tile):
        stop = start + tile
        mask_own = own_mask(tile, start, core, length, block)
        mask_other = other_mask(tile, start, core, length, block)
        query = q_ref[start:stop, :] * jnp.asarray(SCALE, BF16)
        outs = []
        for half in range(2):
            picked = jnp.where(lane // HEAD_DIM == half, query, jnp.zeros_like(query))
            s_own = dot_nt(ko_ref[:stop, :], picked)
            s_other = dot_nt(kx_ref[:stop, :], picked)
            d_own = jnp.where(mask_own, s_own[start:], MASKED)
            d_other = jnp.where(mask_other, s_other[start:], MASKED)
            if start:
                s_own = jnp.concatenate([s_own[:start], d_own], axis=0)
                s_other = jnp.concatenate([s_other[:start], d_other], axis=0)
            else:
                s_own, s_other = d_own, d_other
            top = jnp.maximum(
                jnp.max(s_own, axis=0, keepdims=True), jnp.max(s_other, axis=0, keepdims=True)
            )
            e_own = jnp.exp(s_own - top)
            e_other = jnp.exp(s_other - top)
            total = jnp.sum(e_own, axis=0, keepdims=True) + jnp.sum(e_other, axis=0, keepdims=True)
            lanes = slice(half * HEAD_DIM, (half + 1) * HEAD_DIM)
            mixed = dot_nn(vo_t[lanes, :stop], e_own.astype(BF16)) + dot_nn(
                vx_t[lanes, :stop], e_other.astype(BF16)
            )
            outs.append(mixed / total)
            lse_ref[0, half : half + 1, start:stop] = top + jnp.log(total)
        out_ref[start:stop, :] = jnp.concatenate(outs, axis=0).T.astype(BF16)


def attend_backward_kernel(
    tile, block, info, q_ref, ko_ref, vo_ref, kx_ref, vx_ref, go_ref, out_ref, lse_ref,
    dq_ref, dko_ref, dvo_ref, dkx_ref, dvx_ref, ako, avo, akx, avx,
):
    core, length = info[0], info[1]
    rows = q_ref.shape[0]
    lane = lax.broadcasted_iota(jnp.int32, (1, LANES), 1)
    ko_t = ko_ref[...].T
    kx_t = kx_ref[...].T
    for acc in (ako, avo, akx, avx):
        acc[...] = jnp.zeros_like(acc)
    for start in range(0, rows, tile):
        stop = start + tile
        mask_own = own_mask(tile, start, core, length, block)
        mask_other = other_mask(tile, start, core, length, block)
        query = q_ref[start:stop, :] * jnp.asarray(SCALE, BF16)
        grad = go_ref[start:stop, :]
        product = grad.astype(F32) * out_ref[start:stop, :].astype(F32)
        parts = []
        for half in range(2):
            mine = lane // HEAD_DIM == half
            picked = jnp.where(mine, query, jnp.zeros_like(query))
            grad_half = jnp.where(mine, grad, jnp.zeros_like(grad))
            pick = jnp.broadcast_to(jnp.where(mine, 1.0, 0.0).astype(F32), (8, LANES))
            inner = lax.dot_general(
                pick, product, (((1,), (1,)), ((), ())),
                precision=lax.Precision.HIGHEST, preferred_element_type=F32,
            )[:1]
            lse = lse_ref[0, half : half + 1, start:stop]
            lanes = slice(half * HEAD_DIM, (half + 1) * HEAD_DIM)
            part = jnp.zeros((HEAD_DIM, tile), F32)
            for key_ref, value_ref, key_t, mask, acc_k, acc_v in (
                (ko_ref, vo_ref, ko_t, mask_own, ako, avo),
                (kx_ref, vx_ref, kx_t, mask_other, akx, avx),
            ):
                prob = jnp.exp(dot_nt(key_ref[:stop, :], picked) - lse)
                last = jnp.where(mask, prob[start:], 0.0)
                prob = jnp.concatenate([prob[:start], last], axis=0) if start else last
                grad_prob = dot_nt(value_ref[:stop, :], grad_half)
                grad_score = (prob * (grad_prob - inner)).astype(BF16)
                acc_v[:stop, :] += dot_nn(prob.astype(BF16), grad_half)
                acc_k[:stop, :] += dot_nn(grad_score, picked)
                part = part + dot_nn(key_t[lanes, :stop], grad_score)
            parts.append(part)
        dq_ref[start:stop, :] = (jnp.concatenate(parts, axis=0) * SCALE).T.astype(BF16)
    for acc, ref in ((ako, dko_ref), (avo, dvo_ref), (akx, dkx_ref), (avx, dvx_ref)):
        ref[...] = acc[...].astype(ref.dtype)


def attend_forward(info, block, queries, keys_own, values_own, keys_other, values_other):
    rows, width = queries.shape
    pairs = width // LANES
    tile = min(256, rows)
    column = pl.BlockSpec((rows, LANES), lambda pair, info: (0, pair))
    return pl.pallas_call(
        functools.partial(attend_forward_kernel, tile, block),
        grid_spec=pltpu.PrefetchScalarGridSpec(
            num_scalar_prefetch=1,
            grid=(pairs,),
            in_specs=[column] * 5,
            out_specs=[column, pl.BlockSpec((1, 2, rows), lambda pair, info: (pair, 0, 0))],
        ),
        out_shape=[
            jax.ShapeDtypeStruct((rows, width), BF16),
            jax.ShapeDtypeStruct((pairs, 2, rows), F32),
        ],
        name="attend_forward",
    )(info, queries, keys_own, values_own, keys_other, values_other)


def attend_backward(info, block, first, pairs, queries, keys_own, values_own, keys_other, values_other, grad_heads,
                    heads_out, lse):
    rows = queries.shape[0]
    tile = min(256, rows)
    column = pl.BlockSpec((rows, LANES), lambda pair, info: (0, first + pair))
    result = pl.BlockSpec((rows, LANES), lambda pair, info: (0, pair))
    dtypes = (BF16, F32, F32, BF16, BF16)
    return pl.pallas_call(
        functools.partial(attend_backward_kernel, tile, block),
        grid_spec=pltpu.PrefetchScalarGridSpec(
            num_scalar_prefetch=1,
            grid=(pairs,),
            in_specs=[column] * 7 + [pl.BlockSpec((1, 2, rows), lambda pair, info: (first + pair, 0, 0))],
            out_specs=[result] * 5,
            scratch_shapes=[pltpu.VMEM((rows, LANES), F32)] * 4,
        ),
        out_shape=[jax.ShapeDtypeStruct((rows, pairs * LANES), dtype) for dtype in dtypes],
        name="attend_backward",
    )(info, queries, keys_own, values_own, keys_other, values_other, grad_heads, heads_out, lse)


HALF = 384


def spec(shape, index):
    return pl.BlockSpec(shape, index)


def whole(shape):
    zeros = (0,) * len(shape)
    return pl.BlockSpec(shape, lambda *_: zeros)


def call(kernel, name, grid, in_specs, out_specs, out_shape, scratch=()):
    return pl.pallas_call(
        kernel,
        grid_spec=pltpu.PrefetchScalarGridSpec(
            num_scalar_prefetch=1, grid=grid, in_specs=in_specs, out_specs=out_specs, scratch_shapes=list(scratch)
        ),
        out_shape=out_shape,
        name=name,
    )


def like(shape, dtype):
    return jax.ShapeDtypeStruct(shape, dtype)


def gather_slots(index, array, dtype):
    slots, block, width = array.shape
    steps = 4
    per = slots // steps

    def kernel(index_ref, array_ref, out_ref):
        first = pl.program_id(0) * per

        def copy(i, carry):
            out_ref[i] = array_ref[index_ref[first + i]].astype(dtype)
            return carry

        lax.fori_loop(0, per, copy, 0, unroll=min(per, 4))

    return call(
        kernel, "gather_slots", (steps,), [whole(array.shape)],
        spec((per, block, width), lambda i, _: (i, 0, 0)), like(array.shape, dtype),
    )(index, array)


def statistics(features):
    mean = jnp.mean(features, axis=-1, keepdims=True)
    centred = features - mean
    variance = jnp.mean(centred * centred, axis=-1, keepdims=True)
    scale = lax.rsqrt(variance + 1e-05)
    return centred * scale, scale


def norm_rows_back(grad, gain, xhat, scale):
    scaled = grad * gain
    return scale * (
        scaled
        - jnp.mean(scaled, axis=-1, keepdims=True)
        - xhat * jnp.mean(scaled * xhat, axis=-1, keepdims=True)
    )


def sum_rows(value):
    return jnp.sum(value, axis=0, keepdims=True)


def row_positions(tile, block, core):
    row = pl.program_id(0) * tile + lax.broadcasted_iota(jnp.int32, (tile, 1), 0)
    return (2 * (row // block) + core) * block + row % block


def rows_of(pieces_ref, tile):
    halves = [pieces_ref[:, side].astype(F32).reshape(tile, HALF) for side in range(2)]
    return jnp.concatenate(halves, axis=1)


def cols(index):
    return pl.ds(pl.multiple_of(index * HALF, LANES), HALF)


def rows_at(index):
    return pl.ds(pl.multiple_of(index * HALF, LANES), HALF)


ROOT = 0.7978845608028654
CUBE = 0.044715


def gelu_and_slope(value):
    square = value * value
    turn = jnp.tanh(ROOT * value * (1.0 + CUBE * square))
    slope = 0.5 * (1.0 + turn) + 0.5 * value * (1.0 - turn * turn) * ROOT * (1.0 + 3.0 * CUBE * square)
    return 0.5 * value * (1.0 + turn), slope


def enter_kernel(tile, block, info, pieces, thoughts, norms, bias_own, bias_other, own_k, own_v, direct, partner,
                 inputs_ref, normed_ref, k_ref, v_ref):
    core = info[0]
    position = row_positions(tile, block, core)
    features = rows_of(pieces, tile)
    for index in range(6):
        features = jnp.where(position == info[2 + index], thoughts[index : index + 1, :], features)
    inputs_ref[...] = features
    xhat, _ = statistics(features)
    normed = (xhat * norms[0:1, :] + norms[1:2, :]).astype(BF16)
    normed_ref[...] = normed
    project(core, normed_ref, own_k[0], direct[0], partner[0], None, None, k_ref)
    project(core, normed_ref, own_v[0], direct[1], partner[1], bias_own[1:2, :], bias_other[1:2, :], v_ref)


def project(core, normed, own, direct, partner, bias_own, bias_other, ref):
    mine = dot_nn(normed[...], own)
    theirs = dot_nn(normed[:, cols(core)], direct) + dot_nn(normed[:, cols(1 - core)], partner)
    if bias_own is not None:
        mine = mine + bias_own
        theirs = theirs + bias_other
    ref[:, :HALF] = mine.astype(BF16)
    ref[:, HALF:] = theirs.astype(BF16)


def queries_kernel(info, normed, bias_own, bias_other, own, direct, partner, q_ref):
    project(info[0], normed, own[0], direct[0], partner[0], bias_own[0:1, :], bias_other[0:1, :], q_ref)


def cotangent_kernel(tile, block, info, pieces, grad_ref):
    position = row_positions(tile, block, info[0])
    grad_ref[...] = jnp.where(position < info[1], rows_of(pieces, tile), 0.0).astype(BF16)


def middle_kernel(info, heads, inputs, norms, own, direct, partner, residual_ref, normed_ref, mixed):
    core = info[0]
    mixed[...] = dot_nn(heads[:, :HALF], own[...]) + norms[2:3, :]
    mixed[:, cols(core)] += dot_nn(heads[:, HALF:], direct[...])
    mixed[:, cols(1 - core)] += dot_nn(heads[:, HALF:], partner[...])
    residual = inputs[...] + mixed[...]
    residual_ref[...] = residual
    xhat, _ = statistics(residual)
    normed_ref[...] = (xhat * norms[0:1, :] + norms[1:2, :]).astype(BF16)


def mlp_rows_kernel(info, normed, grad, fc, bias, proj, mlp_ref, back_ref, active_t_ref, pre_ref, fcb_ref, mlp_sum, back_sum):
    step = pl.program_id(1)
    active, slope = gelu_and_slope(dot_nn(normed[...], fc[...]) + bias[...])
    active = active.astype(BF16)
    active_t_ref[...] = active.T
    grad_pre = (dot_nt(grad[...], proj[...]) * slope).astype(BF16)
    pre_ref[...] = grad_pre
    fcb_ref[0] = sum_rows(grad_pre.astype(F32))
    mlp = dot_nn(active, proj[...])
    back = dot_nt(grad_pre, fc[...])

    @pl.when(step == 0)
    def _():
        mlp_sum[...] = mlp
        back_sum[...] = back

    @pl.when((step > 0) & (step < pl.num_programs(1) - 1))
    def _():
        mlp_sum[...] += mlp
        back_sum[...] += back

    @pl.when(step == pl.num_programs(1) - 1)
    def _():
        mlp_ref[...] = (mlp_sum[...] + mlp).astype(mlp_ref.dtype)
        back_ref[...] = (back_sum[...] + back).astype(back_ref.dtype)


def mlp_grads_kernel(info, normed0, normed1, grad0, grad1, active0, active1, pre0, pre1, keep, send, normed_t):
    core = info[0]

    @pl.when(pl.program_id(0) == 0)
    def _():
        normed_t[0] = normed0[...].T
        normed_t[1] = normed1[...].T

    for index, ref in ((core, keep), (1 - core, send)):
        fc = dot_nn(normed_t[0, rows_at(index), :], pre0[...]) + dot_nn(normed_t[1, rows_at(index), :], pre1[...])
        proj = dot_nn(active0[rows_at(index), :], grad0[...]) + dot_nn(active1[rows_at(index), :], grad1[...])
        ref[:, : 2 * HALF] = fc.astype(BF16)
        ref[:, 2 * HALF :] = proj.astype(BF16)


def back_kernel(info, back, back_far, residual, grad, norms, own, direct, partner,
                grad_residual_ref, grad_attn_ref, grad_heads_ref, small_ref):
    core = info[0]
    xhat, scale = statistics(residual[...])
    incoming = back[...] + back_far[...].astype(F32)
    grad_out = grad[...].astype(F32)
    grad_residual = grad_out + norm_rows_back(incoming, norms[0:1, :], xhat, scale)
    grad_residual_ref[...] = grad_residual
    grad_attn = grad_residual.astype(BF16)
    grad_attn_ref[...] = grad_attn
    grad_heads_ref[:, :HALF] = dot_nt(grad_attn, own[...]).astype(BF16)
    theirs = dot_nt(grad_attn_ref[:, cols(core)], direct[...])
    theirs = theirs + dot_nt(grad_attn_ref[:, cols(1 - core)], partner[...])
    grad_heads_ref[:, HALF:] = theirs.astype(BF16)
    sums = jnp.concatenate(
        [sum_rows(incoming * xhat), sum_rows(incoming), sum_rows(grad_out), sum_rows(grad_attn.astype(F32))], axis=0
    )

    @pl.when(pl.program_id(0) == 0)
    def _():
        small_ref[...] = sums

    @pl.when(pl.program_id(0) > 0)
    def _():
        small_ref[...] += sums


def block_kernel(tile, block, info, residual, mlp, mlp_far, bias, block_ref):
    position = row_positions(tile, block, info[0])
    result = residual[...] + (mlp[...] + mlp_far[...].astype(F32) + bias[...])
    result = jnp.where(position < info[1], result, 0.0)
    for side in range(2):
        half = result[:, side * HALF : (side + 1) * HALF].reshape(tile // block, block, HALF)
        block_ref[:, side] = half.astype(BF16)


def key_value_grads(dk, dk_far, dv, dv_far):
    return (
        (dk[...] + dk_far[...].astype(F32)).astype(BF16),
        (dv[...] + dv_far[...].astype(F32)).astype(BF16),
    )


def attention_grads_kernel(info, normed, heads, grad_attn, dq, dk, dk_far, dv, dv_far, keep, send, normed_t):
    core = info[0]
    normed_t[...] = normed[...].T
    grads = (dq[...], *key_value_grads(dk, dk_far, dv, dv_far))
    heads_t = heads[...].T
    for index, ref in ((1 - core, send), (core, keep)):
        left = normed_t[rows_at(index), :]
        for place, grad in enumerate(grads):
            ref[:, place * HALF : (place + 1) * HALF] = dot_nn(left, grad).astype(BF16)
        ref[:, 3 * HALF :] = dot_nn(heads_t, grad_attn[:, cols(index)]).astype(BF16)


def leave_kernel(tile, block, info, inputs, grad_residual, norms, dq0, dk0, dk_far0, dv0, dv_far0,
                 dq1, dk1, dk_far1, dv1, dv_far1, own, direct, partner, direct_q, partner_q, pieces_ref, small_ref, back):
    core = info[0]
    mine = (dq0[...], *key_value_grads(dk0, dk_far0, dv0, dv_far0))
    theirs = (dq1[...], *key_value_grads(dk1, dk_far1, dv1, dv_far1))
    back[...] = sum(dot_nt(grad, own[index]) for index, grad in enumerate(mine))
    far_q, far_k, far_v = theirs
    back[:, cols(core)] += dot_nt(far_q, direct_q[0]) + dot_nt(far_k, direct[0]) + dot_nt(far_v, direct[1])
    back[:, cols(1 - core)] += dot_nt(far_q, partner_q[0]) + dot_nt(far_k, partner[0]) + dot_nt(far_v, partner[1])
    incoming = back[...]
    xhat, scale = statistics(inputs[...])
    result = grad_residual[...] + norm_rows_back(incoming, norms[0:1, :], xhat, scale)
    blocks = tile // block
    for side in range(2):
        pieces_ref[:, side] = result[:, side * HALF : (side + 1) * HALF].reshape(blocks, block, HALF).astype(BF16)
    biases = [
        jnp.concatenate([sum_rows(mine[place].astype(F32)), sum_rows(theirs[place].astype(F32))], axis=1)
        for place in (0, 2)
    ]
    sums = jnp.concatenate([sum_rows(incoming * xhat), sum_rows(incoming), *biases], axis=0)

    @pl.when(pl.program_id(0) == 0)
    def _():
        small_ref[...] = sums

    @pl.when(pl.program_id(0) > 0)
    def _():
        small_ref[...] += sums


def finish_rows(info, refs):
    core, near = info[0], info[8]
    size = refs[0].shape[0]
    for index, ref in enumerate(refs):
        base = (core if index < 2 else 1 - core) * HALF
        yield base, (near if index % 2 == 0 else 1 - near) * size, ref


def finish_mlp_kernel(info, *refs):
    fc_ref, proj_ref = refs[4:]
    for base, offset, ref in finish_rows(info, refs[:4]):
        rows = pl.ds(pl.multiple_of(base + offset, 64), ref.shape[0])
        fc_ref[rows, :] = ref[:, : 2 * HALF].astype(F32)
        proj_ref[rows, :] = ref[:, 2 * HALF :].astype(F32)


def finish_attention_kernel(info, *refs):
    qkv_ref, out_ref = refs[4:]
    for base, offset, ref in finish_rows(info, refs[:4]):
        rows = pl.ds(pl.multiple_of(base + offset, 64), ref.shape[0])
        for place in range(3):
            qkv_ref[place, rows, :] = ref[:, place * HALF : (place + 1) * HALF].astype(F32)
        heads = pl.ds(pl.multiple_of(offset, 64), ref.shape[0])
        out_ref[heads, pl.ds(pl.multiple_of(base, LANES), HALF)] = ref[:, 3 * HALF :].astype(F32)


def solution(mesh):
    groups = mesh.shape["dp"]
    bits = groups.bit_length() - 1
    assert groups == 1 << bits and mesh.shape["tensor"] == 2

    def pairs_of(change):
        table = []
        for group in range(groups):
            for side in range(2):
                to_group, to_side = change(group, side)
                table.append((group * 2 + side, to_group * 2 + to_side))
        return table

    tensor_pairs = pairs_of(lambda group, side: (group, 1 - side))
    bit_pairs = [pairs_of(lambda group, side, k=k: (group ^ (1 << k), side)) for k in range(bits)]
    deal_groups = [
        [group * 2 + side for group in range(core, groups, 2) for side in range(2)] for core in range(2)
    ]

    def body(
        tokens, cotangent, thoughts, latent_pos, lengths, dealing, qkv_weight, qv_bias, out_weight,
        out_bias, fc_weight, fc_bias, proj_weight, norm_gain, norm_shift,
    ):
        group = lax.axis_index("dp")
        side = lax.axis_index("tensor")
        core = group % 2
        slot = group - core + side
        slots, block, half_width = tokens.shape
        width = 2 * half_width
        rows = slots * block // 2
        hidden_half = fc_weight.shape[1]
        assert half_width == HALF and hidden_half == 4 * HALF
        tile = 256
        blocks = tile // block

        def cross(value):
            return lax.ppermute(value, AXES, tensor_pairs)

        def flip(value, bit=0):
            return lax.ppermute(value, AXES, bit_pairs[bit])

        def part(value, index, axis=0):
            size = value.shape[axis] // 2
            return lax.dynamic_slice_in_dim(value, index * size, size, axis)

        def join(flag, mine, theirs, axis=0):
            return jnp.where(
                flag == 0,
                jnp.concatenate([mine, theirs], axis=axis),
                jnp.concatenate([theirs, mine], axis=axis),
            )

        def exchange(array):
            return lax.all_to_all(
                array, AXES, split_axis=0, concat_axis=0, tiled=True, axis_index_groups=deal_groups
            )

        def deal(array):
            return exchange(gather_slots(dealing, array, BF16)).reshape(slots // 2, 2, block, half_width)

        order = jnp.arange(slots, dtype=jnp.int32)
        restore = jnp.sum(jnp.where(dealing[None, :] == order[:, None], order[None, :], 0), axis=1)

        qkv_sent = part(qkv_weight, core, 1)
        thoughts_core = flip(thoughts[0])
        tokens, thoughts_core = lax.optimization_barrier((tokens, thoughts_core))
        dealt = deal(tokens)
        kv_direct = cross(qkv_sent[1:])
        kv_partner = flip(kv_direct)
        biases_other = cross(qv_bias)
        near = jnp.where(core == side, thoughts[0], thoughts_core)
        far = cross(jnp.where(core == side, thoughts_core, thoughts[0]))
        latent_core = flip(latent_pos)
        latent = jnp.where(core == side, latent_pos, latent_core)[0]
        length = lengths[dealing[slot]]
        info = jnp.concatenate(
            [jnp.stack([core, length]).astype(jnp.int32), latent, jnp.stack([(group >> 1) & 1, group >> 2]).astype(jnp.int32)]
        )

        cot_dealt = gather_slots(dealing, cotangent, BF16)
        out_sent = part(out_weight, core, 1)
        thought_rows = join(side, near, far, axis=1).astype(F32)
        norms_in = jnp.stack([norm_gain[0], norm_shift[0]])
        norms_mid = jnp.stack([norm_gain[1], norm_shift[1], out_bias[0]])
        q_sent, out_sent, kv_direct, cot_dealt, thought_rows, biases_other, info, norms_in, norms_mid = (
            lax.optimization_barrier(
                (qkv_sent[:1], out_sent, kv_direct, cot_dealt, thought_rows, biases_other, info, norms_in, norms_mid)
            )
        )
        q_direct = cross(q_sent)
        qv_other = biases_other
        out_direct = cross(out_sent)
        cot_pieces = exchange(cot_dealt).reshape(slots // 2, 2, block, half_width)

        steps = rows // tile
        rowwise = spec((tile, width), lambda i, _: (i, 0))
        pieces_spec = spec((blocks, 2, block, half_width), lambda i, _: (i, 0, 0, 0))
        one, two, three = (spec((1, width, half_width), lambda i, _, place=place: (place, 0, 0)) for place in range(3))
        kv_specs = [whole(kv_direct.shape)] * 2
        q_specs = [whole(q_direct.shape)] * 2
        out_specs = [whole(out_weight.shape), whole(out_sent.shape), whole(out_sent.shape)]
        rows_bf, rows_f = like((rows, width), BF16), like((rows, width), F32)

        inputs, normed, keys_own, values_own = call(
            functools.partial(enter_kernel, tile, block), "enter", (steps,),
            [pieces_spec, whole((6, width)), whole((2, width)), whole((2, half_width)), whole((2, half_width)), two, three, *kv_specs],
            [rowwise] * 4, [rows_f, rows_bf, rows_bf, rows_bf],
        )(info, dealt, thought_rows, norms_in, qv_bias, qv_other,
          qkv_weight, qkv_weight, kv_direct, kv_partner)
        q_direct, keys_own, values_own, normed = lax.optimization_barrier((q_direct, keys_own, values_own, normed))
        q_partner = flip(q_direct)
        keys_other, values_other = flip(keys_own), flip(values_own)
        queries = call(
            queries_kernel, "queries", (steps,),
            [rowwise, whole((2, half_width)), whole((2, half_width)), one, *q_specs], rowwise, rows_bf,
        )(info, normed, qv_bias, qv_other, qkv_weight, q_direct, q_partner)
        queries, out_direct, cot_pieces = lax.optimization_barrier((queries, out_direct, cot_pieces))
        grad_mlp = call(
            functools.partial(cotangent_kernel, tile, block), "cotangent", (steps,), [pieces_spec], rowwise, rows_bf
        )(info, cot_pieces)
        queries, grad_mlp, keys_other, values_other = lax.optimization_barrier(
            (queries, grad_mlp, keys_other, values_other)
        )
        grad_far = cross(grad_mlp)
        out_partner = flip(out_direct)
        heads_out, lse = attend_forward(info, block, queries, keys_own, values_own, keys_other, values_other)
        heads_out, grad_far = lax.optimization_barrier((heads_out, grad_far))
        residual, normed_mlp = call(
            middle_kernel, "middle", (steps,),
            [rowwise, rowwise, whole((3, width)), *out_specs],
            [rowwise] * 2, [rows_f, rows_bf], [pltpu.VMEM((tile, width), F32)],
        )(info, heads_out, inputs, norms_mid,
          out_weight, out_direct, out_partner)
        normed_far = cross(normed_mlp)

        full = whole((rows, width))
        chunk = 2 * half_width

        def mlp_rows(normed_rows, grad_rows, dtype):
            units = hidden_half // 3
            by_row = spec((tile, width), lambda r, i, _: (r, 0))
            result = like((rows, width), dtype)
            return call(
                mlp_rows_kernel, "mlp_rows", (steps, 3),
                [by_row, by_row, spec((width, units), lambda r, i, _: (0, i)), spec((1, units), lambda r, i, _: (0, i)),
                 spec((units, width), lambda r, i, _: (i, 0))],
                [by_row, by_row, spec((units, tile), lambda r, i, _: (i, r)), spec((tile, units), lambda r, i, _: (r, i)),
                 spec((1, 1, units), lambda r, i, _: (r, 0, i))],
                [result, result, like((hidden_half, rows), BF16), like((rows, hidden_half), BF16),
                 like((steps, 1, hidden_half), F32)],
                [pltpu.VMEM((tile, width), F32)] * 2,
            )(info, normed_rows, grad_rows, fc_weight, fc_bias.reshape(1, hidden_half), proj_weight)

        mlp, back, active0, pre0, fcb0 = mlp_rows(normed_mlp, grad_mlp, F32)
        normed_far, mlp = lax.optimization_barrier((normed_far, mlp))
        mlp_sent, back_sent, active1, pre1, fcb1 = mlp_rows(normed_far, grad_far, BF16)
        back_far = cross(back_sent)
        quarter_spec = spec((half_width, 2 * chunk), lambda i, _: (0, i))
        by_unit = spec((rows, chunk), lambda i, _: (0, i))
        unit_rows = spec((chunk, rows), lambda i, _: (i, 0))
        mlp_keep, mlp_send = call(
            mlp_grads_kernel, "mlp_grads", (2,),
            [full] * 4 + [unit_rows] * 2 + [by_unit] * 2, [quarter_spec] * 2,
            [like((half_width, 4 * chunk), BF16)] * 2, [pltpu.VMEM((2, width, rows), BF16)],
        )(info, normed_mlp, normed_far, grad_mlp, grad_far, active0, active1, pre0, pre1)

        back_far, mlp_keep, mlp_send, mlp_sent = lax.optimization_barrier((back_far, mlp_keep, mlp_send, mlp_sent))
        mlp_far = cross(mlp_sent)
        near = (group >> 1) & 1
        half = half_width // 2
        upper = list(range(2, bits))
        levels = len(upper)
        flags = [(group >> link) & 1 for link in upper]
        sizes = [half >> (level + 1) for level in range(levels)]
        starts = [sum(flag * size for flag, size in zip(flags[:level], sizes)) for level in range(levels + 1)]

        def rows_sum(terms, start, size):
            total = 0.0
            for array, base in terms:
                total = total + lax.dynamic_slice_in_dim(array, base + start, size, 0).astype(F32)
            return total.astype(BF16)

        def section(level):
            if level == levels:
                return starts[level], sizes[-1]
            return starts[level] + (1 - flags[level]) * sizes[level], sizes[level]

        def widen(level, mine, theirs):
            return join(flags[level], mine, theirs)

        mlp_got = flip(mlp_send)
        grad_residual, grad_attn, grad_heads, small_mlp = call(
            back_kernel, "back", (steps,),
            [rowwise, rowwise, rowwise, rowwise, whole((1, width)), *out_specs],
            [rowwise, rowwise, rowwise, whole((4, width))],
            [rows_f, rows_bf, rows_bf, like((4, width), F32)],
        )(info, back, back_far, residual, grad_mlp, norm_gain[1:], out_weight, out_direct, out_partner)
        pairs = half_width // LANES
        grad_heads, mlp_got = lax.optimization_barrier((grad_heads, mlp_got))
        mlp_rows_kept = [(mlp_keep, near * half), (mlp_got, near * half)]
        mlp_rows_sent = [(mlp_keep, (1 - near) * half), (mlp_got, (1 - near) * half)]
        over_y = [rows_sum(mlp_rows_sent, *section(level)) for level in range(levels + 1)]
        grad_heads, *over_y = lax.optimization_barrier((grad_heads, *over_y))
        over_y[0] = flip(over_y[0], 1)

        def mlp_section(level):
            start, size = section(level)
            return rows_sum([*mlp_rows_kept, (over_y[level], -start)], start, size)

        def backward(first, grad):
            grad_q, grad_ko, grad_vo, grad_kx, grad_vx = attend_backward(
                info, block, first, pairs, queries, keys_own, values_own, keys_other, values_other, grad, heads_out, lse
            )
            return grad_q, grad_ko, grad_vo, grad_kx, grad_vx

        def with_far(grads, *ties):
            grad_q, grad_ko, grad_vo, grad_kx, grad_vx = grads
            far_k, far_v, *ties = lax.optimization_barrier((flip(grad_kx), flip(grad_vx), *ties))
            return (grad_q, grad_ko, far_k, grad_vo, far_v), ties

        other = backward(pairs, grad_heads)
        mlp_far, *tied = lax.optimization_barrier((mlp_far, *over_y, *other))
        over_y, other = tied[: levels + 1], tied[levels + 1 :]
        over_y[1] = flip(over_y[1], 1)
        block_pieces = call(
            functools.partial(block_kernel, tile, block), "block", (steps,),
            [rowwise, rowwise, rowwise, whole((1, width))], pieces_spec,
            like((slots // 2, 2, block, half_width), BF16),
        )(info, residual, mlp, mlp_far, out_bias[1:])
        other, (block_pieces,) = with_far(other, block_pieces)
        block_back = exchange(block_pieces.reshape(slots, block, half_width))

        def attention_grads(column, grads):
            shape = (half_width, 4 * half_width)
            return call(
                attention_grads_kernel, "attention_grads", (1,),
                [full, spec((rows, half_width), lambda i, _: (0, column)), full, *[whole((rows, half_width))] * 5],
                [whole(shape)] * 2, [like(shape, BF16)] * 2, [pltpu.VMEM((width, rows), BF16)],
            )(info, normed, heads_out, grad_attn, *grads)

        keep_other, send_other = attention_grads(1, other)
        keep_other, send_other, *over_y = lax.optimization_barrier((keep_other, send_other, *over_y))
        over_y[2:] = [flip(value, 1) for value in over_y[2:]]
        got_other = flip(send_other)
        mlp_stage = mlp_section(0)
        x_first, x_last = (
            rows_sum([(keep_other, place * half), (got_other, place * half)], 0, half) for place in (1 - near, near)
        )
        x_first, x_last, mlp_stage, grad_heads = lax.optimization_barrier((x_first, x_last, mlp_stage, grad_heads))
        x_first = cross(x_first)
        mlp_stage = flip(mlp_stage, upper[0])
        own = backward(0, grad_heads)
        x_first, x_last, mlp_stage, block_back, *tied = lax.optimization_barrier(
            (x_first, x_last, mlp_stage, block_back, *over_y[2:], *own)
        )
        over_y[2:], own = tied[: levels - 1], tied[levels - 1 :]
        x_last = cross(x_last)
        mlp_rows_kept.append((mlp_stage, -starts[1]))
        own, (mlp_stage,) = with_far(own, mlp_section(1))
        mlp_stage = flip(mlp_stage, upper[1])
        keep_own, send_own = attention_grads(0, own)
        keep_own, send_own, mlp_stage, x_last = lax.optimization_barrier((keep_own, send_own, mlp_stage, x_last))
        block_out = gather_slots(restore, block_back, F32)
        got_own, block_out = lax.optimization_barrier((flip(send_own), block_out))
        mlp_rows_kept.append((mlp_stage, -starts[2]))
        for level in range(2, levels):
            mlp_rows_kept.append((flip(mlp_section(level), upper[level]), -starts[level + 1]))
        mlp_piece = mlp_section(levels)
        for level in reversed(range(2, levels)):
            mlp_piece = widen(level, mlp_piece, flip(mlp_piece, upper[level]))
        sent = rows_sum([(keep_own, (1 - near) * half), (got_own, (1 - near) * half), (x_first, 0)], 0, half)
        sent, mlp_piece, *own = lax.optimization_barrier((sent, mlp_piece, *own))
        over_bit = flip(sent, 1)
        mlp_stage = flip(mlp_piece, upper[1])
        half_rows = spec((tile, half_width), lambda i, _: (i, 0))
        input_pieces, small_attn = call(
            functools.partial(leave_kernel, tile, block), "leave", (steps,),
            [rowwise, rowwise, whole((1, width)), *[half_rows] * 10, whole(qkv_weight.shape), *kv_specs, *q_specs],
            [pieces_spec, whole((4, width))],
            [like((slots // 2, 2, block, half_width), BF16), like((4, width), F32)],
            [pltpu.VMEM((tile, width), F32)],
        )(info, inputs, grad_residual, norm_gain[:1], *own, *other, qkv_weight, kv_direct, kv_partner, q_direct, q_partner)
        input_pieces, small_attn, over_bit, mlp_stage = lax.optimization_barrier(
            (input_pieces, small_attn, over_bit, mlp_stage)
        )
        input_back = exchange(input_pieces.reshape(slots, block, half_width))

        def ordered(vectors):
            return join(side, vectors[:, :half_width], vectors[:, half_width:], axis=1)

        hidden = 2 * hidden_half
        fcb0 = jnp.sum(fcb0 + fcb1, axis=0)
        fcb = join(side, fcb0, jnp.zeros_like(fcb0), axis=1).reshape(hidden // width, width)
        small = jnp.concatenate([small_mlp, small_attn[:2], ordered(small_attn[2:]), fcb], axis=0)
        links = [functools.partial(flip, bit=1), flip, cross, *[functools.partial(flip, bit=bit) for bit in upper]]

        def add_over(value):
            return value + links.pop(0)(value) if links else value

        mlp_piece = widen(1, mlp_piece, mlp_stage)
        mlp_stage = flip(mlp_piece, upper[0])
        small = add_over(small)
        mlp_stage, small, over_bit = lax.optimization_barrier((mlp_stage, small, over_bit))
        mlp_piece = widen(0, mlp_piece, mlp_stage)
        mlp_over, mlp_core = flip(mlp_piece, 1), flip(mlp_piece)
        kept = [(keep_own, near * half), (got_own, near * half), (x_last, 0), (over_bit, 0)]
        for level in range(levels):
            stage = flip(rows_sum(kept, *section(level)), upper[level])
            small = add_over(small)
            stage, small = lax.optimization_barrier((stage, small))
            if level == 0:
                stage, mlp_core = lax.optimization_barrier((stage, mlp_core))
            kept.append((stage, -starts[level + 1]))
        piece = rows_sum(kept, *section(levels))
        for level in reversed(range(levels)):
            stage = flip(piece, upper[level])
            small = add_over(small)
            stage, small = lax.optimization_barrier((stage, small))
            if level == levels - 1:
                stage, input_back = lax.optimization_barrier((stage, input_back))
            if level == 0:
                stage, mlp_over = lax.optimization_barrier((stage, mlp_over))
            piece = widen(level, piece, stage)
        while links:
            small = add_over(small)
        over, near_core = flip(piece, 1), flip(piece)
        mlp_over, mlp_core, piece = lax.optimization_barrier((mlp_over, mlp_core, piece))
        mlp_all = [mlp_piece, mlp_over, mlp_core, flip(mlp_over)]
        input_grad = gather_slots(restore, input_back, F32)
        fc_grad, proj_grad = call(
            finish_mlp_kernel, "finish_mlp", (2,), [spec((half, 2 * chunk), lambda i, _: (0, i))] * 4,
            [spec((width, chunk), lambda i, _: (0, i)), spec((chunk, width), lambda i, _: (i, 0))],
            [like(fc_weight.shape, F32), like(proj_weight.shape, F32)],
        )(info, *mlp_all)
        over, fc_grad, proj_grad, input_grad, small = lax.optimization_barrier((over, fc_grad, proj_grad, input_grad, small))
        qkv_grad, out_grad = call(
            finish_attention_kernel, "finish_attention", (1,), [whole((half, 2 * chunk))] * 4,
            [whole(qkv_weight.shape), whole(out_weight.shape)],
            [like(qkv_weight.shape, F32), like(out_weight.shape, F32)],
        )(info, piece, over, near_core, flip(over))

        gain_mlp, shift_mlp, bias_mlp, bias_attn, gain_attn, shift_attn = (small[i] for i in range(6))
        return (
            block_out,
            input_grad,
            qkv_grad,
            part(small[6:8], side, 1),
            out_grad,
            jnp.stack([bias_attn, bias_mlp]),
            fc_grad,
            part(small[8:].reshape(hidden), side),
            proj_grad,
            jnp.stack([gain_attn, gain_mlp]),
            jnp.stack([shift_attn, shift_mlp]),
        )

    return jax.shard_map(
        body,
        mesh=mesh,
        in_specs=(
            P(None, "dp", "tensor"),
            P(None, "dp", "tensor"),
            P("dp", None, "tensor"),
            P("dp", None),
            P(),
            P(),
            P(None, None, "tensor"),
            P(None, "tensor"),
            P("tensor", None),
            P(),
            P(None, "tensor"),
            P("tensor"),
            P("tensor", None),
            P(),
            P(),
        ),
        out_specs=(
            P(None, "dp", "tensor"),
            P(None, "dp", "tensor"),
            P(None, None, "tensor"),
            P(None, "tensor"),
            P("tensor", None),
            P(),
            P(None, "tensor"),
            P("tensor"),
            P("tensor", None),
            P(),
            P(),
        ),
        check_vma=False,
    )
```

```python
import functools

import jax
import jax.numpy as jnp
from jax import lax
from jax.experimental import pallas as pl
from jax.experimental.pallas import tpu as pltpu
from jax.sharding import PartitionSpec as P

HEAD_DIM = 64
LANES = 128
AXES = ("dp", "tensor")
SCALE = HEAD_DIM ** (-0.5)
MASKED = -1e30
BF16 = jnp.bfloat16
F32 = jnp.float32


def dot_nn(left, right):
    return lax.dot_general(left, right, (((1,), (0,)), ((), ())), preferred_element_type=F32)


def dot_nt(left, right):
    return lax.dot_general(left, right, (((1,), (1,)), ((), ())), preferred_element_type=F32)


def dot_tn(left, right):
    return lax.dot_general(left, right, (((0,), (0,)), ((), ())), preferred_element_type=F32)


def own_mask(tile, start, core, length, block):
    key = lax.broadcasted_iota(jnp.int32, (tile, tile), 0)
    query = lax.broadcasted_iota(jnp.int32, (tile, tile), 1)
    key_row = start + key
    key_pos = (2 * (key_row // block) + core) * block + key_row % block
    return (key <= query) & (key_pos < length)


def other_mask(tile, start, core, length, block):
    key = lax.broadcasted_iota(jnp.int32, (tile, tile), 0)
    query = lax.broadcasted_iota(jnp.int32, (tile, tile), 1)
    key_row = start + key
    key_pos = (2 * (key_row // block) + 1 - core) * block + key_row % block
    return (key // block <= query // block - (1 - core)) & (key_pos < length)


def attend_forward_kernel(tile, block, info, q_ref, ko_ref, vo_ref, kx_ref, vx_ref, out_ref, lse_ref):
    core, length = info[0], info[1]
    rows = q_ref.shape[0]
    lane = lax.broadcasted_iota(jnp.int32, (1, LANES), 1)
    vo_t = vo_ref[...].T
    vx_t = vx_ref[...].T
    for start in range(0, rows, tile):
        stop = start + tile
        mask_own = own_mask(tile, start, core, length, block)
        mask_other = other_mask(tile, start, core, length, block)
        query = q_ref[start:stop, :] * jnp.asarray(SCALE, BF16)
        outs = []
        for half in range(2):
            picked = jnp.where(lane // HEAD_DIM == half, query, jnp.zeros_like(query))
            s_own = dot_nt(ko_ref[:stop, :], picked)
            s_other = dot_nt(kx_ref[:stop, :], picked)
            d_own = jnp.where(mask_own, s_own[start:], MASKED)
            d_other = jnp.where(mask_other, s_other[start:], MASKED)
            if start:
                s_own = jnp.concatenate([s_own[:start], d_own], axis=0)
                s_other = jnp.concatenate([s_other[:start], d_other], axis=0)
            else:
                s_own, s_other = d_own, d_other
            top = jnp.maximum(
                jnp.max(s_own, axis=0, keepdims=True), jnp.max(s_other, axis=0, keepdims=True)
            )
            e_own = jnp.exp(s_own - top)
            e_other = jnp.exp(s_other - top)
            total = jnp.sum(e_own, axis=0, keepdims=True) + jnp.sum(e_other, axis=0, keepdims=True)
            lanes = slice(half * HEAD_DIM, (half + 1) * HEAD_DIM)
            mixed = dot_nn(vo_t[lanes, :stop], e_own.astype(BF16)) + dot_nn(
                vx_t[lanes, :stop], e_other.astype(BF16)
            )
            outs.append(mixed / total)
            lse_ref[0, half : half + 1, start:stop] = top + jnp.log(total)
        out_ref[start:stop, :] = jnp.concatenate(outs, axis=0).T.astype(BF16)


def attend_backward_kernel(
    tile, block, info, q_ref, ko_ref, vo_ref, kx_ref, vx_ref, go_ref, out_ref, lse_ref,
    dq_ref, dko_ref, dvo_ref, dkx_ref, dvx_ref, ako, avo, akx, avx,
):
    core, length = info[0], info[1]
    rows = q_ref.shape[0]
    lane = lax.broadcasted_iota(jnp.int32, (1, LANES), 1)
    ko_t = ko_ref[...].T
    kx_t = kx_ref[...].T
    for acc in (ako, avo, akx, avx):
        acc[...] = jnp.zeros_like(acc)
    for start in range(0, rows, tile):
        stop = start + tile
        mask_own = own_mask(tile, start, core, length, block)
        mask_other = other_mask(tile, start, core, length, block)
        query = q_ref[start:stop, :] * jnp.asarray(SCALE, BF16)
        grad = go_ref[start:stop, :]
        product = grad.astype(F32) * out_ref[start:stop, :].astype(F32)
        parts = []
        for half in range(2):
            mine = lane // HEAD_DIM == half
            picked = jnp.where(mine, query, jnp.zeros_like(query))
            grad_half = jnp.where(mine, grad, jnp.zeros_like(grad))
            pick = jnp.broadcast_to(jnp.where(mine, 1.0, 0.0).astype(F32), (8, LANES))
            inner = lax.dot_general(
                pick, product, (((1,), (1,)), ((), ())),
                precision=lax.Precision.HIGHEST, preferred_element_type=F32,
            )[:1]
            lse = lse_ref[0, half : half + 1, start:stop]
            lanes = slice(half * HEAD_DIM, (half + 1) * HEAD_DIM)
            part = jnp.zeros((HEAD_DIM, tile), F32)
            for key_ref, value_ref, key_t, mask, acc_k, acc_v in (
                (ko_ref, vo_ref, ko_t, mask_own, ako, avo),
                (kx_ref, vx_ref, kx_t, mask_other, akx, avx),
            ):
                prob = jnp.exp(dot_nt(key_ref[:stop, :], picked) - lse)
                last = jnp.where(mask, prob[start:], 0.0)
                prob = jnp.concatenate([prob[:start], last], axis=0) if start else last
                grad_prob = dot_nt(value_ref[:stop, :], grad_half)
                grad_score = (prob * (grad_prob - inner)).astype(BF16)
                acc_v[:stop, :] += dot_nn(prob.astype(BF16), grad_half)
                acc_k[:stop, :] += dot_nn(grad_score, picked)
                part = part + dot_nn(key_t[lanes, :stop], grad_score)
            parts.append(part)
        dq_ref[start:stop, :] = (jnp.concatenate(parts, axis=0) * SCALE).T.astype(BF16)
    for acc, ref in ((ako, dko_ref), (avo, dvo_ref), (akx, dkx_ref), (avx, dvx_ref)):
        ref[...] = acc[...].astype(ref.dtype)


def attend_forward(info, block, queries, keys_own, values_own, keys_other, values_other):
    rows, width = queries.shape
    pairs = width // LANES
    tile = min(256, rows)
    column = pl.BlockSpec((rows, LANES), lambda pair, info: (0, pair))
    return pl.pallas_call(
        functools.partial(attend_forward_kernel, tile, block),
        grid_spec=pltpu.PrefetchScalarGridSpec(
            num_scalar_prefetch=1,
            grid=(pairs,),
            in_specs=[column] * 5,
            out_specs=[column, pl.BlockSpec((1, 2, rows), lambda pair, info: (pair, 0, 0))],
        ),
        out_shape=[
            jax.ShapeDtypeStruct((rows, width), BF16),
            jax.ShapeDtypeStruct((pairs, 2, rows), F32),
        ],
        name="attend_forward",
    )(info, queries, keys_own, values_own, keys_other, values_other)


def attend_backward(info, block, first, pairs, queries, keys_own, values_own, keys_other, values_other, grad_heads,
                    heads_out, lse):
    rows = queries.shape[0]
    tile = min(256, rows)
    column = pl.BlockSpec((rows, LANES), lambda pair, info: (0, first + pair))
    result = pl.BlockSpec((rows, LANES), lambda pair, info: (0, pair))
    dtypes = (BF16, F32, F32, BF16, BF16)
    return pl.pallas_call(
        functools.partial(attend_backward_kernel, tile, block),
        grid_spec=pltpu.PrefetchScalarGridSpec(
            num_scalar_prefetch=1,
            grid=(pairs,),
            in_specs=[column] * 7 + [pl.BlockSpec((1, 2, rows), lambda pair, info: (first + pair, 0, 0))],
            out_specs=[result] * 5,
            scratch_shapes=[pltpu.VMEM((rows, LANES), F32)] * 4,
        ),
        out_shape=[jax.ShapeDtypeStruct((rows, pairs * LANES), dtype) for dtype in dtypes],
        name="attend_backward",
    )(info, queries, keys_own, values_own, keys_other, values_other, grad_heads, heads_out, lse)


HALF = 384


def spec(shape, index):
    return pl.BlockSpec(shape, index)


def whole(shape):
    zeros = (0,) * len(shape)
    return pl.BlockSpec(shape, lambda *_: zeros)


def call(kernel, name, grid, in_specs, out_specs, out_shape, scratch=()):
    return pl.pallas_call(
        kernel,
        grid_spec=pltpu.PrefetchScalarGridSpec(
            num_scalar_prefetch=1, grid=grid, in_specs=in_specs, out_specs=out_specs, scratch_shapes=list(scratch)
        ),
        out_shape=out_shape,
        name=name,
    )


def like(shape, dtype):
    return jax.ShapeDtypeStruct(shape, dtype)


def gather_slots(index, array, dtype):
    slots, block, width = array.shape
    steps = 4
    per = slots // steps

    def kernel(index_ref, array_ref, out_ref):
        first = pl.program_id(0) * per

        def copy(i, carry):
            out_ref[i] = array_ref[index_ref[first + i]].astype(dtype)
            return carry

        lax.fori_loop(0, per, copy, 0, unroll=min(per, 4))

    return call(
        kernel, "gather_slots", (steps,), [whole(array.shape)],
        spec((per, block, width), lambda i, _: (i, 0, 0)), like(array.shape, dtype),
    )(index, array)


def statistics(features):
    mean = jnp.mean(features, axis=-1, keepdims=True)
    centred = features - mean
    variance = jnp.mean(centred * centred, axis=-1, keepdims=True)
    scale = lax.rsqrt(variance + 1e-05)
    return centred * scale, scale


def norm_rows_back(grad, gain, xhat, scale):
    scaled = grad * gain
    return scale * (
        scaled
        - jnp.mean(scaled, axis=-1, keepdims=True)
        - xhat * jnp.mean(scaled * xhat, axis=-1, keepdims=True)
    )


def sum_rows(value):
    return jnp.sum(value, axis=0, keepdims=True)


def row_positions(tile, block, core):
    row = pl.program_id(0) * tile + lax.broadcasted_iota(jnp.int32, (tile, 1), 0)
    return (2 * (row // block) + core) * block + row % block


def rows_of(pieces_ref, tile):
    halves = [pieces_ref[:, side].astype(F32).reshape(tile, HALF) for side in range(2)]
    return jnp.concatenate(halves, axis=1)


def cols(index):
    return pl.ds(pl.multiple_of(index * HALF, LANES), HALF)


def rows_at(index):
    return pl.ds(pl.multiple_of(index * HALF, LANES), HALF)


ROOT = 0.7978845608028654
CUBE = 0.044715


def gelu_and_slope(value):
    square = value * value
    turn = jnp.tanh(ROOT * value * (1.0 + CUBE * square))
    slope = 0.5 * (1.0 + turn) + 0.5 * value * (1.0 - turn * turn) * ROOT * (1.0 + 3.0 * CUBE * square)
    return 0.5 * value * (1.0 + turn), slope


def enter_kernel(tile, block, info, pieces, thoughts, norms, bias_own, bias_other, own_k, own_v, direct, partner,
                 inputs_ref, normed_ref, k_ref, v_ref):
    core = info[0]
    position = row_positions(tile, block, core)
    features = rows_of(pieces, tile)
    for index in range(6):
        features = jnp.where(position == info[2 + index], thoughts[index : index + 1, :], features)
    inputs_ref[...] = features
    xhat, _ = statistics(features)
    normed = (xhat * norms[0:1, :] + norms[1:2, :]).astype(BF16)
    normed_ref[...] = normed
    project(core, normed_ref, own_k[0], direct[0], partner[0], None, None, k_ref)
    project(core, normed_ref, own_v[0], direct[1], partner[1], bias_own[1:2, :], bias_other[1:2, :], v_ref)


def project(core, normed, own, direct, partner, bias_own, bias_other, ref):
    mine = dot_nn(normed[...], own)
    theirs = dot_nn(normed[:, cols(core)], direct) + dot_nn(normed[:, cols(1 - core)], partner)
    if bias_own is not None:
        mine = mine + bias_own
        theirs = theirs + bias_other
    ref[:, :HALF] = mine.astype(BF16)
    ref[:, HALF:] = theirs.astype(BF16)


def queries_kernel(info, normed, bias_own, bias_other, own, direct, partner, q_ref):
    project(info[0], normed, own[0], direct[0], partner[0], bias_own[0:1, :], bias_other[0:1, :], q_ref)


def cotangent_kernel(tile, block, info, pieces, grad_ref):
    position = row_positions(tile, block, info[0])
    grad_ref[...] = jnp.where(position < info[1], rows_of(pieces, tile), 0.0).astype(BF16)


def middle_kernel(info, heads, inputs, norms, own, direct, partner, residual_ref, normed_ref, mixed):
    core = info[0]
    mixed[...] = dot_nn(heads[:, :HALF], own[...]) + norms[2:3, :]
    mixed[:, cols(core)] += dot_nn(heads[:, HALF:], direct[...])
    mixed[:, cols(1 - core)] += dot_nn(heads[:, HALF:], partner[...])
    residual = inputs[...] + mixed[...]
    residual_ref[...] = residual
    xhat, _ = statistics(residual)
    normed_ref[...] = (xhat * norms[0:1, :] + norms[1:2, :]).astype(BF16)


def mlp_rows_kernel(info, normed, grad, fc, bias, proj, mlp_ref, back_ref, active_t_ref, pre_ref, fcb_ref, mlp_sum, back_sum):
    step = pl.program_id(1)
    active, slope = gelu_and_slope(dot_nn(normed[...], fc[...]) + bias[...])
    active = active.astype(BF16)
    active_t_ref[...] = active.T
    grad_pre = (dot_nt(grad[...], proj[...]) * slope).astype(BF16)
    pre_ref[...] = grad_pre
    fcb_ref[0] = sum_rows(grad_pre.astype(F32))
    mlp = dot_nn(active, proj[...])
    back = dot_nt(grad_pre, fc[...])

    @pl.when(step == 0)
    def _():
        mlp_sum[...] = mlp
        back_sum[...] = back

    @pl.when((step > 0) & (step < pl.num_programs(1) - 1))
    def _():
        mlp_sum[...] += mlp
        back_sum[...] += back

    @pl.when(step == pl.num_programs(1) - 1)
    def _():
        mlp_ref[...] = (mlp_sum[...] + mlp).astype(mlp_ref.dtype)
        back_ref[...] = (back_sum[...] + back).astype(back_ref.dtype)


def mlp_grads_kernel(info, normed0, normed1, grad0, grad1, active0, active1, pre0, pre1, keep, send, normed_t):
    core = info[0]

    @pl.when(pl.program_id(0) == 0)
    def _():
        normed_t[0] = normed0[...].T
        normed_t[1] = normed1[...].T

    for index, ref in ((core, keep), (1 - core, send)):
        fc = dot_nn(normed_t[0, rows_at(index), :], pre0[...]) + dot_nn(normed_t[1, rows_at(index), :], pre1[...])
        proj = dot_nn(active0[rows_at(index), :], grad0[...]) + dot_nn(active1[rows_at(index), :], grad1[...])
        ref[:, : 2 * HALF] = fc.astype(BF16)
        ref[:, 2 * HALF :] = proj.astype(BF16)


def back_kernel(info, back, back_far, residual, grad, norms, own, direct, partner,
                grad_residual_ref, grad_attn_ref, grad_heads_ref, small_ref):
    core = info[0]
    xhat, scale = statistics(residual[...])
    incoming = back[...] + back_far[...].astype(F32)
    grad_out = grad[...].astype(F32)
    grad_residual = grad_out + norm_rows_back(incoming, norms[0:1, :], xhat, scale)
    grad_residual_ref[...] = grad_residual
    grad_attn = grad_residual.astype(BF16)
    grad_attn_ref[...] = grad_attn
    grad_heads_ref[:, :HALF] = dot_nt(grad_attn, own[...]).astype(BF16)
    theirs = dot_nt(grad_attn_ref[:, cols(core)], direct[...])
    theirs = theirs + dot_nt(grad_attn_ref[:, cols(1 - core)], partner[...])
    grad_heads_ref[:, HALF:] = theirs.astype(BF16)
    sums = jnp.concatenate(
        [sum_rows(incoming * xhat), sum_rows(incoming), sum_rows(grad_out), sum_rows(grad_attn.astype(F32))], axis=0
    )

    @pl.when(pl.program_id(0) == 0)
    def _():
        small_ref[...] = sums

    @pl.when(pl.program_id(0) > 0)
    def _():
        small_ref[...] += sums


def block_kernel(tile, block, info, residual, mlp, mlp_far, bias, block_ref):
    position = row_positions(tile, block, info[0])
    result = residual[...] + (mlp[...] + mlp_far[...].astype(F32) + bias[...])
    result = jnp.where(position < info[1], result, 0.0)
    for side in range(2):
        half = result[:, side * HALF : (side + 1) * HALF].reshape(tile // block, block, HALF)
        block_ref[:, side] = half.astype(BF16)


def key_value_grads(dk, dk_far, dv, dv_far):
    return (
        (dk[...] + dk_far[...].astype(F32)).astype(BF16),
        (dv[...] + dv_far[...].astype(F32)).astype(BF16),
    )


def attention_grads_kernel(info, normed, heads, grad_attn, dq, dk, dk_far, dv, dv_far, keep, send, normed_t):
    core = info[0]
    normed_t[...] = normed[...].T
    grads = (dq[...], *key_value_grads(dk, dk_far, dv, dv_far))
    heads_t = heads[...].T
    for index, ref in ((1 - core, send), (core, keep)):
        left = normed_t[rows_at(index), :]
        for place, grad in enumerate(grads):
            ref[:, place * HALF : (place + 1) * HALF] = dot_nn(left, grad).astype(BF16)
        ref[:, 3 * HALF :] = dot_nn(heads_t, grad_attn[:, cols(index)]).astype(BF16)


def leave_kernel(tile, block, info, inputs, grad_residual, norms, dq0, dk0, dk_far0, dv0, dv_far0,
                 dq1, dk1, dk_far1, dv1, dv_far1, own, direct, partner, direct_q, partner_q, pieces_ref, small_ref, back):
    core = info[0]
    mine = (dq0[...], *key_value_grads(dk0, dk_far0, dv0, dv_far0))
    theirs = (dq1[...], *key_value_grads(dk1, dk_far1, dv1, dv_far1))
    back[...] = sum(dot_nt(grad, own[index]) for index, grad in enumerate(mine))
    far_q, far_k, far_v = theirs
    back[:, cols(core)] += dot_nt(far_q, direct_q[0]) + dot_nt(far_k, direct[0]) + dot_nt(far_v, direct[1])
    back[:, cols(1 - core)] += dot_nt(far_q, partner_q[0]) + dot_nt(far_k, partner[0]) + dot_nt(far_v, partner[1])
    incoming = back[...]
    xhat, scale = statistics(inputs[...])
    result = grad_residual[...] + norm_rows_back(incoming, norms[0:1, :], xhat, scale)
    blocks = tile // block
    for side in range(2):
        pieces_ref[:, side] = result[:, side * HALF : (side + 1) * HALF].reshape(blocks, block, HALF).astype(BF16)
    biases = [
        jnp.concatenate([sum_rows(mine[place].astype(F32)), sum_rows(theirs[place].astype(F32))], axis=1)
        for place in (0, 2)
    ]
    sums = jnp.concatenate([sum_rows(incoming * xhat), sum_rows(incoming), *biases], axis=0)

    @pl.when(pl.program_id(0) == 0)
    def _():
        small_ref[...] = sums

    @pl.when(pl.program_id(0) > 0)
    def _():
        small_ref[...] += sums


def finish_rows(info, refs):
    core, near = info[0], info[8]
    size = refs[0].shape[0]
    for index, ref in enumerate(refs):
        base = (core if index < 2 else 1 - core) * HALF
        yield base, (near if index % 2 == 0 else 1 - near) * size, ref


def finish_mlp_kernel(info, *refs):
    fc_ref, proj_ref = refs[4:]
    for base, offset, ref in finish_rows(info, refs[:4]):
        rows = pl.ds(pl.multiple_of(base + offset, 64), ref.shape[0])
        fc_ref[rows, :] = ref[:, : 2 * HALF].astype(F32)
        proj_ref[rows, :] = ref[:, 2 * HALF :].astype(F32)


def finish_attention_kernel(info, *refs):
    qkv_ref, out_ref = refs[4:]
    for base, offset, ref in finish_rows(info, refs[:4]):
        rows = pl.ds(pl.multiple_of(base + offset, 64), ref.shape[0])
        for place in range(3):
            qkv_ref[place, rows, :] = ref[:, place * HALF : (place + 1) * HALF].astype(F32)
        heads = pl.ds(pl.multiple_of(offset, 64), ref.shape[0])
        out_ref[heads, pl.ds(pl.multiple_of(base, LANES), HALF)] = ref[:, 3 * HALF :].astype(F32)


def solution(mesh):
    groups = mesh.shape["dp"]
    bits = groups.bit_length() - 1
    assert groups == 1 << bits and mesh.shape["tensor"] == 2

    def pairs_of(change):
        table = []
        for group in range(groups):
            for side in range(2):
                to_group, to_side = change(group, side)
                table.append((group * 2 + side, to_group * 2 + to_side))
        return table

    tensor_pairs = pairs_of(lambda group, side: (group, 1 - side))
    bit_pairs = [pairs_of(lambda group, side, k=k: (group ^ (1 << k), side)) for k in range(bits)]
    deal_groups = [
        [group * 2 + side for group in range(core, groups, 2) for side in range(2)] for core in range(2)
    ]

    def body(
        tokens, cotangent, thoughts, latent_pos, lengths, dealing, qkv_weight, qv_bias, out_weight,
        out_bias, fc_weight, fc_bias, proj_weight, norm_gain, norm_shift,
    ):
        group = lax.axis_index("dp")
        side = lax.axis_index("tensor")
        core = group % 2
        slot = group - core + side
        slots, block, half_width = tokens.shape
        width = 2 * half_width
        rows = slots * block // 2
        hidden_half = fc_weight.shape[1]
        assert half_width == HALF and hidden_half == 4 * HALF
        tile = 256
        blocks = tile // block

        def cross(value):
            return lax.ppermute(value, AXES, tensor_pairs)

        def flip(value, bit=0):
            return lax.ppermute(value, AXES, bit_pairs[bit])

        def part(value, index, axis=0):
            size = value.shape[axis] // 2
            return lax.dynamic_slice_in_dim(value, index * size, size, axis)

        def join(flag, mine, theirs, axis=0):
            return jnp.where(
                flag == 0,
                jnp.concatenate([mine, theirs], axis=axis),
                jnp.concatenate([theirs, mine], axis=axis),
            )

        def exchange(array):
            return lax.all_to_all(
                array, AXES, split_axis=0, concat_axis=0, tiled=True, axis_index_groups=deal_groups
            )

        def deal(array):
            return exchange(gather_slots(dealing, array, BF16)).reshape(slots // 2, 2, block, half_width)

        order = jnp.arange(slots, dtype=jnp.int32)
        restore = jnp.sum(jnp.where(dealing[None, :] == order[:, None], order[None, :], 0), axis=1)

        qkv_sent = part(qkv_weight, core, 1)
        thoughts_core = flip(thoughts[0])
        tokens, thoughts_core = lax.optimization_barrier((tokens, thoughts_core))
        dealt = deal(tokens)
        kv_direct = cross(qkv_sent[1:])
        kv_partner = flip(kv_direct)
        biases_other = cross(qv_bias)
        near = jnp.where(core == side, thoughts[0], thoughts_core)
        far = cross(jnp.where(core == side, thoughts_core, thoughts[0]))
        latent_core = flip(latent_pos)
        latent = jnp.where(core == side, latent_pos, latent_core)[0]
        length = lengths[dealing[slot]]
        info = jnp.concatenate(
            [jnp.stack([core, length]).astype(jnp.int32), latent, jnp.stack([(group >> 1) & 1, group >> 2]).astype(jnp.int32)]
        )

        cot_dealt = gather_slots(dealing, cotangent, BF16)
        out_sent = part(out_weight, core, 1)
        thought_rows = join(side, near, far, axis=1).astype(F32)
        norms_in = jnp.stack([norm_gain[0], norm_shift[0]])
        norms_mid = jnp.stack([norm_gain[1], norm_shift[1], out_bias[0]])
        q_sent, out_sent, kv_direct, cot_dealt, thought_rows, biases_other, info, norms_in, norms_mid = (
            lax.optimization_barrier(
                (qkv_sent[:1], out_sent, kv_direct, cot_dealt, thought_rows, biases_other, info, norms_in, norms_mid)
            )
        )
        q_direct = cross(q_sent)
        qv_other = biases_other
        out_direct = cross(out_sent)
        cot_pieces = exchange(cot_dealt).reshape(slots // 2, 2, block, half_width)

        steps = rows // tile
        rowwise = spec((tile, width), lambda i, _: (i, 0))
        pieces_spec = spec((blocks, 2, block, half_width), lambda i, _: (i, 0, 0, 0))
        one, two, three = (spec((1, width, half_width), lambda i, _, place=place: (place, 0, 0)) for place in range(3))
        kv_specs = [whole(kv_direct.shape)] * 2
        q_specs = [whole(q_direct.shape)] * 2
        out_specs = [whole(out_weight.shape), whole(out_sent.shape), whole(out_sent.shape)]
        rows_bf, rows_f = like((rows, width), BF16), like((rows, width), F32)

        inputs, normed, keys_own, values_own = call(
            functools.partial(enter_kernel, tile, block), "enter", (steps,),
            [pieces_spec, whole((6, width)), whole((2, width)), whole((2, half_width)), whole((2, half_width)), two, three, *kv_specs],
            [rowwise] * 4, [rows_f, rows_bf, rows_bf, rows_bf],
        )(info, dealt, thought_rows, norms_in, qv_bias, qv_other,
          qkv_weight, qkv_weight, kv_direct, kv_partner)
        q_direct, keys_own, values_own, normed = lax.optimization_barrier((q_direct, keys_own, values_own, normed))
        q_partner = flip(q_direct)
        keys_other, values_other = flip(keys_own), flip(values_own)
        queries = call(
            queries_kernel, "queries", (steps,),
            [rowwise, whole((2, half_width)), whole((2, half_width)), one, *q_specs], rowwise, rows_bf,
        )(info, normed, qv_bias, qv_other, qkv_weight, q_direct, q_partner)
        queries, out_direct, cot_pieces = lax.optimization_barrier((queries, out_direct, cot_pieces))
        grad_mlp = call(
            functools.partial(cotangent_kernel, tile, block), "cotangent", (steps,), [pieces_spec], rowwise, rows_bf
        )(info, cot_pieces)
        queries, grad_mlp, keys_other, values_other = lax.optimization_barrier(
            (queries, grad_mlp, keys_other, values_other)
        )
        grad_far = cross(grad_mlp)
        out_partner = flip(out_direct)
        heads_out, lse = attend_forward(info, block, queries, keys_own, values_own, keys_other, values_other)
        heads_out, grad_far = lax.optimization_barrier((heads_out, grad_far))
        residual, normed_mlp = call(
            middle_kernel, "middle", (steps,),
            [rowwise, rowwise, whole((3, width)), *out_specs],
            [rowwise] * 2, [rows_f, rows_bf], [pltpu.VMEM((tile, width), F32)],
        )(info, heads_out, inputs, norms_mid,
          out_weight, out_direct, out_partner)
        normed_far = cross(normed_mlp)

        full = whole((rows, width))
        chunk = 2 * half_width

        def mlp_rows(normed_rows, grad_rows, dtype):
            units = hidden_half // 3
            by_row = spec((tile, width), lambda r, i, _: (r, 0))
            result = like((rows, width), dtype)
            return call(
                mlp_rows_kernel, "mlp_rows", (steps, 3),
                [by_row, by_row, spec((width, units), lambda r, i, _: (0, i)), spec((1, units), lambda r, i, _: (0, i)),
                 spec((units, width), lambda r, i, _: (i, 0))],
                [by_row, by_row, spec((units, tile), lambda r, i, _: (i, r)), spec((tile, units), lambda r, i, _: (r, i)),
                 spec((1, 1, units), lambda r, i, _: (r, 0, i))],
                [result, result, like((hidden_half, rows), BF16), like((rows, hidden_half), BF16),
                 like((steps, 1, hidden_half), F32)],
                [pltpu.VMEM((tile, width), F32)] * 2,
            )(info, normed_rows, grad_rows, fc_weight, fc_bias.reshape(1, hidden_half), proj_weight)

        mlp, back, active0, pre0, fcb0 = mlp_rows(normed_mlp, grad_mlp, F32)
        normed_far, mlp = lax.optimization_barrier((normed_far, mlp))
        mlp_sent, back_sent, active1, pre1, fcb1 = mlp_rows(normed_far, grad_far, BF16)
        back_far = cross(back_sent)
        quarter_spec = spec((half_width, 2 * chunk), lambda i, _: (0, i))
        by_unit = spec((rows, chunk), lambda i, _: (0, i))
        unit_rows = spec((chunk, rows), lambda i, _: (i, 0))
        mlp_keep, mlp_send = call(
            mlp_grads_kernel, "mlp_grads", (2,),
            [full] * 4 + [unit_rows] * 2 + [by_unit] * 2, [quarter_spec] * 2,
            [like((half_width, 4 * chunk), BF16)] * 2, [pltpu.VMEM((2, width, rows), BF16)],
        )(info, normed_mlp, normed_far, grad_mlp, grad_far, active0, active1, pre0, pre1)

        back_far, mlp_keep, mlp_send, mlp_sent = lax.optimization_barrier((back_far, mlp_keep, mlp_send, mlp_sent))
        mlp_far = cross(mlp_sent)
        near = (group >> 1) & 1
        half = half_width // 2
        upper = list(range(2, bits))
        levels = len(upper)
        flags = [(group >> link) & 1 for link in upper]
        sizes = [half >> (level + 1) for level in range(levels)]
        starts = [sum(flag * size for flag, size in zip(flags[:level], sizes)) for level in range(levels + 1)]

        def rows_sum(terms, start, size):
            total = 0.0
            for array, base in terms:
                total = total + lax.dynamic_slice_in_dim(array, base + start, size, 0).astype(F32)
            return total.astype(BF16)

        def section(level):
            if level == levels:
                return starts[level], sizes[-1]
            return starts[level] + (1 - flags[level]) * sizes[level], sizes[level]

        def widen(level, mine, theirs):
            return join(flags[level], mine, theirs)

        mlp_got = flip(mlp_send)
        grad_residual, grad_attn, grad_heads, small_mlp = call(
            back_kernel, "back", (steps,),
            [rowwise, rowwise, rowwise, rowwise, whole((1, width)), *out_specs],
            [rowwise, rowwise, rowwise, whole((4, width))],
            [rows_f, rows_bf, rows_bf, like((4, width), F32)],
        )(info, back, back_far, residual, grad_mlp, norm_gain[1:], out_weight, out_direct, out_partner)
        pairs = half_width // LANES
        grad_heads, mlp_got = lax.optimization_barrier((grad_heads, mlp_got))
        mlp_rows_kept = [(mlp_keep, near * half), (mlp_got, near * half)]
        mlp_rows_sent = [(mlp_keep, (1 - near) * half), (mlp_got, (1 - near) * half)]
        over_y = [rows_sum(mlp_rows_sent, *section(level)) for level in range(levels + 1)]
        grad_heads, *over_y = lax.optimization_barrier((grad_heads, *over_y))
        over_y[0] = flip(over_y[0], 1)

        def mlp_section(level):
            start, size = section(level)
            return rows_sum([*mlp_rows_kept, (over_y[level], -start)], start, size)

        def backward(first, grad):
            grad_q, grad_ko, grad_vo, grad_kx, grad_vx = attend_backward(
                info, block, first, pairs, queries, keys_own, values_own, keys_other, values_other, grad, heads_out, lse
            )
            return grad_q, grad_ko, grad_vo, grad_kx, grad_vx

        def with_far(grads, *ties):
            grad_q, grad_ko, grad_vo, grad_kx, grad_vx = grads
            far_k, far_v, *ties = lax.optimization_barrier((flip(grad_kx), flip(grad_vx), *ties))
            return (grad_q, grad_ko, far_k, grad_vo, far_v), ties

        other = backward(pairs, grad_heads)
        mlp_far, *tied = lax.optimization_barrier((mlp_far, *over_y, *other))
        over_y, other = tied[: levels + 1], tied[levels + 1 :]
        over_y[1] = flip(over_y[1], 1)
        block_pieces = call(
            functools.partial(block_kernel, tile, block), "block", (steps,),
            [rowwise, rowwise, rowwise, whole((1, width))], pieces_spec,
            like((slots // 2, 2, block, half_width), BF16),
        )(info, residual, mlp, mlp_far, out_bias[1:])
        other, (block_pieces,) = with_far(other, block_pieces)
        block_back = exchange(block_pieces.reshape(slots, block, half_width))

        def attention_grads(column, grads):
            shape = (half_width, 4 * half_width)
            return call(
                attention_grads_kernel, "attention_grads", (1,),
                [full, spec((rows, half_width), lambda i, _: (0, column)), full, *[whole((rows, half_width))] * 5],
                [whole(shape)] * 2, [like(shape, BF16)] * 2, [pltpu.VMEM((width, rows), BF16)],
            )(info, normed, heads_out, grad_attn, *grads)

        keep_other, send_other = attention_grads(1, other)
        keep_other, send_other, *over_y = lax.optimization_barrier((keep_other, send_other, *over_y))
        over_y[2:] = [flip(value, 1) for value in over_y[2:]]
        got_other = flip(send_other)
        mlp_stage = mlp_section(0)
        x_first, x_last = (
            rows_sum([(keep_other, place * half), (got_other, place * half)], 0, half) for place in (1 - near, near)
        )
        x_first, x_last, mlp_stage, grad_heads = lax.optimization_barrier((x_first, x_last, mlp_stage, grad_heads))
        x_first = cross(x_first)
        mlp_stage = flip(mlp_stage, upper[0])
        own = backward(0, grad_heads)
        x_first, x_last, mlp_stage, *tied = lax.optimization_barrier((x_first, x_last, mlp_stage, *over_y[2:], *own))
        over_y[2:], own = tied[: levels - 1], tied[levels - 1 :]
        x_last = cross(x_last)
        mlp_rows_kept.append((mlp_stage, -starts[1]))
        own, (mlp_stage,) = with_far(own, mlp_section(1))
        mlp_stage = flip(mlp_stage, upper[1])
        keep_own, send_own = attention_grads(0, own)
        block_out = gather_slots(restore, block_back, F32)
        keep_own, send_own, mlp_stage, x_last, block_out = lax.optimization_barrier(
            (keep_own, send_own, mlp_stage, x_last, block_out)
        )
        mlp_rows_kept.append((mlp_stage, -starts[2]))
        for level in range(2, levels):
            mlp_rows_kept.append((flip(mlp_section(level), upper[level]), -starts[level + 1]))
        mlp_piece = mlp_section(levels)
        for level in reversed(range(2, levels)):
            mlp_piece = widen(level, mlp_piece, flip(mlp_piece, upper[level]))
        mlp_piece, *own = lax.optimization_barrier((mlp_piece, *own))
        mlp_stage = flip(mlp_piece, upper[1])
        got_own = flip(send_own)
        half_rows = spec((tile, half_width), lambda i, _: (i, 0))
        input_pieces, small_attn = call(
            functools.partial(leave_kernel, tile, block), "leave", (steps,),
            [rowwise, rowwise, whole((1, width)), *[half_rows] * 10, whole(qkv_weight.shape), *kv_specs, *q_specs],
            [pieces_spec, whole((4, width))],
            [like((slots // 2, 2, block, half_width), BF16), like((4, width), F32)],
            [pltpu.VMEM((tile, width), F32)],
        )(info, inputs, grad_residual, norm_gain[:1], *own, *other, qkv_weight, kv_direct, kv_partner, q_direct, q_partner)
        input_pieces, small_attn, got_own, mlp_stage = lax.optimization_barrier(
            (input_pieces, small_attn, got_own, mlp_stage)
        )
        sent = rows_sum([(keep_own, (1 - near) * half), (got_own, (1 - near) * half), (x_first, 0)], 0, half)
        over_bit = flip(sent, 1)
        mlp_piece = widen(1, mlp_piece, mlp_stage)
        mlp_stage = flip(mlp_piece, upper[0])
        input_back = exchange(input_pieces.reshape(slots, block, half_width))

        def ordered(vectors):
            return join(side, vectors[:, :half_width], vectors[:, half_width:], axis=1)

        hidden = 2 * hidden_half
        fcb0 = jnp.sum(fcb0 + fcb1, axis=0)
        fcb = join(side, fcb0, jnp.zeros_like(fcb0), axis=1).reshape(hidden // width, width)
        small = jnp.concatenate([small_mlp, small_attn[:2], ordered(small_attn[2:]), fcb], axis=0)
        links = [flip, cross, *[functools.partial(flip, bit=bit) for bit in range(1, bits)]]

        def add_over(value):
            return value + links.pop(0)(value) if links else value

        small = add_over(small)
        over_bit, mlp_stage, small = lax.optimization_barrier((over_bit, mlp_stage, small))
        mlp_piece = widen(0, mlp_piece, mlp_stage)
        kept = [(keep_own, near * half), (got_own, near * half), (x_last, 0), (over_bit, 0)]
        for level in range(levels):
            stage = flip(rows_sum(kept, *section(level)), upper[level])
            if level == 0:
                mlp_over, mlp_core = flip(mlp_piece, 1), flip(mlp_piece)
            small = add_over(small)
            stage, small, input_back = lax.optimization_barrier((stage, small, input_back))
            kept.append((stage, -starts[level + 1]))
        piece = rows_sum(kept, *section(levels))
        for level in reversed(range(levels)):
            stage = flip(piece, upper[level])
            small = add_over(small)
            stage, small = lax.optimization_barrier((stage, small))
            piece = widen(level, piece, stage)
        while links:
            small = add_over(small)
        over, near_core = flip(piece, 1), flip(piece)
        mlp_over, mlp_core, piece = lax.optimization_barrier((mlp_over, mlp_core, piece))
        mlp_all = [mlp_piece, mlp_over, mlp_core, flip(mlp_over)]
        input_grad = gather_slots(restore, input_back, F32)
        fc_grad, proj_grad = call(
            finish_mlp_kernel, "finish_mlp", (2,), [spec((half, 2 * chunk), lambda i, _: (0, i))] * 4,
            [spec((width, chunk), lambda i, _: (0, i)), spec((chunk, width), lambda i, _: (i, 0))],
            [like(fc_weight.shape, F32), like(proj_weight.shape, F32)],
        )(info, *mlp_all)
        over, fc_grad, proj_grad, input_grad, small = lax.optimization_barrier((over, fc_grad, proj_grad, input_grad, small))
        qkv_grad, out_grad = call(
            finish_attention_kernel, "finish_attention", (1,), [whole((half, 2 * chunk))] * 4,
            [whole(qkv_weight.shape), whole(out_weight.shape)],
            [like(qkv_weight.shape, F32), like(out_weight.shape, F32)],
        )(info, piece, over, near_core, flip(over))

        gain_mlp, shift_mlp, bias_mlp, bias_attn, gain_attn, shift_attn = (small[i] for i in range(6))
        return (
            block_out,
            input_grad,
            qkv_grad,
            part(small[6:8], side, 1),
            out_grad,
            jnp.stack([bias_attn, bias_mlp]),
            fc_grad,
            part(small[8:].reshape(hidden), side),
            proj_grad,
            jnp.stack([gain_attn, gain_mlp]),
            jnp.stack([shift_attn, shift_mlp]),
        )

    return jax.shard_map(
        body,
        mesh=mesh,
        in_specs=(
            P(None, "dp", "tensor"),
            P(None, "dp", "tensor"),
            P("dp", None, "tensor"),
            P("dp", None),
            P(),
            P(),
            P(None, None, "tensor"),
            P(None, "tensor"),
            P("tensor", None),
            P(),
            P(None, "tensor"),
            P("tensor"),
            P("tensor", None),
            P(),
            P(),
        ),
        out_specs=(
            P(None, "dp", "tensor"),
            P(None, "dp", "tensor"),
            P(None, None, "tensor"),
            P(None, "tensor"),
            P("tensor", None),
            P(),
            P(None, "tensor"),
            P("tensor"),
            P("tensor", None),
            P(),
            P(),
        ),
        check_vma=False,
    )
```

```python
import functools

import jax
import jax.numpy as jnp
from jax import lax
from jax.experimental import pallas as pl
from jax.experimental.pallas import tpu as pltpu
from jax.sharding import PartitionSpec as P

HEAD_DIM = 64
LANES = 128
AXES = ("dp", "tensor")
SCALE = HEAD_DIM ** (-0.5)
MASKED = -1e30
BF16 = jnp.bfloat16
F32 = jnp.float32


def dot_nn(left, right):
    return lax.dot_general(left, right, (((1,), (0,)), ((), ())), preferred_element_type=F32)


def dot_nt(left, right):
    return lax.dot_general(left, right, (((1,), (1,)), ((), ())), preferred_element_type=F32)


def dot_tn(left, right):
    return lax.dot_general(left, right, (((0,), (0,)), ((), ())), preferred_element_type=F32)


def own_mask(tile, start, core, length, block):
    key = lax.broadcasted_iota(jnp.int32, (tile, tile), 0)
    query = lax.broadcasted_iota(jnp.int32, (tile, tile), 1)
    key_row = start + key
    key_pos = (2 * (key_row // block) + core) * block + key_row % block
    return (key <= query) & (key_pos < length)


def other_mask(tile, start, core, length, block):
    key = lax.broadcasted_iota(jnp.int32, (tile, tile), 0)
    query = lax.broadcasted_iota(jnp.int32, (tile, tile), 1)
    key_row = start + key
    key_pos = (2 * (key_row // block) + 1 - core) * block + key_row % block
    return (key // block <= query // block - (1 - core)) & (key_pos < length)


def attend_forward_kernel(tile, block, info, q_ref, ko_ref, vo_ref, kx_ref, vx_ref, out_ref, lse_ref):
    core, length = info[0], info[1]
    rows = q_ref.shape[0]
    lane = lax.broadcasted_iota(jnp.int32, (1, LANES), 1)
    vo_t = vo_ref[...].T
    vx_t = vx_ref[...].T
    for start in range(0, rows, tile):
        stop = start + tile
        mask_own = own_mask(tile, start, core, length, block)
        mask_other = other_mask(tile, start, core, length, block)
        query = q_ref[start:stop, :] * jnp.asarray(SCALE, BF16)
        outs = []
        for half in range(2):
            picked = jnp.where(lane // HEAD_DIM == half, query, jnp.zeros_like(query))
            s_own = dot_nt(ko_ref[:stop, :], picked)
            s_other = dot_nt(kx_ref[:stop, :], picked)
            d_own = jnp.where(mask_own, s_own[start:], MASKED)
            d_other = jnp.where(mask_other, s_other[start:], MASKED)
            if start:
                s_own = jnp.concatenate([s_own[:start], d_own], axis=0)
                s_other = jnp.concatenate([s_other[:start], d_other], axis=0)
            else:
                s_own, s_other = d_own, d_other
            top = jnp.maximum(
                jnp.max(s_own, axis=0, keepdims=True), jnp.max(s_other, axis=0, keepdims=True)
            )
            e_own = jnp.exp(s_own - top)
            e_other = jnp.exp(s_other - top)
            total = jnp.sum(e_own, axis=0, keepdims=True) + jnp.sum(e_other, axis=0, keepdims=True)
            lanes = slice(half * HEAD_DIM, (half + 1) * HEAD_DIM)
            mixed = dot_nn(vo_t[lanes, :stop], e_own.astype(BF16)) + dot_nn(
                vx_t[lanes, :stop], e_other.astype(BF16)
            )
            outs.append(mixed / total)
            lse_ref[0, half : half + 1, start:stop] = top + jnp.log(total)
        out_ref[start:stop, :] = jnp.concatenate(outs, axis=0).T.astype(BF16)


def attend_backward_kernel(
    tile, block, info, q_ref, ko_ref, vo_ref, kx_ref, vx_ref, go_ref, out_ref, lse_ref,
    dq_ref, dko_ref, dvo_ref, dkx_ref, dvx_ref, ako, avo, akx, avx,
):
    core, length = info[0], info[1]
    rows = q_ref.shape[0]
    lane = lax.broadcasted_iota(jnp.int32, (1, LANES), 1)
    ko_t = ko_ref[...].T
    kx_t = kx_ref[...].T
    for acc in (ako, avo, akx, avx):
        acc[...] = jnp.zeros_like(acc)
    for start in range(0, rows, tile):
        stop = start + tile
        mask_own = own_mask(tile, start, core, length, block)
        mask_other = other_mask(tile, start, core, length, block)
        query = q_ref[start:stop, :] * jnp.asarray(SCALE, BF16)
        grad = go_ref[start:stop, :]
        product = grad.astype(F32) * out_ref[start:stop, :].astype(F32)
        parts = []
        for half in range(2):
            mine = lane // HEAD_DIM == half
            picked = jnp.where(mine, query, jnp.zeros_like(query))
            grad_half = jnp.where(mine, grad, jnp.zeros_like(grad))
            pick = jnp.broadcast_to(jnp.where(mine, 1.0, 0.0).astype(F32), (8, LANES))
            inner = lax.dot_general(
                pick, product, (((1,), (1,)), ((), ())),
                precision=lax.Precision.HIGHEST, preferred_element_type=F32,
            )[:1]
            lse = lse_ref[0, half : half + 1, start:stop]
            lanes = slice(half * HEAD_DIM, (half + 1) * HEAD_DIM)
            part = jnp.zeros((HEAD_DIM, tile), F32)
            for key_ref, value_ref, key_t, mask, acc_k, acc_v in (
                (ko_ref, vo_ref, ko_t, mask_own, ako, avo),
                (kx_ref, vx_ref, kx_t, mask_other, akx, avx),
            ):
                prob = jnp.exp(dot_nt(key_ref[:stop, :], picked) - lse)
                last = jnp.where(mask, prob[start:], 0.0)
                prob = jnp.concatenate([prob[:start], last], axis=0) if start else last
                grad_prob = dot_nt(value_ref[:stop, :], grad_half)
                grad_score = (prob * (grad_prob - inner)).astype(BF16)
                acc_v[:stop, :] += dot_nn(prob.astype(BF16), grad_half)
                acc_k[:stop, :] += dot_nn(grad_score, picked)
                part = part + dot_nn(key_t[lanes, :stop], grad_score)
            parts.append(part)
        dq_ref[start:stop, :] = (jnp.concatenate(parts, axis=0) * SCALE).T.astype(BF16)
    for acc, ref in ((ako, dko_ref), (avo, dvo_ref), (akx, dkx_ref), (avx, dvx_ref)):
        ref[...] = acc[...].astype(ref.dtype)


def attend_forward(info, block, queries, keys_own, values_own, keys_other, values_other):
    rows, width = queries.shape
    pairs = width // LANES
    tile = min(256, rows)
    column = pl.BlockSpec((rows, LANES), lambda pair, info: (0, pair))
    return pl.pallas_call(
        functools.partial(attend_forward_kernel, tile, block),
        grid_spec=pltpu.PrefetchScalarGridSpec(
            num_scalar_prefetch=1,
            grid=(pairs,),
            in_specs=[column] * 5,
            out_specs=[column, pl.BlockSpec((1, 2, rows), lambda pair, info: (pair, 0, 0))],
        ),
        out_shape=[
            jax.ShapeDtypeStruct((rows, width), BF16),
            jax.ShapeDtypeStruct((pairs, 2, rows), F32),
        ],
        name="attend_forward",
    )(info, queries, keys_own, values_own, keys_other, values_other)


def attend_backward(info, block, first, pairs, queries, keys_own, values_own, keys_other, values_other, grad_heads,
                    heads_out, lse):
    rows = queries.shape[0]
    tile = min(256, rows)
    column = pl.BlockSpec((rows, LANES), lambda pair, info: (0, first + pair))
    result = pl.BlockSpec((rows, LANES), lambda pair, info: (0, pair))
    dtypes = (BF16, F32, F32, BF16, BF16)
    return pl.pallas_call(
        functools.partial(attend_backward_kernel, tile, block),
        grid_spec=pltpu.PrefetchScalarGridSpec(
            num_scalar_prefetch=1,
            grid=(pairs,),
            in_specs=[column] * 7 + [pl.BlockSpec((1, 2, rows), lambda pair, info: (first + pair, 0, 0))],
            out_specs=[result] * 5,
            scratch_shapes=[pltpu.VMEM((rows, LANES), F32)] * 4,
        ),
        out_shape=[jax.ShapeDtypeStruct((rows, pairs * LANES), dtype) for dtype in dtypes],
        name="attend_backward",
    )(info, queries, keys_own, values_own, keys_other, values_other, grad_heads, heads_out, lse)


HALF = 384


def spec(shape, index):
    return pl.BlockSpec(shape, index)


def whole(shape):
    zeros = (0,) * len(shape)
    return pl.BlockSpec(shape, lambda *_: zeros)


def call(kernel, name, grid, in_specs, out_specs, out_shape, scratch=()):
    return pl.pallas_call(
        kernel,
        grid_spec=pltpu.PrefetchScalarGridSpec(
            num_scalar_prefetch=1, grid=grid, in_specs=in_specs, out_specs=out_specs, scratch_shapes=list(scratch)
        ),
        out_shape=out_shape,
        name=name,
    )


def like(shape, dtype):
    return jax.ShapeDtypeStruct(shape, dtype)


def gather_slots(index, array, dtype):
    slots, block, width = array.shape
    steps = 4
    per = slots // steps

    def kernel(index_ref, array_ref, out_ref):
        first = pl.program_id(0) * per

        def copy(i, carry):
            out_ref[i] = array_ref[index_ref[first + i]].astype(dtype)
            return carry

        lax.fori_loop(0, per, copy, 0, unroll=min(per, 4))

    return call(
        kernel, "gather_slots", (steps,), [whole(array.shape)],
        spec((per, block, width), lambda i, _: (i, 0, 0)), like(array.shape, dtype),
    )(index, array)


def statistics(features):
    mean = jnp.mean(features, axis=-1, keepdims=True)
    centred = features - mean
    variance = jnp.mean(centred * centred, axis=-1, keepdims=True)
    scale = lax.rsqrt(variance + 1e-05)
    return centred * scale, scale


def norm_rows_back(grad, gain, xhat, scale):
    scaled = grad * gain
    return scale * (
        scaled
        - jnp.mean(scaled, axis=-1, keepdims=True)
        - xhat * jnp.mean(scaled * xhat, axis=-1, keepdims=True)
    )


def sum_rows(value):
    return jnp.sum(value, axis=0, keepdims=True)


def row_positions(tile, block, core):
    row = pl.program_id(0) * tile + lax.broadcasted_iota(jnp.int32, (tile, 1), 0)
    return (2 * (row // block) + core) * block + row % block


def rows_of(pieces_ref, tile):
    halves = [pieces_ref[:, side].astype(F32).reshape(tile, HALF) for side in range(2)]
    return jnp.concatenate(halves, axis=1)


def cols(index):
    return pl.ds(pl.multiple_of(index * HALF, LANES), HALF)


def rows_at(index):
    return pl.ds(pl.multiple_of(index * HALF, LANES), HALF)


ROOT = 0.7978845608028654
CUBE = 0.044715


def gelu_and_slope(value):
    square = value * value
    turn = jnp.tanh(ROOT * value * (1.0 + CUBE * square))
    slope = 0.5 * (1.0 + turn) + 0.5 * value * (1.0 - turn * turn) * ROOT * (1.0 + 3.0 * CUBE * square)
    return 0.5 * value * (1.0 + turn), slope


def enter_kernel(tile, block, info, pieces, thoughts, norms, bias_own, bias_other, own_k, own_v, direct, partner,
                 inputs_ref, normed_ref, k_ref, v_ref):
    core = info[0]
    position = row_positions(tile, block, core)
    features = rows_of(pieces, tile)
    for index in range(6):
        features = jnp.where(position == info[2 + index], thoughts[index : index + 1, :], features)
    inputs_ref[...] = features
    xhat, _ = statistics(features)
    normed = (xhat * norms[0:1, :] + norms[1:2, :]).astype(BF16)
    normed_ref[...] = normed
    project(core, normed_ref, own_k[0], direct[0], partner[0], None, None, k_ref)
    project(core, normed_ref, own_v[0], direct[1], partner[1], bias_own[1:2, :], bias_other[1:2, :], v_ref)


def project(core, normed, own, direct, partner, bias_own, bias_other, ref):
    mine = dot_nn(normed[...], own)
    theirs = dot_nn(normed[:, cols(core)], direct) + dot_nn(normed[:, cols(1 - core)], partner)
    if bias_own is not None:
        mine = mine + bias_own
        theirs = theirs + bias_other
    ref[:, :HALF] = mine.astype(BF16)
    ref[:, HALF:] = theirs.astype(BF16)


def queries_kernel(info, normed, bias_own, bias_other, own, direct, partner, q_ref):
    project(info[0], normed, own[0], direct[0], partner[0], bias_own[0:1, :], bias_other[0:1, :], q_ref)


def cotangent_kernel(tile, block, info, pieces, grad_ref):
    position = row_positions(tile, block, info[0])
    grad_ref[...] = jnp.where(position < info[1], rows_of(pieces, tile), 0.0).astype(BF16)


def middle_kernel(info, heads, inputs, norms, own, direct, partner, residual_ref, normed_ref, mixed):
    core = info[0]
    mixed[...] = dot_nn(heads[:, :HALF], own[...]) + norms[2:3, :]
    mixed[:, cols(core)] += dot_nn(heads[:, HALF:], direct[...])
    mixed[:, cols(1 - core)] += dot_nn(heads[:, HALF:], partner[...])
    residual = inputs[...] + mixed[...]
    residual_ref[...] = residual
    xhat, _ = statistics(residual)
    normed_ref[...] = (xhat * norms[0:1, :] + norms[1:2, :]).astype(BF16)


def mlp_rows_kernel(info, normed, grad, fc, bias, proj, mlp_ref, back_ref, active_t_ref, pre_ref, fcb_ref, mlp_sum, back_sum):
    step = pl.program_id(1)
    active, slope = gelu_and_slope(dot_nn(normed[...], fc[...]) + bias[...])
    active = active.astype(BF16)
    active_t_ref[...] = active.T
    grad_pre = (dot_nt(grad[...], proj[...]) * slope).astype(BF16)
    pre_ref[...] = grad_pre
    fcb_ref[0] = sum_rows(grad_pre.astype(F32))
    mlp = dot_nn(active, proj[...])
    back = dot_nt(grad_pre, fc[...])

    @pl.when(step == 0)
    def _():
        mlp_sum[...] = mlp
        back_sum[...] = back

    @pl.when((step > 0) & (step < pl.num_programs(1) - 1))
    def _():
        mlp_sum[...] += mlp
        back_sum[...] += back

    @pl.when(step == pl.num_programs(1) - 1)
    def _():
        mlp_ref[...] = (mlp_sum[...] + mlp).astype(mlp_ref.dtype)
        back_ref[...] = (back_sum[...] + back).astype(back_ref.dtype)


def mlp_grads_kernel(info, normed0, normed1, grad0, grad1, active0, active1, pre0, pre1, keep, send, normed_t):
    core = info[0]

    @pl.when(pl.program_id(0) == 0)
    def _():
        normed_t[0] = normed0[...].T
        normed_t[1] = normed1[...].T

    for index, ref in ((core, keep), (1 - core, send)):
        fc = dot_nn(normed_t[0, rows_at(index), :], pre0[...]) + dot_nn(normed_t[1, rows_at(index), :], pre1[...])
        proj = dot_nn(active0[rows_at(index), :], grad0[...]) + dot_nn(active1[rows_at(index), :], grad1[...])
        ref[:, : 2 * HALF] = fc.astype(BF16)
        ref[:, 2 * HALF :] = proj.astype(BF16)


def back_kernel(info, back, back_far, residual, grad, norms, own, direct, partner,
                grad_residual_ref, grad_attn_ref, grad_heads_ref, small_ref):
    core = info[0]
    xhat, scale = statistics(residual[...])
    incoming = back[...] + back_far[...].astype(F32)
    grad_out = grad[...].astype(F32)
    grad_residual = grad_out + norm_rows_back(incoming, norms[0:1, :], xhat, scale)
    grad_residual_ref[...] = grad_residual
    grad_attn = grad_residual.astype(BF16)
    grad_attn_ref[...] = grad_attn
    grad_heads_ref[:, :HALF] = dot_nt(grad_attn, own[...]).astype(BF16)
    theirs = dot_nt(grad_attn_ref[:, cols(core)], direct[...])
    theirs = theirs + dot_nt(grad_attn_ref[:, cols(1 - core)], partner[...])
    grad_heads_ref[:, HALF:] = theirs.astype(BF16)
    sums = jnp.concatenate(
        [sum_rows(incoming * xhat), sum_rows(incoming), sum_rows(grad_out), sum_rows(grad_attn.astype(F32))], axis=0
    )

    @pl.when(pl.program_id(0) == 0)
    def _():
        small_ref[...] = sums

    @pl.when(pl.program_id(0) > 0)
    def _():
        small_ref[...] += sums


def block_kernel(tile, block, info, residual, mlp, mlp_far, bias, block_ref):
    position = row_positions(tile, block, info[0])
    result = residual[...] + (mlp[...] + mlp_far[...].astype(F32) + bias[...])
    result = jnp.where(position < info[1], result, 0.0)
    for side in range(2):
        half = result[:, side * HALF : (side + 1) * HALF].reshape(tile // block, block, HALF)
        block_ref[:, side] = half.astype(BF16)


def key_value_grads(dk, dk_far, dv, dv_far):
    return (
        (dk[...] + dk_far[...].astype(F32)).astype(BF16),
        (dv[...] + dv_far[...].astype(F32)).astype(BF16),
    )


def attention_grads_kernel(info, normed, heads, grad_attn, dq, dk, dk_far, dv, dv_far, keep, send, normed_t):
    core = info[0]
    normed_t[...] = normed[...].T
    grads = (dq[...], *key_value_grads(dk, dk_far, dv, dv_far))
    heads_t = heads[...].T
    for index, ref in ((1 - core, send), (core, keep)):
        left = normed_t[rows_at(index), :]
        for place, grad in enumerate(grads):
            ref[:, place * HALF : (place + 1) * HALF] = dot_nn(left, grad).astype(BF16)
        ref[:, 3 * HALF :] = dot_nn(heads_t, grad_attn[:, cols(index)]).astype(BF16)


def leave_kernel(tile, block, info, inputs, grad_residual, norms, dq0, dk0, dk_far0, dv0, dv_far0,
                 dq1, dk1, dk_far1, dv1, dv_far1, own, direct, partner, direct_q, partner_q, pieces_ref, small_ref, back):
    core = info[0]
    mine = (dq0[...], *key_value_grads(dk0, dk_far0, dv0, dv_far0))
    theirs = (dq1[...], *key_value_grads(dk1, dk_far1, dv1, dv_far1))
    back[...] = sum(dot_nt(grad, own[index]) for index, grad in enumerate(mine))
    far_q, far_k, far_v = theirs
    back[:, cols(core)] += dot_nt(far_q, direct_q[0]) + dot_nt(far_k, direct[0]) + dot_nt(far_v, direct[1])
    back[:, cols(1 - core)] += dot_nt(far_q, partner_q[0]) + dot_nt(far_k, partner[0]) + dot_nt(far_v, partner[1])
    incoming = back[...]
    xhat, scale = statistics(inputs[...])
    result = grad_residual[...] + norm_rows_back(incoming, norms[0:1, :], xhat, scale)
    blocks = tile // block
    for side in range(2):
        pieces_ref[:, side] = result[:, side * HALF : (side + 1) * HALF].reshape(blocks, block, HALF).astype(BF16)
    biases = [
        jnp.concatenate([sum_rows(mine[place].astype(F32)), sum_rows(theirs[place].astype(F32))], axis=1)
        for place in (0, 2)
    ]
    sums = jnp.concatenate([sum_rows(incoming * xhat), sum_rows(incoming), *biases], axis=0)

    @pl.when(pl.program_id(0) == 0)
    def _():
        small_ref[...] = sums

    @pl.when(pl.program_id(0) > 0)
    def _():
        small_ref[...] += sums


def finish_rows(info, refs):
    core, near = info[0], info[8]
    size = refs[0].shape[0]
    for index, ref in enumerate(refs):
        base = (core if index < 2 else 1 - core) * HALF
        yield base, (near if index % 2 == 0 else 1 - near) * size, ref


def finish_mlp_kernel(info, *refs):
    fc_ref, proj_ref = refs[4:]
    for base, offset, ref in finish_rows(info, refs[:4]):
        rows = pl.ds(pl.multiple_of(base + offset, 64), ref.shape[0])
        fc_ref[rows, :] = ref[:, : 2 * HALF].astype(F32)
        proj_ref[rows, :] = ref[:, 2 * HALF :].astype(F32)


def finish_attention_kernel(info, *refs):
    qkv_ref, out_ref = refs[4:]
    for base, offset, ref in finish_rows(info, refs[:4]):
        rows = pl.ds(pl.multiple_of(base + offset, 64), ref.shape[0])
        for place in range(3):
            qkv_ref[place, rows, :] = ref[:, place * HALF : (place + 1) * HALF].astype(F32)
        heads = pl.ds(pl.multiple_of(offset, 64), ref.shape[0])
        out_ref[heads, pl.ds(pl.multiple_of(base, LANES), HALF)] = ref[:, 3 * HALF :].astype(F32)


def solution(mesh):
    groups = mesh.shape["dp"]
    bits = groups.bit_length() - 1
    assert groups == 1 << bits and mesh.shape["tensor"] == 2

    def pairs_of(change):
        table = []
        for group in range(groups):
            for side in range(2):
                to_group, to_side = change(group, side)
                table.append((group * 2 + side, to_group * 2 + to_side))
        return table

    tensor_pairs = pairs_of(lambda group, side: (group, 1 - side))
    bit_pairs = [pairs_of(lambda group, side, k=k: (group ^ (1 << k), side)) for k in range(bits)]
    deal_groups = [
        [group * 2 + side for group in range(core, groups, 2) for side in range(2)] for core in range(2)
    ]

    def body(
        tokens, cotangent, thoughts, latent_pos, lengths, dealing, qkv_weight, qv_bias, out_weight,
        out_bias, fc_weight, fc_bias, proj_weight, norm_gain, norm_shift,
    ):
        group = lax.axis_index("dp")
        side = lax.axis_index("tensor")
        core = group % 2
        slot = group - core + side
        slots, block, half_width = tokens.shape
        width = 2 * half_width
        rows = slots * block // 2
        hidden_half = fc_weight.shape[1]
        assert half_width == HALF and hidden_half == 4 * HALF
        tile = 256
        blocks = tile // block

        def cross(value):
            return lax.ppermute(value, AXES, tensor_pairs)

        def flip(value, bit=0):
            return lax.ppermute(value, AXES, bit_pairs[bit])

        def part(value, index, axis=0):
            size = value.shape[axis] // 2
            return lax.dynamic_slice_in_dim(value, index * size, size, axis)

        def join(flag, mine, theirs, axis=0):
            return jnp.where(
                flag == 0,
                jnp.concatenate([mine, theirs], axis=axis),
                jnp.concatenate([theirs, mine], axis=axis),
            )

        def exchange(array):
            return lax.all_to_all(
                array, AXES, split_axis=0, concat_axis=0, tiled=True, axis_index_groups=deal_groups
            )

        def deal(array):
            return exchange(gather_slots(dealing, array, BF16)).reshape(slots // 2, 2, block, half_width)

        order = jnp.arange(slots, dtype=jnp.int32)
        restore = jnp.sum(jnp.where(dealing[None, :] == order[:, None], order[None, :], 0), axis=1)

        qkv_sent = part(qkv_weight, core, 1)
        thoughts_core = flip(thoughts[0])
        tokens, thoughts_core = lax.optimization_barrier((tokens, thoughts_core))
        dealt = deal(tokens)
        kv_direct = cross(qkv_sent[1:])
        kv_partner = flip(kv_direct)
        biases_other = cross(qv_bias)
        near = jnp.where(core == side, thoughts[0], thoughts_core)
        far = cross(jnp.where(core == side, thoughts_core, thoughts[0]))
        latent_core = flip(latent_pos)
        latent = jnp.where(core == side, latent_pos, latent_core)[0]
        length = lengths[dealing[slot]]
        info = jnp.concatenate(
            [jnp.stack([core, length]).astype(jnp.int32), latent, jnp.stack([(group >> 1) & 1, group >> 2]).astype(jnp.int32)]
        )

        cot_dealt = gather_slots(dealing, cotangent, BF16)
        out_sent = part(out_weight, core, 1)
        thought_rows = join(side, near, far, axis=1).astype(F32)
        norms_in = jnp.stack([norm_gain[0], norm_shift[0]])
        norms_mid = jnp.stack([norm_gain[1], norm_shift[1], out_bias[0]])
        q_sent, out_sent, kv_direct, cot_dealt, thought_rows, biases_other, info, norms_in, norms_mid = (
            lax.optimization_barrier(
                (qkv_sent[:1], out_sent, kv_direct, cot_dealt, thought_rows, biases_other, info, norms_in, norms_mid)
            )
        )
        q_direct = cross(q_sent)
        qv_other = biases_other
        out_direct = cross(out_sent)
        cot_pieces = exchange(cot_dealt).reshape(slots // 2, 2, block, half_width)

        steps = rows // tile
        rowwise = spec((tile, width), lambda i, _: (i, 0))
        pieces_spec = spec((blocks, 2, block, half_width), lambda i, _: (i, 0, 0, 0))
        one, two, three = (spec((1, width, half_width), lambda i, _, place=place: (place, 0, 0)) for place in range(3))
        kv_specs = [whole(kv_direct.shape)] * 2
        q_specs = [whole(q_direct.shape)] * 2
        out_specs = [whole(out_weight.shape), whole(out_sent.shape), whole(out_sent.shape)]
        rows_bf, rows_f = like((rows, width), BF16), like((rows, width), F32)

        inputs, normed, keys_own, values_own = call(
            functools.partial(enter_kernel, tile, block), "enter", (steps,),
            [pieces_spec, whole((6, width)), whole((2, width)), whole((2, half_width)), whole((2, half_width)), two, three, *kv_specs],
            [rowwise] * 4, [rows_f, rows_bf, rows_bf, rows_bf],
        )(info, dealt, thought_rows, norms_in, qv_bias, qv_other,
          qkv_weight, qkv_weight, kv_direct, kv_partner)
        q_direct, keys_own, values_own, normed = lax.optimization_barrier((q_direct, keys_own, values_own, normed))
        q_partner = flip(q_direct)
        keys_other, values_other = flip(keys_own), flip(values_own)
        queries = call(
            queries_kernel, "queries", (steps,),
            [rowwise, whole((2, half_width)), whole((2, half_width)), one, *q_specs], rowwise, rows_bf,
        )(info, normed, qv_bias, qv_other, qkv_weight, q_direct, q_partner)
        queries, out_direct, cot_pieces = lax.optimization_barrier((queries, out_direct, cot_pieces))
        grad_mlp = call(
            functools.partial(cotangent_kernel, tile, block), "cotangent", (steps,), [pieces_spec], rowwise, rows_bf
        )(info, cot_pieces)
        queries, grad_mlp, keys_other, values_other = lax.optimization_barrier(
            (queries, grad_mlp, keys_other, values_other)
        )
        grad_far = cross(grad_mlp)
        out_partner = flip(out_direct)
        heads_out, lse = attend_forward(info, block, queries, keys_own, values_own, keys_other, values_other)
        heads_out, grad_far = lax.optimization_barrier((heads_out, grad_far))
        residual, normed_mlp = call(
            middle_kernel, "middle", (steps,),
            [rowwise, rowwise, whole((3, width)), *out_specs],
            [rowwise] * 2, [rows_f, rows_bf], [pltpu.VMEM((tile, width), F32)],
        )(info, heads_out, inputs, norms_mid,
          out_weight, out_direct, out_partner)
        normed_far = cross(normed_mlp)

        full = whole((rows, width))
        chunk = 2 * half_width

        def mlp_rows(normed_rows, grad_rows, dtype):
            units = hidden_half // 3
            by_row = spec((tile, width), lambda r, i, _: (r, 0))
            result = like((rows, width), dtype)
            return call(
                mlp_rows_kernel, "mlp_rows", (steps, 3),
                [by_row, by_row, spec((width, units), lambda r, i, _: (0, i)), spec((1, units), lambda r, i, _: (0, i)),
                 spec((units, width), lambda r, i, _: (i, 0))],
                [by_row, by_row, spec((units, tile), lambda r, i, _: (i, r)), spec((tile, units), lambda r, i, _: (r, i)),
                 spec((1, 1, units), lambda r, i, _: (r, 0, i))],
                [result, result, like((hidden_half, rows), BF16), like((rows, hidden_half), BF16),
                 like((steps, 1, hidden_half), F32)],
                [pltpu.VMEM((tile, width), F32)] * 2,
            )(info, normed_rows, grad_rows, fc_weight, fc_bias.reshape(1, hidden_half), proj_weight)

        mlp, back, active0, pre0, fcb0 = mlp_rows(normed_mlp, grad_mlp, F32)
        normed_far, mlp = lax.optimization_barrier((normed_far, mlp))
        mlp_sent, back_sent, active1, pre1, fcb1 = mlp_rows(normed_far, grad_far, BF16)
        back_far = cross(back_sent)
        quarter_spec = spec((half_width, 2 * chunk), lambda i, _: (0, i))
        by_unit = spec((rows, chunk), lambda i, _: (0, i))
        unit_rows = spec((chunk, rows), lambda i, _: (i, 0))
        mlp_keep, mlp_send = call(
            mlp_grads_kernel, "mlp_grads", (2,),
            [full] * 4 + [unit_rows] * 2 + [by_unit] * 2, [quarter_spec] * 2,
            [like((half_width, 4 * chunk), BF16)] * 2, [pltpu.VMEM((2, width, rows), BF16)],
        )(info, normed_mlp, normed_far, grad_mlp, grad_far, active0, active1, pre0, pre1)

        back_far, mlp_keep, mlp_send, mlp_sent = lax.optimization_barrier((back_far, mlp_keep, mlp_send, mlp_sent))
        mlp_far = cross(mlp_sent)
        near = (group >> 1) & 1
        half = half_width // 2
        upper = list(range(2, bits))
        levels = len(upper)
        flags = [(group >> link) & 1 for link in upper]
        sizes = [half >> (level + 1) for level in range(levels)]
        starts = [sum(flag * size for flag, size in zip(flags[:level], sizes)) for level in range(levels + 1)]

        def rows_sum(terms, start, size):
            total = 0.0
            for array, base in terms:
                total = total + lax.dynamic_slice_in_dim(array, base + start, size, 0).astype(F32)
            return total.astype(BF16)

        def section(level):
            if level == levels:
                return starts[level], sizes[-1]
            return starts[level] + (1 - flags[level]) * sizes[level], sizes[level]

        def widen(level, mine, theirs):
            return join(flags[level], mine, theirs)

        mlp_got = flip(mlp_send)
        grad_residual, grad_attn, grad_heads, small_mlp = call(
            back_kernel, "back", (steps,),
            [rowwise, rowwise, rowwise, rowwise, whole((1, width)), *out_specs],
            [rowwise, rowwise, rowwise, whole((4, width))],
            [rows_f, rows_bf, rows_bf, like((4, width), F32)],
        )(info, back, back_far, residual, grad_mlp, norm_gain[1:], out_weight, out_direct, out_partner)
        pairs = half_width // LANES
        grad_heads, mlp_got = lax.optimization_barrier((grad_heads, mlp_got))
        mlp_rows_kept = [(mlp_keep, near * half), (mlp_got, near * half)]
        mlp_rows_sent = [(mlp_keep, (1 - near) * half), (mlp_got, (1 - near) * half)]
        over_y = [rows_sum(mlp_rows_sent, *section(level)) for level in range(levels + 1)]
        grad_heads, *over_y = lax.optimization_barrier((grad_heads, *over_y))
        over_y[0] = flip(over_y[0], 1)

        def mlp_section(level):
            start, size = section(level)
            return rows_sum([*mlp_rows_kept, (over_y[level], -start)], start, size)

        def backward(first, grad):
            grad_q, grad_ko, grad_vo, grad_kx, grad_vx = attend_backward(
                info, block, first, pairs, queries, keys_own, values_own, keys_other, values_other, grad, heads_out, lse
            )
            return grad_q, grad_ko, grad_vo, grad_kx, grad_vx

        def with_far(grads, *ties):
            grad_q, grad_ko, grad_vo, grad_kx, grad_vx = grads
            far_k, far_v, *ties = lax.optimization_barrier((flip(grad_kx), flip(grad_vx), *ties))
            return (grad_q, grad_ko, far_k, grad_vo, far_v), ties

        other = backward(pairs, grad_heads)
        mlp_far, *tied = lax.optimization_barrier((mlp_far, *over_y, *other))
        over_y, other = tied[: levels + 1], tied[levels + 1 :]
        over_y[1] = flip(over_y[1], 1)
        block_pieces = call(
            functools.partial(block_kernel, tile, block), "block", (steps,),
            [rowwise, rowwise, rowwise, whole((1, width))], pieces_spec,
            like((slots // 2, 2, block, half_width), BF16),
        )(info, residual, mlp, mlp_far, out_bias[1:])
        other, (block_pieces,) = with_far(other, block_pieces)
        block_back = exchange(block_pieces.reshape(slots, block, half_width))

        def attention_grads(column, grads):
            shape = (half_width, 4 * half_width)
            return call(
                attention_grads_kernel, "attention_grads", (1,),
                [full, spec((rows, half_width), lambda i, _: (0, column)), full, *[whole((rows, half_width))] * 5],
                [whole(shape)] * 2, [like(shape, BF16)] * 2, [pltpu.VMEM((width, rows), BF16)],
            )(info, normed, heads_out, grad_attn, *grads)

        keep_other, send_other = attention_grads(1, other)
        keep_other, send_other, *over_y = lax.optimization_barrier((keep_other, send_other, *over_y))
        over_y[2:] = [flip(value, 1) for value in over_y[2:]]
        got_other = flip(send_other)
        mlp_stage = mlp_section(0)
        x_first, x_last = (
            rows_sum([(keep_other, place * half), (got_other, place * half)], 0, half) for place in (1 - near, near)
        )
        x_first, x_last, mlp_stage, grad_heads = lax.optimization_barrier((x_first, x_last, mlp_stage, grad_heads))
        x_first = cross(x_first)
        mlp_stage = flip(mlp_stage, upper[0])
        own = backward(0, grad_heads)
        x_first, x_last, mlp_stage, *tied = lax.optimization_barrier((x_first, x_last, mlp_stage, *over_y[2:], *own))
        over_y[2:], own = tied[: levels - 1], tied[levels - 1 :]
        x_last = cross(x_last)
        mlp_rows_kept.append((mlp_stage, -starts[1]))
        own, (mlp_stage,) = with_far(own, mlp_section(1))
        mlp_stage = flip(mlp_stage, upper[1])
        keep_own, send_own = attention_grads(0, own)
        block_out = gather_slots(restore, block_back, F32)
        keep_own, send_own, mlp_stage, x_last, block_out = lax.optimization_barrier(
            (keep_own, send_own, mlp_stage, x_last, block_out)
        )
        mlp_rows_kept.append((mlp_stage, -starts[2]))
        for level in range(2, levels):
            mlp_rows_kept.append((flip(mlp_section(level), upper[level]), -starts[level + 1]))
        mlp_piece = mlp_section(levels)
        for level in reversed(range(2, levels)):
            mlp_piece = widen(level, mlp_piece, flip(mlp_piece, upper[level]))
        mlp_piece, *own = lax.optimization_barrier((mlp_piece, *own))
        mlp_stage = flip(mlp_piece, upper[1])
        got_own = flip(send_own)
        half_rows = spec((tile, half_width), lambda i, _: (i, 0))
        input_pieces, small_attn = call(
            functools.partial(leave_kernel, tile, block), "leave", (steps,),
            [rowwise, rowwise, whole((1, width)), *[half_rows] * 10, whole(qkv_weight.shape), *kv_specs, *q_specs],
            [pieces_spec, whole((4, width))],
            [like((slots // 2, 2, block, half_width), BF16), like((4, width), F32)],
            [pltpu.VMEM((tile, width), F32)],
        )(info, inputs, grad_residual, norm_gain[:1], *own, *other, qkv_weight, kv_direct, kv_partner, q_direct, q_partner)
        input_pieces, small_attn, got_own, mlp_stage = lax.optimization_barrier(
            (input_pieces, small_attn, got_own, mlp_stage)
        )
        sent = rows_sum([(keep_own, (1 - near) * half), (got_own, (1 - near) * half), (x_first, 0)], 0, half)
        over_bit = flip(sent, 1)
        mlp_piece = widen(1, mlp_piece, mlp_stage)
        mlp_stage = flip(mlp_piece, upper[0])
        input_back = exchange(input_pieces.reshape(slots, block, half_width))

        def ordered(vectors):
            return join(side, vectors[:, :half_width], vectors[:, half_width:], axis=1)

        hidden = 2 * hidden_half
        fcb0 = jnp.sum(fcb0 + fcb1, axis=0)
        fcb = join(side, fcb0, jnp.zeros_like(fcb0), axis=1).reshape(hidden // width, width)
        small = jnp.concatenate([small_mlp, small_attn[:2], ordered(small_attn[2:]), fcb], axis=0)
        links = [flip, cross, *[functools.partial(flip, bit=bit) for bit in range(1, bits)]]

        def add_over(value):
            return value + links.pop(0)(value) if links else value

        small = add_over(small)
        over_bit, mlp_stage, small = lax.optimization_barrier((over_bit, mlp_stage, small))
        mlp_piece = widen(0, mlp_piece, mlp_stage)
        kept = [(keep_own, near * half), (got_own, near * half), (x_last, 0), (over_bit, 0)]
        for level in range(levels):
            stage = flip(rows_sum(kept, *section(level)), upper[level])
            if level == 0:
                mlp_over, mlp_core = flip(mlp_piece, 1), flip(mlp_piece)
            small = add_over(small)
            stage, small = lax.optimization_barrier((stage, small))
            kept.append((stage, -starts[level + 1]))
        piece = rows_sum(kept, *section(levels))
        for level in reversed(range(levels)):
            stage = flip(piece, upper[level])
            small = add_over(small)
            stage, small = lax.optimization_barrier((stage, small))
            if level == levels - 1:
                stage, input_back = lax.optimization_barrier((stage, input_back))
            piece = widen(level, piece, stage)
        while links:
            small = add_over(small)
        over, near_core = flip(piece, 1), flip(piece)
        mlp_over, mlp_core, piece = lax.optimization_barrier((mlp_over, mlp_core, piece))
        mlp_all = [mlp_piece, mlp_over, mlp_core, flip(mlp_over)]
        input_grad = gather_slots(restore, input_back, F32)
        fc_grad, proj_grad = call(
            finish_mlp_kernel, "finish_mlp", (2,), [spec((half, 2 * chunk), lambda i, _: (0, i))] * 4,
            [spec((width, chunk), lambda i, _: (0, i)), spec((chunk, width), lambda i, _: (i, 0))],
            [like(fc_weight.shape, F32), like(proj_weight.shape, F32)],
        )(info, *mlp_all)
        over, fc_grad, proj_grad, input_grad, small = lax.optimization_barrier((over, fc_grad, proj_grad, input_grad, small))
        qkv_grad, out_grad = call(
            finish_attention_kernel, "finish_attention", (1,), [whole((half, 2 * chunk))] * 4,
            [whole(qkv_weight.shape), whole(out_weight.shape)],
            [like(qkv_weight.shape, F32), like(out_weight.shape, F32)],
        )(info, piece, over, near_core, flip(over))

        gain_mlp, shift_mlp, bias_mlp, bias_attn, gain_attn, shift_attn = (small[i] for i in range(6))
        return (
            block_out,
            input_grad,
            qkv_grad,
            part(small[6:8], side, 1),
            out_grad,
            jnp.stack([bias_attn, bias_mlp]),
            fc_grad,
            part(small[8:].reshape(hidden), side),
            proj_grad,
            jnp.stack([gain_attn, gain_mlp]),
            jnp.stack([shift_attn, shift_mlp]),
        )

    return jax.shard_map(
        body,
        mesh=mesh,
        in_specs=(
            P(None, "dp", "tensor"),
            P(None, "dp", "tensor"),
            P("dp", None, "tensor"),
            P("dp", None),
            P(),
            P(),
            P(None, None, "tensor"),
            P(None, "tensor"),
            P("tensor", None),
            P(),
            P(None, "tensor"),
            P("tensor"),
            P("tensor", None),
            P(),
            P(),
        ),
        out_specs=(
            P(None, "dp", "tensor"),
            P(None, "dp", "tensor"),
            P(None, None, "tensor"),
            P(None, "tensor"),
            P("tensor", None),
            P(),
            P(None, "tensor"),
            P("tensor"),
            P("tensor", None),
            P(),
            P(),
        ),
        check_vma=False,
    )
```
